128 devices in a mesh: rows: 8 (over x_hi, z), samples: 4 (over x_lo, core), chan: 4 (over y).
Axes of the slice: x: 4 (x_hi: 2, x_lo: 2; x = x_hi * 2 + x_lo), y: 4, z: 4, core: 2. Of those that a mesh axis runs over, the one named last changes fastest.
Arguments:
- feature: bfloat16 [4, 256, 64, 512], P('samples', 'chan', 'rows'), may hold values from -6 to 6
- out_grad: bfloat16 [4, 256, 64, 512], P('samples', 'chan', 'rows'), may hold values from -6 to 6
- bank: float32 [4, 9, 256, 256], P(None, None, 'chan', 'rows'), may hold values from -0.125 to 0.125
- select: int32 [4, 4], P('samples'), may hold values from 1 to 8
- latent: float32 [4, 512], P('samples'), may hold values from -6 to 6
- affine_w: float32 [512, 256], P(None, 'rows'), may hold values from -0.25 to 0.25
- affine_b: float32 [256], P('rows'), may hold values from 0.5 to 1.5
Outputs:
- feature_grad: bfloat16 [4, 256, 64, 512], P('samples', 'chan', 'rows')
- bank_grad: float32 [4, 9, 256, 256], P(None, None, 'chan', 'rows')
- affine_w_grad: float32 [512, 256], P(None, 'rows')
- affine_b_grad: float32 [256], P('rows')
The draws below stay inside these ranges and needn't reach their ends.
All inputs are finite; a program needn't handle non-finite values.
Results may differ from the reference program's by a relative error of at most 0.0049.
Values may be sent and summed in bfloat16 or wider, within the bound.
A program may use at most 128 MiB of HBM per device.

```python
import jax
import jax.numpy as jnp
from jax import lax

C = 256
NB = 4
Z = 512
WIDTH = 512
HEIGHT = 64
SAMPLES = 4


def set_ends(array, own_key, low, largest):
    place = [jax.random.randint(jax.random.fold_in(own_key, axis), (), 0, length) for axis, length in enumerate(array.shape)]
    longest = array.shape.index(max(array.shape))
    next_to = place[:longest] + [(place[longest] + 1) % array.shape[longest]] + place[longest + 1:]
    return array.at[tuple(place)].set(low).at[tuple(next_to)].set(largest)


def block_scale(rng, dims, split, low, top_value):
    factor_of, own = 1.0, jax.random.fold_in(rng, 6)
    for position, blocks in split:
        draws = jnp.exp(jax.random.uniform(jax.random.fold_in(own, position), (blocks,), jnp.float32, low / len(split), top_value / len(split)))
        factor_of = factor_of * jnp.repeat(draws, dims[position] // blocks).reshape([-1 if axis == position else 1 for axis in range(len(dims))])
    return factor_of


def bell_draw(stream_key, dims, scale, most, pieces=(), held_as=jnp.bfloat16):
    result = jax.random.normal(stream_key, dims, jnp.float32) * scale
    if len(pieces) > 0:
        result = block_scale(stream_key, dims, pieces, -0.22, 0.18) * result
    return jnp.clip(result, min=-most, max=most).astype(held_as)


def setup_inputs(seed: int = 0) -> dict:
    streams_of = jax.random.split(jax.random.key(seed), 8)
    return {
        "feature": bell_draw(streams_of[0], (SAMPLES, C, HEIGHT, WIDTH), 1.0, 6.0, ((0, 4), (1, 4), (2, 8))),
        "out_grad": bell_draw(streams_of[1], (SAMPLES, C, HEIGHT, WIDTH), 1.0, 6.0, ((0, 4), (1, 4), (2, 8))),
        "bank": bell_draw(streams_of[2], (NB, 9, C, C), (9 * C) ** -0.5, 0.125, ((2, 4), (3, 8)), jnp.float32),
        "select": set_ends(jax.random.randint(streams_of[3], (SAMPLES, NB), 1, 9), jax.random.fold_in(streams_of[3], 1), 1, 8).astype(jnp.int32),
        "latent": bell_draw(streams_of[4], (SAMPLES, Z), 1.0, 6.0, ((0, 4),), jnp.float32),
        "affine_w": bell_draw(streams_of[5], (Z, C), Z ** -0.5, 0.25, ((1, 8),), jnp.float32),
        "affine_b": jnp.clip(0.5 + 1.0 * jax.random.uniform(streams_of[6], (C,), jnp.float32) ** block_scale(streams_of[6], (C,), ((0, 8),), -0.2, 0.2), 0.5, 1.5),
    }


EPS = 1e-08

def reference(feature, out_grad, bank, select, latent, affine_w, affine_b):
    chans = feature.shape[1]
    height = feature.shape[2]
    width = feature.shape[3]

    def one_sample(items):
        feat, cotan, weights, style_in = items
        kernel = jnp.einsum('k,ktoc->toc', weights.astype(jnp.float32), bank, precision=lax.Precision.HIGHEST)
        style = jnp.dot(style_in, affine_w, precision=lax.Precision.HIGHEST) + affine_b
        plain = kernel * style[None, None, :]
        scale = lax.rsqrt(lax.optimization_barrier(jnp.sum(plain * plain, axis=(0, 2))) + EPS)
        modulated = (plain * scale[None, :, None]).astype(jnp.bfloat16)
        feat_pad = jnp.pad(feat, ((0, 0), (1, 1), (1, 1)))
        cotan_pad = jnp.pad(cotan, ((0, 0), (1, 1), (1, 1)))
        cotan_flat = cotan.reshape(chans, height * width)
        input_total = jnp.zeros((chans, height * width), jnp.float32)
        grads = []
        for tap_index in range(9):
            row_off = tap_index // 3
            col_off = tap_index % 3
            feat_tap = feat_pad[:, row_off:row_off + height, col_off:col_off + width].reshape(chans, height * width)
            cotan_tap = cotan_pad[:, 2 - row_off:2 - row_off + height, 2 - col_off:2 - col_off + width].reshape(chans, height * width)
            grads.append(jnp.dot(cotan_flat, feat_tap.T, preferred_element_type=jnp.float32))
            input_total = input_total + jnp.dot(modulated[tap_index].T, cotan_tap, preferred_element_type=jnp.float32)
        mod_grad = jnp.stack(grads, 0)
        slope = lax.optimization_barrier(jnp.sum(mod_grad * plain, axis=(0, 2)))
        plain_grad = mod_grad * scale[None, :, None] - plain * (slope * scale ** 3)[None, :, None]
        kernel_grad = plain_grad * style[None, None, :]
        style_grad = lax.optimization_barrier(jnp.sum(plain_grad * kernel, axis=(0, 1)))
        return (input_total.reshape(chans, height, width).astype(jnp.bfloat16), kernel_grad, style_grad)
    feature_grad, kernel_grads, style_grads = lax.map(one_sample, (feature, out_grad, select, latent))
    bank_grad = jnp.einsum('bk,btoc->ktoc', select.astype(jnp.float32), kernel_grads, precision=lax.Precision.HIGHEST)
    affine_w_grad = jnp.dot(latent.T, style_grads, precision=lax.Precision.HIGHEST)
    affine_b_grad = lax.optimization_barrier(jnp.sum(style_grads, axis=0))
    return (feature_grad, bank_grad, affine_w_grad, affine_b_grad)
```

```python
import jax
import jax.numpy as jnp
from jax import lax
from jax.experimental import pallas as pl
from jax.experimental.pallas import tpu as pltpu
from jax.sharding import PartitionSpec as P

EPS = 1e-08
MESH = pl.DeviceIdType.MESH
ROWS, SAMPLES, CHANS = 8, 4, 4
F32, BF16 = jnp.float32, jnp.bfloat16


def lane_iota(shape):
    return lax.broadcasted_iota(jnp.int32, shape, len(shape) - 1)


def moved_right(x):
    return jnp.where(lane_iota(x.shape) == 0, 0.0, pltpu.roll(x, 1, axis=1))


def moved_left(x):
    width = x.shape[1]
    return jnp.where(lane_iota(x.shape) == width - 1, 0.0, pltpu.roll(x, width - 1, axis=1))


def over_taps(x):
    flat = jnp.sum(x, axis=(0, 1))[None, :]
    half = flat[:, :128] + flat[:, 128:]
    return half + pltpu.roll(half, 64, axis=1)


def kernel(
    x_ref, f_ref, bank_ref, sel_ref, lat_ref, aw_ref, ab_ref,
    d_ref, bg_ref, awg_ref, abg_ref,
    xbuf, fs, mm, mown, gs, gbuf, latb, selb, en, sl, kg, st, ker_ref, plain_ref,
    ag_s, ag_r, ha_s, ha_r, own_s, in_s, in_r, en_s, en_r, m_s, m_r, g_s, g_r, sl_s, sl_r, kg_s, kg_r, st_s, st_r,
):
    r, b, c = lax.axis_index("rows"), lax.axis_index("samples"), lax.axis_index("chan")
    height, ch, width = x_ref.shape
    nb, ib = bank_ref.shape[0], bank_ref.shape[2]
    left, right, opp = lax.rem(c + 3, CHANS), lax.rem(c + 1, CHANS), lax.rem(c + 2, CHANS)

    def remote(src, dst, send, recv, **where):
        return pltpu.make_async_remote_copy(
            src_ref=src, dst_ref=dst, send_sem=send, recv_sem=recv, device_id=where, device_id_type=MESH
        )

    sent = []

    def go(copy):
        copy.start()
        sent.append(copy)

    barrier = pltpu.get_barrier_semaphore()
    greeted = 0
    for dr in range(ROWS):
        for dc in range(CHANS):
            if dr or dc:
                pl.semaphore_signal(
                    barrier, inc=1,
                    device_id={"rows": lax.rem(r + dr, ROWS), "chan": lax.rem(c + dc, CHANS)},
                    device_id_type=MESH,
                )
                greeted += 1
    for db in range(1, SAMPLES):
        for dc in range(CHANS):
            pl.semaphore_signal(
                barrier, inc=1,
                device_id={"samples": lax.rem(b + db, SAMPLES), "chan": lax.rem(c + dc, CHANS)},
                device_id_type=MESH,
            )
            greeted += 1

    lat = lat_ref[...]
    latb[pl.ds(b, 1)] = jnp.broadcast_to(lat[None], (1, 8, lat.shape[1]))
    sel = sel_ref[...].astype(F32)
    selrow = jnp.zeros((8, 128), F32)
    for k in range(nb):
        selrow = jnp.where(lane_iota((8, 128)) == k, sel[:, k : k + 1], selrow)
    selb[pl.ds(b, 1)] = selrow[None]
    square = lax.broadcasted_iota(jnp.int32, (ib, ib), 0) == lane_iota((ib, ib))
    bias = jnp.sum(jnp.where(square, ab_ref[...], 0.0), axis=1, keepdims=True)
    style = jnp.sum(aw_ref[...] * lat, axis=1, keepdims=True) + bias
    ker_ref[...] = jnp.zeros_like(ker_ref)
    for kh in range(3):
        for kw in range(3):
            tap = sum(sel[:, k : k + 1] * bank_ref[k, 3 * kh + kw] for k in range(nb))
            ker_ref[kw, :, (2 - kh) * ch : (3 - kh) * ch] = tap
    ker = ker_ref[...]
    plain_ref[...] = ker * style[None]
    plain = plain_ref[...]
    en[pl.ds(r, 1)] = jnp.broadcast_to(over_taps(plain * plain)[None], (1, 8, 128))

    own = pltpu.make_async_copy(x_ref, xbuf.at[pl.ds(1, height), c], own_s)
    own.start()
    xbuf[height + 2] = jnp.zeros(xbuf.shape[1:], BF16)

    @pl.when(r == 0)
    def _():
        xbuf[0] = jnp.zeros(xbuf.shape[1:], BF16)

    @pl.when(r == ROWS - 1)
    def _():
        xbuf[height + 1] = jnp.zeros(xbuf.shape[1:], BF16)

    pl.semaphore_wait(barrier, greeted)

    for d in range(1, ROWS):
        go(remote(en.at[r], en.at[r], en_s.at[d], en_r.at[d], rows=lax.rem(r + d, ROWS)))
    half = height // 2
    quarter = height // 4

    def rows_of(shard, first, count):
        return xbuf.at[pl.ds(first + 1, count), shard]

    to_right, to_left = {"chan": right}, {"chan": left}
    go(remote(x_ref.at[pl.ds(0, half)], rows_of(c, 0, half), ag_s.at[0, 0], ag_r.at[0, 0], **to_right))
    go(remote(x_ref.at[pl.ds(half, half)], rows_of(c, half, half), ag_s.at[1, 0], ag_r.at[1, 0], **to_left))

    def halo(i, shard, top, from_own):
        at = 0 if top else height - 1
        src = x_ref.at[pl.ds(at, 1)] if from_own else rows_of(shard, at, 1)
        dst = xbuf.at[pl.ds(height + 1 if top else 0, 1), shard]
        there = jnp.maximum(r - 1, 0) if top else jnp.minimum(r + 1, ROWS - 1)
        side = 0 if top else 1
        return remote(src, dst, ha_s.at[i, side], ha_r.at[i, side], rows=there)

    def start_halo(i, shard, top, from_own=False):
        @pl.when(r > 0 if top else r < ROWS - 1)
        def _():
            halo(i, shard, top, from_own).start()

    def wait_halo(i, shard):
        @pl.when(r < ROWS - 1)
        def _():
            halo(i, shard, True, False).wait_recv()

        @pl.when(r > 0)
        def _():
            halo(i, shard, False, False).wait_recv()

    start_halo(0, c, True, True)
    start_halo(0, c, False, True)
    go(remote(x_ref.at[pl.ds(half, half)], rows_of(c, half, half), ag_s.at[0, 1], ag_r.at[0, 1], **to_right))
    go(remote(x_ref.at[pl.ds(0, half)], rows_of(c, 0, half), ag_s.at[1, 1], ag_r.at[1, 1], **to_left))
    for d in range(1, SAMPLES):
        there = lax.rem(b + d, SAMPLES)
        go(remote(latb.at[b], latb.at[b], in_s.at[0, d], in_r.at[0, d], samples=there))
        go(remote(selb.at[b], selb.at[b], in_s.at[1, d], in_r.at[1, d], samples=there))

    def shifted(h, carry):
        f = f_ref[h]
        wide = f.astype(F32)
        fs[h, 0:ch] = moved_right(wide).astype(BF16)
        fs[h, ch : 2 * ch] = f
        fs[h, 2 * ch : 3 * ch] = moved_left(wide).astype(BF16)
        return carry

    lax.fori_loop(0, height, shifted, 0)

    for d in range(1, ROWS):
        src = lax.rem(r + ROWS - d, ROWS)
        remote(en.at[src], en.at[src], en_s.at[d], en_r.at[d], rows=src).wait_recv()
    scale = lax.rsqrt(jnp.sum(en[...], axis=0)[0:1] + EPS)
    scale = jnp.concatenate([scale, scale], axis=1)[None]
    mown[...] = (plain * scale).astype(BF16)
    home = r // 2
    place = pl.multiple_of(lax.rem(r, 2) * ib, ib)

    def mm_block(row, chan):
        return mm.at[chan, :, pl.ds(pl.multiple_of(lax.rem(row, 2) * ib, ib), ib), :]

    mine = mm_block(r, c)
    for d in range(1, ROWS):
        go(remote(mown, mine, m_s.at[d], m_r.at[lax.rem(r, 2), c], rows=lax.rem(r + d, ROWS), chan=home))
    m_here = remote(mown, mine, m_s.at[0], m_r.at[lax.rem(r, 2), c], chan=home)
    m_local = pltpu.make_async_copy(mown, mine, m_r.at[lax.rem(r, 2), c])

    @pl.when(home == c)
    def _():
        m_local.start()

    @pl.when(home != c)
    def _():
        m_here.start()

    def grad_of(i, shard):
        def step(h, acc):
            around = xbuf[pl.ds(h, 4), shard].reshape(4 * ch, width)
            return acc + lax.dot_general(
                fs[h], around, (((1,), (1,)), ((), ())), preferred_element_type=F32
            )

        acc = lax.fori_loop(0, height, step, jnp.zeros((3 * ch, 4 * ch), F32))
        gs[i] = acc.reshape(3, ch, 4 * ch).astype(BF16)
        for part in range(2):
            src = gs.at[i, :, pl.ds(part * ib, ib), :]
            target = 2 * c + part
            if i == 0:
                @pl.when(target == r)
                def _():
                    pltpu.make_async_copy(src, gbuf.at[r], g_r.at[r]).start()

                @pl.when(target != r)
                def _():
                    remote(src, gbuf.at[r], g_s.at[i, part], g_r.at[r], rows=target).start()
            else:
                go(remote(src, gbuf.at[r], g_s.at[i, part], g_r.at[r], rows=target, chan=shard))

    own.wait()
    wait_halo(0, c)
    grad_of(0, c)

    def from_left(k, first, count, shard):
        return remote(rows_of(shard, first, count), rows_of(shard, first, count), ag_s.at[0, k], ag_r.at[0, k], **to_right)

    def from_right(k, first, count, shard):
        return remote(rows_of(shard, first, count), rows_of(shard, first, count), ag_s.at[1, k], ag_r.at[1, k], **to_left)

    from_left(0, 0, half, left).wait_recv()
    go(from_left(2, 0, quarter, left))
    go(from_left(3, quarter, quarter, left))
    start_halo(1, left, True)
    from_right(0, half, half, right).wait_recv()
    go(from_right(2, height - quarter, quarter, right))
    go(from_right(3, half, quarter, right))
    start_halo(2, right, False)
    from_left(1, half, half, left).wait_recv()
    start_halo(1, left, False)
    from_right(1, 0, half, right).wait_recv()
    start_halo(2, right, True)
    wait_halo(1, left)
    grad_of(1, left)
    wait_halo(2, right)
    grad_of(2, right)
    from_left(2, 0, quarter, opp).wait_recv()
    start_halo(3, opp, True)
    from_right(2, height - quarter, quarter, opp).wait_recv()
    start_halo(3, opp, False)
    from_left(3, quarter, quarter, opp).wait_recv()
    from_right(3, half, quarter, opp).wait_recv()
    wait_halo(3, opp)
    grad_of(3, opp)

    for part in range(2):
        for chan in range(CHANS):
            remote(mown, mm_block(part, chan), m_s.at[0], m_r.at[part, chan], chan=home).wait_recv()

    def rows_out(h, carry):
        total = jnp.zeros((3 * ch, width), F32)
        for shard in range(CHANS):
            around = xbuf[pl.ds(h, 4), shard].reshape(4 * ch, width)
            total = total + jnp.dot(mm[shard].reshape(3 * ch, 4 * ch), around, preferred_element_type=F32)
        out = total[ch : 2 * ch] + moved_left(total[:ch]) + moved_right(total[2 * ch :])
        d_ref[h] = out.astype(BF16)
        return carry

    lax.fori_loop(0, height, rows_out, 0)

    for src in range(ROWS):
        remote(gs.at[0, :, pl.ds(0, ib), :], gbuf.at[src], g_s.at[0, 0], g_r.at[src], rows=home).wait_recv()
    grad = gbuf[0].astype(F32)
    for src in range(1, ROWS):
        grad = grad + gbuf[src].astype(F32)
    sl[pl.ds(r, 1)] = jnp.broadcast_to(over_taps(grad * plain)[None], (1, 8, 128))
    for d in range(1, ROWS):
        go(remote(sl.at[r], sl.at[r], sl_s.at[d], sl_r.at[d], rows=lax.rem(r + d, ROWS)))
    for d in range(1, ROWS):
        src = lax.rem(r + ROWS - d, ROWS)
        remote(sl.at[src], sl.at[src], sl_s.at[d], sl_r.at[d], rows=src).wait_recv()
    slope = jnp.sum(sl[...], axis=0)[0:1]
    slope = jnp.concatenate([slope, slope], axis=1)[None]
    plain_grad = grad * scale - plain * (slope * (scale * scale * scale))
    kg[pl.ds(b, 1)] = (plain_grad * style[None])[None]
    for d in range(1, SAMPLES):
        go(remote(kg.at[b], kg.at[b], kg_s.at[d], kg_r.at[d], samples=lax.rem(b + d, SAMPLES)))
    by_input = jnp.sum(plain_grad * ker, axis=0)
    by_input = jnp.concatenate([by_input, jnp.zeros((128 - ib, by_input.shape[1]), F32)], axis=0)
    style_part = lax.dot_general(
        jnp.ones((8, by_input.shape[1]), F32), by_input, (((1,), (1,)), ((), ())),
        preferred_element_type=F32, precision=lax.Precision.HIGHEST,
    )
    st[pl.ds(b, 1), pl.ds(c, 1)] = style_part[None, None]
    for db in range(SAMPLES):
        for dc in range(CHANS):
            if db or dc:
                go(remote(
                    st.at[b, c], st.at[b, c], st_s.at[db, dc], st_r.at[db, dc],
                    samples=lax.rem(b + db, SAMPLES), chan=lax.rem(c + dc, CHANS),
                ))

    for d in range(1, SAMPLES):
        src = lax.rem(b + SAMPLES - d, SAMPLES)
        remote(latb.at[src], latb.at[src], in_s.at[0, d], in_r.at[0, d], samples=src).wait_recv()
        remote(selb.at[src], selb.at[src], in_s.at[1, d], in_r.at[1, d], samples=src).wait_recv()
    for db in range(SAMPLES):
        for dc in range(CHANS):
            if db or dc:
                bs, cs = lax.rem(b + SAMPLES - db, SAMPLES), lax.rem(c + CHANS - dc, CHANS)
                remote(
                    st.at[bs, cs], st.at[bs, cs], st_s.at[db, dc], st_r.at[db, dc], samples=bs, chan=cs
                ).wait_recv()
    diagonal = lax.broadcasted_iota(jnp.int32, (ib, 128), 0) == lane_iota((ib, 128))
    style_sum = jnp.zeros((1, 128), F32)
    affine = jnp.zeros(awg_ref.shape, F32)
    for s in range(SAMPLES):
        row = st[s, 0] + st[s, 1] + st[s, 2] + st[s, 3]
        row = row[0:1]
        style_sum = style_sum + row
        column = jnp.sum(jnp.where(diagonal, row, 0.0), axis=1, keepdims=True)
        affine = affine + column * latb[s][0:1]
    awg_ref[...] = affine
    abg_ref[...] = style_sum[:, :ib]
    for d in range(1, SAMPLES):
        src = lax.rem(b + SAMPLES - d, SAMPLES)
        remote(kg.at[src], kg.at[src], kg_s.at[d], kg_r.at[d], samples=src).wait_recv()
    for k in range(nb):
        weights = [selb[s][0:1, k : k + 1] for s in range(SAMPLES)]
        for kw in range(3):
            total = sum(weights[s] * kg[s, kw] for s in range(SAMPLES))
            for kh in range(3):
                bg_ref[k, 3 * kh + kw] = total[:, (2 - kh) * ch : (3 - kh) * ch]

    for copy in sent:
        copy.wait_send()

    @pl.when(home != c)
    def _():
        m_here.wait_send()

    for part in range(2):
        @pl.when(2 * c + part != r)
        def _():
            remote(
                gs.at[0, :, pl.ds(part * ib, ib), :], gbuf.at[r], g_s.at[0, part], g_r.at[r], rows=2 * c + part
            ).wait_send()

    for i, shard in enumerate((c, left, right, opp)):
        @pl.when(r > 0)
        def _():
            halo(i, shard, True, False).wait_send()

        @pl.when(r < ROWS - 1)
        def _():
            halo(i, shard, False, False).wait_send()


def on_device(feature, out_grad, bank, select, latent, affine_w, affine_b):
    x = jnp.transpose(out_grad[0], (1, 0, 2))
    f = jnp.transpose(feature[0], (1, 0, 2))
    height, ch, width = x.shape
    nb, taps, _, ib = bank.shape
    z = latent.shape[1]
    lanes = 4 * ch
    vmem = pl.BlockSpec(memory_space=pltpu.VMEM)
    dma = pltpu.SemaphoreType.DMA
    d, bg, awg, abg = pl.pallas_call(
        kernel,
        out_shape=(
            jax.ShapeDtypeStruct((height, ch, width), BF16),
            jax.ShapeDtypeStruct((nb, taps, ib, ch), F32),
            jax.ShapeDtypeStruct((ib, z), F32),
            jax.ShapeDtypeStruct((1, ib), F32),
        ),
        in_specs=[vmem] * 7,
        out_specs=(vmem,) * 4,
        scratch_shapes=[
            pltpu.VMEM((height + 3, CHANS, ch, width), BF16),
            pltpu.VMEM((height, 3 * ch, width), BF16),
            pltpu.VMEM((CHANS, 3, ch, lanes), BF16),
            pltpu.VMEM((3, ib, lanes), BF16),
            pltpu.VMEM((CHANS, 3, ch, lanes), BF16),
            pltpu.VMEM((ROWS, 3, ib, lanes), BF16),
            pltpu.VMEM((SAMPLES, 8, z), F32),
            pltpu.VMEM((SAMPLES, 8, 128), F32),
            pltpu.VMEM((ROWS, 8, 128), F32),
            pltpu.VMEM((ROWS, 8, 128), F32),
            pltpu.VMEM((SAMPLES, 3, ib, lanes), F32),
            pltpu.VMEM((SAMPLES, CHANS, 8, 128), F32),
            pltpu.VMEM((3, ib, lanes), F32),
            pltpu.VMEM((3, ib, lanes), F32),
            dma((2, 4)), dma((2, 4)),
            dma((4, 2)), dma((4, 2)),
            dma,
            dma((2, SAMPLES)), dma((2, SAMPLES)),
            dma((ROWS,)), dma((ROWS,)),
            dma((ROWS,)), dma((2, CHANS)),
            dma((CHANS, 2)), dma((ROWS,)),
            dma((ROWS,)), dma((ROWS,)),
            dma((SAMPLES,)), dma((SAMPLES,)),
            dma((SAMPLES, CHANS)), dma((SAMPLES, CHANS)),
        ],
        compiler_params=pltpu.CompilerParams(
            collective_id=0, has_side_effects=True, vmem_limit_bytes=48 * 1024 * 1024
        ),
    )(
        x, f, jnp.transpose(bank, (0, 1, 3, 2)), select, latent,
        jnp.transpose(affine_w), affine_b[None],
    )
    return (
        jnp.transpose(d, (1, 0, 2))[None],
        jnp.transpose(bg, (0, 1, 3, 2)),
        jnp.transpose(awg),
        abg[0],
    )


def solution(mesh):
    return jax.shard_map(
        on_device,
        mesh=mesh,
        in_specs=(
            P("samples", "chan", "rows", None),
            P("samples", "chan", "rows", None),
            P(None, None, "chan", "rows"),
            P("samples", None),
            P("samples", None),
            P(None, "rows"),
            P("rows"),
        ),
        out_specs=(
            P("samples", "chan", "rows", None),
            P(None, None, "chan", "rows"),
            P(None, "rows"),
            P("rows"),
        ),
        check_vma=False,
    )
```

```python
import jax
import jax.numpy as jnp
from jax import lax
from jax.experimental import pallas as pl
from jax.experimental.pallas import tpu as pltpu
from jax.sharding import PartitionSpec as P

EPS = 1e-08
MESH = pl.DeviceIdType.MESH
ROWS, SAMPLES, CHANS = 8, 4, 4
F32, BF16 = jnp.float32, jnp.bfloat16


def lane_iota(shape):
    return lax.broadcasted_iota(jnp.int32, shape, len(shape) - 1)


def moved_right(x):
    return jnp.where(lane_iota(x.shape) == 0, 0.0, pltpu.roll(x, 1, axis=1))


def moved_left(x):
    width = x.shape[1]
    return jnp.where(lane_iota(x.shape) == width - 1, 0.0, pltpu.roll(x, width - 1, axis=1))


def over_taps(x):
    flat = jnp.sum(x, axis=(0, 1))[None, :]
    half = flat[:, :128] + flat[:, 128:]
    return half + pltpu.roll(half, 64, axis=1)


def kernel(
    x_ref, f_ref, bank_ref, sel_ref, lat_ref, aw_ref, ab_ref,
    d_ref, bg_ref, awg_ref, abg_ref,
    xbuf, fs, fhalo, mr, mm, gs, gbuf, latb, selb, en, slv, slo, kg, st, ker_ref, plain_ref, dacc, dsend, dhalo,
    ag_s, ag_r, fh_s, fh_r, dh_s, dh_r, own_s, in_s, in_r, en_s, en_r, mz_s, mf_s, my_s, mr_r, my_r,
    g_s, g_r, sl_s, sl_r, kg_s, kg_r, st_s, st_r,
):
    r, b, c = lax.axis_index("rows"), lax.axis_index("samples"), lax.axis_index("chan")
    height, ch, width = x_ref.shape
    nb, ib = bank_ref.shape[0], bank_ref.shape[2]
    left, right, opp = lax.rem(c + 3, CHANS), lax.rem(c + 1, CHANS), lax.rem(c + 2, CHANS)
    tall = 6 * ib

    def remote(src, dst, send, recv, **where):
        return pltpu.make_async_remote_copy(
            src_ref=src, dst_ref=dst, send_sem=send, recv_sem=recv, device_id=where, device_id_type=MESH
        )

    sent = []

    def go(copy):
        copy.start()
        sent.append(copy)

    barrier = pltpu.get_barrier_semaphore()
    greeted = 0
    for dr in range(ROWS):
        for dc in range(CHANS):
            if dr or dc:
                pl.semaphore_signal(
                    barrier, inc=1,
                    device_id={"rows": lax.rem(r + dr, ROWS), "chan": lax.rem(c + dc, CHANS)},
                    device_id_type=MESH,
                )
                greeted += 1
    for db in range(1, SAMPLES):
        for dc in range(CHANS):
            pl.semaphore_signal(
                barrier, inc=1,
                device_id={"samples": lax.rem(b + db, SAMPLES), "chan": lax.rem(c + dc, CHANS)},
                device_id_type=MESH,
            )
            greeted += 1

    lat = lat_ref[...]
    latb[pl.ds(b, 1)] = jnp.broadcast_to(lat[None], (1, 8, lat.shape[1]))
    sel = sel_ref[...].astype(F32)
    selrow = jnp.zeros((8, 128), F32)
    for k in range(nb):
        selrow = jnp.where(lane_iota((8, 128)) == k, sel[:, k : k + 1], selrow)
    selb[pl.ds(b, 1)] = selrow[None]
    square = lax.broadcasted_iota(jnp.int32, (ib, ib), 0) == lane_iota((ib, ib))
    bias = jnp.sum(jnp.where(square, ab_ref[...], 0.0), axis=1, keepdims=True)
    style = jnp.sum(aw_ref[...] * lat, axis=1, keepdims=True) + bias
    ker_ref[...] = jnp.zeros_like(ker_ref)
    for kh in range(3):
        for kw in range(3):
            tap = sum(sel[:, k : k + 1] * bank_ref[k, 3 * kh + kw] for k in range(nb))
            ker_ref[kw, :, (2 - kh) * ch : (3 - kh) * ch] = tap
    ker = ker_ref[...]
    plain_ref[...] = ker * style[None]
    plain = plain_ref[...]
    en[pl.ds(r, 1)] = over_taps(plain * plain)[None]

    own = pltpu.make_async_copy(x_ref, xbuf.at[pl.ds(2, height), c], own_s)
    own.start()

    def shift_into(at, f):
        wide = f.astype(F32)
        for kw, moved in enumerate((moved_right(wide).astype(BF16), f, moved_left(wide).astype(BF16))):
            for part in range(2):
                first = (3 * part + kw) * ib
                fs[at, first : first + ib] = moved[part * ib : (part + 1) * ib]

    def shifted(h, carry):
        shift_into(h + 1, f_ref[h])
        return carry

    lax.fori_loop(0, height, shifted, 0)
    for row in (0, 1, height + 2, height + 3, height + 4):
        xbuf[row] = jnp.zeros(xbuf.shape[1:], BF16)

    pl.semaphore_wait(barrier, greeted)

    for d in range(1, ROWS):
        go(remote(en.at[r], en.at[r], en_s.at[d], en_r.at[d], rows=lax.rem(r + d, ROWS)))
    half = height // 2
    quarter = height // 4

    def rows_of(shard, first, count):
        return xbuf.at[pl.ds(first + 2, count), shard]

    to_right, to_left = {"chan": right}, {"chan": left}
    go(remote(x_ref.at[pl.ds(0, half)], rows_of(c, 0, half), ag_s.at[0, 0], ag_r.at[0, 0], **to_right))
    go(remote(x_ref.at[pl.ds(half, half)], rows_of(c, half, half), ag_s.at[1, 0], ag_r.at[1, 0], **to_left))

    def edge(src, dst, send, recv, up):
        there = jnp.maximum(r - 1, 0) if up else jnp.minimum(r + 1, ROWS - 1)
        i = 0 if up else 1
        return remote(src, dst.at[1 - i], send.at[i], recv.at[1 - i], rows=there)

    not_first, not_last = r > 0, r < ROWS - 1

    @pl.when(not_first)
    def _():
        edge(f_ref.at[0], fhalo, fh_s, fh_r, True).start()

    @pl.when(not_last)
    def _():
        edge(f_ref.at[height - 1], fhalo, fh_s, fh_r, False).start()

    go(remote(x_ref.at[pl.ds(half, half)], rows_of(c, half, half), ag_s.at[0, 1], ag_r.at[0, 1], **to_right))
    go(remote(x_ref.at[pl.ds(0, half)], rows_of(c, 0, half), ag_s.at[1, 1], ag_r.at[1, 1], **to_left))
    for d in range(1, SAMPLES):
        there = lax.rem(b + d, SAMPLES)
        go(remote(latb.at[b], latb.at[b], in_s.at[0, d], in_r.at[0, d], samples=there))
        go(remote(selb.at[b], selb.at[b], in_s.at[1, d], in_r.at[1, d], samples=there))

    for d in range(1, ROWS):
        src = lax.rem(r + ROWS - d, ROWS)
        remote(en.at[src], en.at[src], en_s.at[d], en_r.at[d], rows=src).wait_recv()
    scale = lax.rsqrt(jnp.sum(en[...], axis=0) + EPS)
    scale = jnp.concatenate([scale, scale], axis=1)[None]

    mr[pl.ds(r, 1)] = (plain * scale).astype(BF16)[None]
    side, level = r // 4, lax.rem(r, 4)
    across = lax.rem(r + 4, ROWS)
    go(remote(mr.at[r], mr.at[r], mz_s.at[0], mr_r.at[0], rows=across))

    def peer(d):
        return 4 * side + lax.rem(level + d, 4)

    def far(d):
        return 4 * (1 - side) + lax.rem(level + d, 4)

    for d in range(1, 4):
        go(remote(mr.at[r], mr.at[r], mz_s.at[d], mr_r.at[d], rows=peer(d)))

    @pl.when(not_first)
    def _():
        edge(f_ref.at[0], fhalo, fh_s, fh_r, False).wait_recv()
        shift_into(0, fhalo[0])

    @pl.when(r == 0)
    def _():
        fs[0] = jnp.zeros(fs.shape[1:], BF16)

    @pl.when(not_last)
    def _():
        edge(f_ref.at[0], fhalo, fh_s, fh_r, True).wait_recv()
        shift_into(height + 1, fhalo[1])

    @pl.when(r == ROWS - 1)
    def _():
        fs[height + 1] = jnp.zeros(fs.shape[1:], BF16)

    def grad_of(i, shard):
        def step(q, acc):
            around = xbuf[pl.ds(q, 4), shard].reshape(4 * ch, width)
            return acc + lax.dot_general(
                fs[q], around, (((1,), (1,)), ((), ())), preferred_element_type=F32
            )

        acc = lax.fori_loop(0, height + 2, step, jnp.zeros((tall, 4 * ch), F32))
        gs[i] = acc.reshape(2, 3, ib, 4 * ch).astype(BF16)
        for part in range(2):
            src = gs.at[i, part]
            target = 2 * c + part
            if i == 0:
                @pl.when(target == r)
                def _():
                    pltpu.make_async_copy(src, gbuf.at[r], g_r.at[r]).start()

                @pl.when(target != r)
                def _():
                    remote(src, gbuf.at[r], g_s.at[i, part], g_r.at[r], rows=target).start()
            else:
                go(remote(src, gbuf.at[r], g_s.at[i, part], g_r.at[r], rows=target, chan=shard))

    own.wait()
    remote(mr.at[across], mr.at[across], mz_s.at[0], mr_r.at[0], rows=across).wait_recv()
    for d in range(1, 4):
        go(remote(mr.at[across], mr.at[across], mf_s.at[d], mr_r.at[4 + d], rows=peer(d)))

    grad_of(0, c)

    def from_left(k, first, count, shard):
        return remote(rows_of(shard, first, count), rows_of(shard, first, count), ag_s.at[0, k], ag_r.at[0, k], **to_right)

    def from_right(k, first, count, shard):
        return remote(rows_of(shard, first, count), rows_of(shard, first, count), ag_s.at[1, k], ag_r.at[1, k], **to_left)

    from_left(0, 0, half, left).wait_recv()
    go(from_left(2, 0, quarter, left))
    from_right(0, half, half, right).wait_recv()
    go(from_right(2, height - quarter, quarter, right))

    for d in range(1, 4):
        src = peer(4 - d)
        remote(mr.at[src], mr.at[src], mz_s.at[d], mr_r.at[d], rows=src).wait_recv()
        src = far(4 - d)
        remote(mr.at[src], mr.at[src], mf_s.at[d], mr_r.at[4 + d], rows=across).wait_recv()
    for d in (1, 3, 2):
        there = lax.rem(c + d, CHANS)
        go(remote(mr.at[pl.ds(2 * there, 2)], mm.at[c], my_s.at[d], my_r.at[d], chan=there))
    mine = pltpu.make_async_copy(mr.at[pl.ds(2 * c, 2)], mm.at[c], my_r.at[0])
    mine.start()
    go(from_left(3, quarter, quarter, left))
    go(from_right(3, half, quarter, right))

    from_left(1, half, half, left).wait_recv()

    grad_of(1, left)

    from_right(1, 0, half, right).wait_recv()

    grad_of(2, right)

    from_left(2, 0, quarter, opp).wait_recv()
    from_right(2, height - quarter, quarter, opp).wait_recv()

    from_left(3, quarter, quarter, opp).wait_recv()
    from_right(3, half, quarter, opp).wait_recv()

    grad_of(3, opp)

    for d in range(1, CHANS):
        src = lax.rem(c + CHANS - d, CHANS)
        remote(mr.at[pl.ds(0, 2)], mm.at[src], my_s.at[d], my_r.at[d], chan=src).wait_recv()
    mine.wait()

    for i, (k, shard) in enumerate(((0, c), (3, left), (1, right), (2, opp))):
        parts = gs[i].astype(F32) * mm[shard].astype(F32)
        slo[i] = over_taps(parts[0] + parts[1])
        for d in range(ROWS):
            if k == 0 and d == 0:
                slv[pl.ds(r, 1), pl.ds(c, 1)] = slo[0][None, None]
            else:
                go(remote(
                    slo.at[i], slv.at[r, c], sl_s.at[d, k], sl_r.at[d, k], rows=lax.rem(r + d, ROWS), chan=shard
                ))

    def rows_out(q, carry):
        total = jnp.zeros((tall, width), F32)
        for shard in range(CHANS):
            around = xbuf[pl.ds(q, 4), shard].reshape(4 * ch, width)
            total = total + jnp.dot(mm[shard].reshape(tall, 4 * ch), around, preferred_element_type=F32)
        for part in range(2):
            t = total[3 * part * ib : 3 * (part + 1) * ib]
            dacc[q, part * ib : (part + 1) * ib] = t[ib : 2 * ib] + moved_left(t[:ib]) + moved_right(t[2 * ib :])
        return carry

    lax.fori_loop(0, height + 2, rows_out, 0)
    dsend[0] = dacc[0].astype(BF16)
    dsend[1] = dacc[height + 1].astype(BF16)

    @pl.when(not_first)
    def _():
        edge(dsend.at[0], dhalo, dh_s, dh_r, True).start()

    @pl.when(not_last)
    def _():
        edge(dsend.at[1], dhalo, dh_s, dh_r, False).start()

    for src in range(ROWS):
        remote(gs.at[0, 0], gbuf.at[src], g_s.at[0, 0], g_r.at[src], rows=across).wait_recv()

    for d in range(ROWS):
        for k in range(CHANS):
            if d or k:
                rs, cs = lax.rem(r + ROWS - d, ROWS), lax.rem(c + CHANS - k, CHANS)
                remote(slo.at[0], slv.at[rs, cs], sl_s.at[d, k], sl_r.at[d, k], rows=rs, chan=cs).wait_recv()

    grad = gbuf[0].astype(F32)
    for src in range(1, ROWS):
        grad = grad + gbuf[src].astype(F32)
    slope = jnp.sum(slv[...], axis=(0, 1))
    slope = jnp.concatenate([slope, slope], axis=1)[None]
    plain_grad = grad * scale - plain * (slope * (scale * scale))
    by_input = jnp.sum(plain_grad * ker, axis=0)
    by_input = jnp.concatenate([by_input, jnp.zeros((128 - ib, by_input.shape[1]), F32)], axis=0)
    style_part = lax.dot_general(
        jnp.ones((8, by_input.shape[1]), F32), by_input, (((1,), (1,)), ((), ())),
        preferred_element_type=F32, precision=lax.Precision.HIGHEST,
    )
    st[pl.ds(b, 1), pl.ds(c, 1)] = style_part[0:1][None, None]
    for db in range(SAMPLES):
        for dc in range(CHANS):
            if db or dc:
                go(remote(
                    st.at[b, c], st.at[b, c], st_s.at[db, dc], st_r.at[db, dc],
                    samples=lax.rem(b + db, SAMPLES), chan=lax.rem(c + dc, CHANS),
                ))
    kg[pl.ds(b, 1)] = (plain_grad * style[None])[None].astype(BF16)
    for d in range(1, SAMPLES):
        go(remote(kg.at[b], kg.at[b], kg_s.at[d], kg_r.at[d], samples=lax.rem(b + d, SAMPLES)))

    for h in range(1, height - 1):
        d_ref[h] = dacc[h + 1].astype(BF16)

    @pl.when(r == 0)
    def _():
        d_ref[0] = dacc[1].astype(BF16)

    @pl.when(not_first)
    def _():
        edge(dsend.at[0], dhalo, dh_s, dh_r, False).wait_recv()
        d_ref[0] = (dacc[1] + dhalo[0].astype(F32)).astype(BF16)

    @pl.when(r == ROWS - 1)
    def _():
        d_ref[height - 1] = dacc[height].astype(BF16)

    @pl.when(not_last)
    def _():
        edge(dsend.at[0], dhalo, dh_s, dh_r, True).wait_recv()
        d_ref[height - 1] = (dacc[height] + dhalo[1].astype(F32)).astype(BF16)

    for d in range(1, SAMPLES):
        src = lax.rem(b + SAMPLES - d, SAMPLES)
        remote(latb.at[src], latb.at[src], in_s.at[0, d], in_r.at[0, d], samples=src).wait_recv()
        remote(selb.at[src], selb.at[src], in_s.at[1, d], in_r.at[1, d], samples=src).wait_recv()
    for db in range(SAMPLES):
        for dc in range(CHANS):
            if db or dc:
                bs, cs = lax.rem(b + SAMPLES - db, SAMPLES), lax.rem(c + CHANS - dc, CHANS)
                remote(
                    st.at[bs, cs], st.at[bs, cs], st_s.at[db, dc], st_r.at[db, dc], samples=bs, chan=cs
                ).wait_recv()

    diagonal = lax.broadcasted_iota(jnp.int32, (ib, 128), 0) == lane_iota((ib, 128))
    style_sum = jnp.zeros((1, 128), F32)
    affine = jnp.zeros(awg_ref.shape, F32)
    for s in range(SAMPLES):
        row = st[s, 0] + st[s, 1] + st[s, 2] + st[s, 3]
        style_sum = style_sum + row
        column = jnp.sum(jnp.where(diagonal, row, 0.0), axis=1, keepdims=True)
        affine = affine + column * latb[s][0:1]
    awg_ref[...] = affine
    abg_ref[...] = style_sum[:, :ib]

    for d in range(1, SAMPLES):
        src = lax.rem(b + SAMPLES - d, SAMPLES)
        remote(kg.at[src], kg.at[src], kg_s.at[d], kg_r.at[d], samples=src).wait_recv()

    for kw in range(3):
        each = [kg[s, kw].astype(F32) for s in range(SAMPLES)]
        for k in range(nb):
            total = sum(selb[s][0:1, k : k + 1] * each[s] for s in range(SAMPLES))
            for kh in range(3):
                bg_ref[k, 3 * kh + kw] = total[:, (2 - kh) * ch : (3 - kh) * ch]

    for copy in sent:
        copy.wait_send()
    for part in range(2):
        @pl.when(2 * c + part != r)
        def _():
            remote(gs.at[0, part], gbuf.at[r], g_s.at[0, part], g_r.at[r], rows=2 * c + part).wait_send()

    @pl.when(not_first)
    def _():
        edge(f_ref.at[0], fhalo, fh_s, fh_r, True).wait_send()
        edge(dsend.at[0], dhalo, dh_s, dh_r, True).wait_send()

    @pl.when(not_last)
    def _():
        edge(f_ref.at[0], fhalo, fh_s, fh_r, False).wait_send()
        edge(dsend.at[1], dhalo, dh_s, dh_r, False).wait_send()


def on_device(feature, out_grad, bank, select, latent, affine_w, affine_b):
    x = jnp.transpose(out_grad[0], (1, 0, 2))
    f = jnp.transpose(feature[0], (1, 0, 2))
    height, ch, width = x.shape
    nb, taps, _, ib = bank.shape
    z = latent.shape[1]
    lanes = 4 * ch
    vmem = pl.BlockSpec(memory_space=pltpu.VMEM)
    dma = pltpu.SemaphoreType.DMA
    d, bg, awg, abg = pl.pallas_call(
        kernel,
        out_shape=(
            jax.ShapeDtypeStruct((height, ch, width), BF16),
            jax.ShapeDtypeStruct((nb, taps, ib, ch), F32),
            jax.ShapeDtypeStruct((ib, z), F32),
            jax.ShapeDtypeStruct((1, ib), F32),
        ),
        in_specs=[vmem] * 7,
        out_specs=(vmem,) * 4,
        scratch_shapes=[
            pltpu.VMEM((height + 5, CHANS, ch, width), BF16),
            pltpu.VMEM((height + 2, 3 * ch, width), BF16),
            pltpu.VMEM((2, ch, width), BF16),
            pltpu.VMEM((ROWS, 3, ib, lanes), BF16),
            pltpu.VMEM((CHANS, 2, 3, ib, lanes), BF16),
            pltpu.VMEM((CHANS, 2, 3, ib, lanes), BF16),
            pltpu.VMEM((ROWS, 3, ib, lanes), BF16),
            pltpu.VMEM((SAMPLES, 8, z), F32),
            pltpu.VMEM((SAMPLES, 8, 128), F32),
            pltpu.VMEM((ROWS, 1, 128), F32),
            pltpu.VMEM((ROWS, CHANS, 1, 128), F32),
            pltpu.VMEM((CHANS, 1, 128), F32),
            pltpu.VMEM((SAMPLES, 3, ib, lanes), BF16),
            pltpu.VMEM((SAMPLES, CHANS, 1, 128), F32),
            pltpu.VMEM((3, ib, lanes), F32),
            pltpu.VMEM((3, ib, lanes), F32),
            pltpu.VMEM((height + 2, ch, width), F32),
            pltpu.VMEM((2, ch, width), BF16),
            pltpu.VMEM((2, ch, width), BF16),
            dma((2, 4)), dma((2, 4)),
            dma((2,)), dma((2,)),
            dma((2,)), dma((2,)),
            dma,
            dma((2, SAMPLES)), dma((2, SAMPLES)),
            dma((ROWS,)), dma((ROWS,)),
            dma((4,)), dma((4,)), dma((4,)), dma((8,)), dma((4,)),
            dma((CHANS, 2)), dma((ROWS,)),
            dma((ROWS, CHANS)), dma((ROWS, CHANS)),
            dma((SAMPLES,)), dma((SAMPLES,)),
            dma((SAMPLES, CHANS)), dma((SAMPLES, CHANS)),
        ],
        compiler_params=pltpu.CompilerParams(
            collective_id=0, has_side_effects=True, vmem_limit_bytes=48 * 1024 * 1024
        ),
    )(
        x, f, jnp.transpose(bank, (0, 1, 3, 2)), select, latent,
        jnp.transpose(affine_w), affine_b[None],
    )
    return (
        jnp.transpose(d, (1, 0, 2))[None],
        jnp.transpose(bg, (0, 1, 3, 2)),
        jnp.transpose(awg),
        abg[0],
    )


def solution(mesh):
    return jax.shard_map(
        on_device,
        mesh=mesh,
        in_specs=(
            P("samples", "chan", "rows", None),
            P("samples", "chan", "rows", None),
            P(None, None, "chan", "rows"),
            P("samples", None),
            P("samples", None),
            P(None, "rows"),
            P("rows"),
        ),
        out_specs=(
            P("samples", "chan", "rows", None),
            P(None, None, "chan", "rows"),
            P(None, "rows"),
            P("rows"),
        ),
        check_vma=False,
    )
```

```python
import jax
import jax.numpy as jnp
from jax import lax
from jax.experimental import pallas as pl
from jax.experimental.pallas import tpu as pltpu
from jax.sharding import PartitionSpec as P

EPS = 1e-08
MESH = pl.DeviceIdType.MESH
ROWS, SAMPLES, CHANS = 8, 4, 4
F32, BF16 = jnp.float32, jnp.bfloat16


def lane_iota(shape):
    return lax.broadcasted_iota(jnp.int32, shape, len(shape) - 1)


def moved_right(x):
    return jnp.where(lane_iota(x.shape) == 0, 0.0, pltpu.roll(x, 1, axis=1))


def moved_left(x):
    width = x.shape[1]
    return jnp.where(lane_iota(x.shape) == width - 1, 0.0, pltpu.roll(x, width - 1, axis=1))


def over_taps(x):
    flat = jnp.sum(x, axis=(0, 1))[None, :]
    half = flat[:, :128] + flat[:, 128:]
    return half + pltpu.roll(half, 64, axis=1)


def kernel(
    x_ref, f_ref, bank_ref, sel_ref, lat_ref, aw_ref, ab_ref,
    d_ref, bg_ref, awg_ref, abg_ref,
    xbuf, fs, fhalo, mown, ms, my, mm, gs, gbuf, latb, selb, en, slv, slo, kg, st, ker_ref, plain_ref, dacc, dsend, dhalo,
    ag_s, ag_r, fh_s, fh_r, dh_s, dh_r, own_s, in_s, in_r, en_s, en_r, ms_s, ms_r, my_s, my_r, mm_s, mm_r,
    g_s, g_r, sl_s, sl_r, kg_s, kg_r, st_s, st_r,
):
    r, b, c = lax.axis_index("rows"), lax.axis_index("samples"), lax.axis_index("chan")
    height, ch, width = x_ref.shape
    nb, ib = bank_ref.shape[0], bank_ref.shape[2]
    left, right, opp = lax.rem(c + 3, CHANS), lax.rem(c + 1, CHANS), lax.rem(c + 2, CHANS)
    tall = 6 * ib

    def remote(src, dst, send, recv, **where):
        return pltpu.make_async_remote_copy(
            src_ref=src, dst_ref=dst, send_sem=send, recv_sem=recv, device_id=where, device_id_type=MESH
        )

    sent = []

    def go(copy):
        copy.start()
        sent.append(copy)

    barrier = pltpu.get_barrier_semaphore()
    greeted = 0
    for dr in range(ROWS):
        for dc in range(CHANS):
            if dr or dc:
                pl.semaphore_signal(
                    barrier, inc=1,
                    device_id={"rows": lax.rem(r + dr, ROWS), "chan": lax.rem(c + dc, CHANS)},
                    device_id_type=MESH,
                )
                greeted += 1
    for db in range(1, SAMPLES):
        for dc in range(CHANS):
            pl.semaphore_signal(
                barrier, inc=1,
                device_id={"samples": lax.rem(b + db, SAMPLES), "chan": lax.rem(c + dc, CHANS)},
                device_id_type=MESH,
            )
            greeted += 1

    lat = lat_ref[...]
    latb[pl.ds(b, 1)] = jnp.broadcast_to(lat[None], (1, 8, lat.shape[1]))
    sel = sel_ref[...].astype(F32)
    selrow = jnp.zeros((8, 128), F32)
    for k in range(nb):
        selrow = jnp.where(lane_iota((8, 128)) == k, sel[:, k : k + 1], selrow)
    selb[pl.ds(b, 1)] = selrow[None]
    square = lax.broadcasted_iota(jnp.int32, (ib, ib), 0) == lane_iota((ib, ib))
    bias = jnp.sum(jnp.where(square, ab_ref[...], 0.0), axis=1, keepdims=True)
    style = jnp.sum(aw_ref[...] * lat, axis=1, keepdims=True) + bias
    ker_ref[...] = jnp.zeros_like(ker_ref)
    for kh in range(3):
        for kw in range(3):
            tap = sum(sel[:, k : k + 1] * bank_ref[k, 3 * kh + kw] for k in range(nb))
            ker_ref[kw, :, (2 - kh) * ch : (3 - kh) * ch] = tap
    ker = ker_ref[...]
    plain_ref[...] = ker * style[None]
    plain = plain_ref[...]
    en[pl.ds(r, 1)] = over_taps(plain * plain)[None]

    own = pltpu.make_async_copy(x_ref, xbuf.at[pl.ds(2, height), c], own_s)
    own.start()

    def shift_into(at, f):
        wide = f.astype(F32)
        for kw, moved in enumerate((moved_right(wide).astype(BF16), f, moved_left(wide).astype(BF16))):
            for part in range(2):
                first = (3 * part + kw) * ib
                fs[at, first : first + ib] = moved[part * ib : (part + 1) * ib]

    def shifted(h, carry):
        shift_into(h + 1, f_ref[h])
        return carry

    lax.fori_loop(0, height, shifted, 0)
    gs[...] = jnp.zeros_like(gs)
    for row in (0, 1, height + 2, height + 3, height + 4):
        xbuf[row] = jnp.zeros(xbuf.shape[1:], BF16)

    pl.semaphore_wait(barrier, greeted)

    for d in range(1, ROWS):
        go(remote(en.at[r], en.at[r], en_s.at[d], en_r.at[d], rows=lax.rem(r + d, ROWS)))
    half = height // 2

    def rows_of(shard, first, count):
        return xbuf.at[pl.ds(first + 2, count), shard]

    to_right, to_left = {"chan": right}, {"chan": left}
    go(remote(x_ref.at[pl.ds(0, half)], rows_of(c, 0, half), ag_s.at[0, 0], ag_r.at[0, 0], **to_right))
    go(remote(x_ref.at[pl.ds(half, half)], rows_of(c, half, half), ag_s.at[1, 0], ag_r.at[1, 0], **to_left))

    def edge(src, dst, send, recv, up):
        there = jnp.maximum(r - 1, 0) if up else jnp.minimum(r + 1, ROWS - 1)
        i = 0 if up else 1
        return remote(src, dst.at[1 - i], send.at[i], recv.at[1 - i], rows=there)

    not_first, not_last = r > 0, r < ROWS - 1

    @pl.when(not_first)
    def _():
        edge(f_ref.at[0], fhalo, fh_s, fh_r, True).start()

    @pl.when(not_last)
    def _():
        edge(f_ref.at[height - 1], fhalo, fh_s, fh_r, False).start()

    go(remote(x_ref.at[pl.ds(half, half)], rows_of(c, half, half), ag_s.at[0, 1], ag_r.at[0, 1], **to_right))
    go(remote(x_ref.at[pl.ds(0, half)], rows_of(c, 0, half), ag_s.at[1, 1], ag_r.at[1, 1], **to_left))
    for d in range(1, SAMPLES):
        there = lax.rem(b + d, SAMPLES)
        go(remote(latb.at[b], latb.at[b], in_s.at[0, d], in_r.at[0, d], samples=there))
        go(remote(selb.at[b], selb.at[b], in_s.at[1, d], in_r.at[1, d], samples=there))

    for d in range(1, ROWS):
        src = lax.rem(r + ROWS - d, ROWS)
        remote(en.at[src], en.at[src], en_s.at[d], en_r.at[d], rows=src).wait_recv()
    scale = lax.rsqrt(jnp.sum(en[...], axis=0) + EPS)
    scale = jnp.concatenate([scale, scale], axis=1)[None]

    side, level = r // 4, lax.rem(r, 4)
    tile, lanes = 3 * ib // 2, 128
    modulated = (plain * scale).astype(BF16).reshape(3 * ib, 4 * ch)
    for quarter in range(4):
        top, start = (quarter // 2) * tile, (quarter % 2) * lanes
        mown[quarter] = modulated[top : top + tile, start : start + lanes]
    ms[pl.ds(r, 1)] = mown[pl.ds(level, 1)]
    for d in range(1, ROWS):
        there = lax.rem(r + d, ROWS)
        go(remote(mown.at[lax.rem(there, 4)], ms.at[r], ms_s.at[d], ms_r.at[d], rows=there))

    @pl.when(not_first)
    def _():
        edge(f_ref.at[0], fhalo, fh_s, fh_r, False).wait_recv()
        shift_into(0, fhalo[0])

    @pl.when(r == 0)
    def _():
        fs[0] = jnp.zeros(fs.shape[1:], BF16)

    @pl.when(not_last)
    def _():
        edge(f_ref.at[0], fhalo, fh_s, fh_r, True).wait_recv()
        shift_into(height + 1, fhalo[1])

    @pl.when(r == ROWS - 1)
    def _():
        fs[height + 1] = jnp.zeros(fs.shape[1:], BF16)

    def grad_rows(acc, shard, first, count):
        def step(q, acc):
            around = xbuf[pl.ds(q, 3), shard].reshape(3 * ch, width)
            return acc + lax.dot_general(
                fs[q], around, (((1,), (1,)), ((), ())), preferred_element_type=F32
            )

        return lax.fori_loop(first, first + count, step, acc)

    no_grad = jnp.zeros((tall, 3 * ch), F32)

    def send_grad(i, shard, acc):
        gs[i, :, :, : 3 * ch] = acc.reshape(2, 3 * ib, 3 * ch).astype(BF16)
        for part in range(2):
            src = gs.at[i, part]
            target = 2 * c + part
            if i == 0:
                @pl.when(target == r)
                def _():
                    pltpu.make_async_copy(src, gbuf.at[r], g_r.at[r]).start()

                @pl.when(target != r)
                def _():
                    remote(src, gbuf.at[r], g_s.at[i, part], g_r.at[r], rows=target).start()
            else:
                go(remote(src, gbuf.at[r], g_s.at[i, part], g_r.at[r], rows=target, chan=shard))

    own.wait()
    send_grad(0, c, grad_rows(no_grad, c, 0, height + 2))

    most = half - 1

    def from_left(k, first, count, shard):
        return remote(rows_of(shard, first, count), rows_of(shard, first, count), ag_s.at[0, k], ag_r.at[0, k], **to_right)

    def from_right(k, first, count, shard):
        return remote(rows_of(shard, first, count), rows_of(shard, first, count), ag_s.at[1, k], ag_r.at[1, k], **to_left)

    from_left(0, 0, half, left).wait_recv()
    go(from_left(2, 0, most, left))
    go(from_left(3, most, 1, left))
    from_right(0, half, half, right).wait_recv()
    go(from_right(2, half + 1, most, right))
    go(from_right(3, half, 1, right))

    for d in range(1, ROWS):
        src = lax.rem(r + ROWS - d, ROWS)
        remote(mown.at[0], ms.at[src], ms_s.at[d], ms_r.at[d], rows=src).wait_recv()
    my[pl.ds(c, 1)] = ms[pl.ds(2 * c, 2)][None]
    for d in (1, 3, 2):
        there = lax.rem(c + d, CHANS)
        go(remote(ms.at[pl.ds(2 * there, 2)], my.at[c], my_s.at[d], my_r.at[d], chan=there))

    from_left(1, half, half, left).wait_recv()

    for d in range(1, CHANS):
        src = lax.rem(c + CHANS - d, CHANS)
        remote(ms.at[pl.ds(0, 2)], my.at[src], my_s.at[d], my_r.at[d], chan=src).wait_recv()

    def quarter_of(level):
        top = pl.multiple_of((level // 2) * tile, tile)
        start = pl.multiple_of(lax.rem(level, 2) * lanes, lanes)
        return mm.at[:, :, pl.ds(top, tile), pl.ds(start, lanes)]

    def peer(d):
        return 4 * side + lax.rem(level + d, 4)

    mine = pltpu.make_async_copy(my, quarter_of(level), mm_r.at[0])
    mine.start()
    for d in (1, 3, 2):
        go(remote(my, quarter_of(level), mm_s.at[d], mm_r.at[d], rows=peer(d)))

    send_grad(1, left, grad_rows(no_grad, left, 0, height + 2))

    from_right(1, 0, half, right).wait_recv()

    send_grad(2, right, grad_rows(no_grad, right, 0, height + 2))

    def send_slope(i, k, shard):
        parts = gs[i].astype(F32) * mm[shard].astype(F32)
        slo[i] = over_taps(parts)
        for d in range(ROWS):
            if k == 0 and d == 0:
                slv[pl.ds(r, 1), pl.ds(c, 1)] = slo[0][None, None]
            else:
                go(remote(
                    slo.at[i], slv.at[r, c], sl_s.at[d, k], sl_r.at[d, k], rows=lax.rem(r + d, ROWS), chan=shard
                ))

    from_left(2, 0, most, opp).wait_recv()
    from_right(2, half + 1, most, opp).wait_recv()

    acc = grad_rows(no_grad, opp, 0, most)
    acc = grad_rows(acc, opp, height + 2 - most, most)

    for d in range(1, 4):
        src = peer(4 - d)
        remote(my, quarter_of(lax.rem(src, 4)), mm_s.at[d], mm_r.at[d], rows=src).wait_recv()
    mine.wait()
    send_slope(0, 0, c)
    send_slope(1, 3, left)
    send_slope(2, 1, right)

    from_left(3, most, 1, opp).wait_recv()
    from_right(3, half, 1, opp).wait_recv()

    send_grad(3, opp, grad_rows(acc, opp, most, height + 2 - 2 * most))
    send_slope(3, 2, opp)

    def rows_out(q, carry):
        total = jnp.zeros((tall, width), F32)
        for shard in range(CHANS):
            around = xbuf[pl.ds(q, 4), shard].reshape(4 * ch, width)
            total = total + jnp.dot(mm[shard].reshape(tall, 4 * ch), around, preferred_element_type=F32)
        for part in range(2):
            t = total[3 * part * ib : 3 * (part + 1) * ib]
            dacc[q, part * ib : (part + 1) * ib] = t[ib : 2 * ib] + moved_left(t[:ib]) + moved_right(t[2 * ib :])
        return carry

    lax.fori_loop(0, height + 2, rows_out, 0)
    dsend[0] = dacc[0].astype(BF16)
    dsend[1] = dacc[height + 1].astype(BF16)

    @pl.when(not_first)
    def _():
        edge(dsend.at[0], dhalo, dh_s, dh_r, True).start()

    @pl.when(not_last)
    def _():
        edge(dsend.at[1], dhalo, dh_s, dh_r, False).start()

    for src in range(ROWS):
        remote(gs.at[0, 0], gbuf.at[src], g_s.at[0, 0], g_r.at[src], rows=lax.rem(r + 1, ROWS)).wait_recv()

    for d in range(ROWS):
        for k in range(CHANS):
            if d or k:
                rs, cs = lax.rem(r + ROWS - d, ROWS), lax.rem(c + CHANS - k, CHANS)
                remote(slo.at[0], slv.at[rs, cs], sl_s.at[d, k], sl_r.at[d, k], rows=rs, chan=cs).wait_recv()

    grad = gbuf[0].astype(F32)
    for src in range(1, ROWS):
        grad = grad + gbuf[src].astype(F32)
    grad = grad.reshape(3, ib, 4 * ch)
    slope = jnp.sum(slv[...], axis=(0, 1))
    slope = jnp.concatenate([slope, slope], axis=1)[None]
    plain_grad = grad * scale - plain * (slope * (scale * scale))
    by_input = jnp.sum(plain_grad * ker, axis=0)
    by_input = jnp.concatenate([by_input, jnp.zeros((128 - ib, by_input.shape[1]), F32)], axis=0)
    style_part = lax.dot_general(
        jnp.ones((8, by_input.shape[1]), F32), by_input, (((1,), (1,)), ((), ())),
        preferred_element_type=F32, precision=lax.Precision.HIGHEST,
    )
    st[pl.ds(b, 1), pl.ds(c, 1)] = style_part[0:1][None, None]
    for db in range(SAMPLES):
        for dc in range(CHANS):
            if db or dc:
                go(remote(
                    st.at[b, c], st.at[b, c], st_s.at[db, dc], st_r.at[db, dc],
                    samples=lax.rem(b + db, SAMPLES), chan=lax.rem(c + dc, CHANS),
                ))
    kg[pl.ds(b, 1)] = (plain_grad * style[None])[None].astype(BF16)
    for d in range(1, SAMPLES):
        go(remote(kg.at[b], kg.at[b], kg_s.at[d], kg_r.at[d], samples=lax.rem(b + d, SAMPLES)))

    for h in range(1, height - 1):
        d_ref[h] = dacc[h + 1].astype(BF16)

    @pl.when(r == 0)
    def _():
        d_ref[0] = dacc[1].astype(BF16)

    @pl.when(not_first)
    def _():
        edge(dsend.at[0], dhalo, dh_s, dh_r, False).wait_recv()
        d_ref[0] = (dacc[1] + dhalo[0].astype(F32)).astype(BF16)

    @pl.when(r == ROWS - 1)
    def _():
        d_ref[height - 1] = dacc[height].astype(BF16)

    @pl.when(not_last)
    def _():
        edge(dsend.at[0], dhalo, dh_s, dh_r, True).wait_recv()
        d_ref[height - 1] = (dacc[height] + dhalo[1].astype(F32)).astype(BF16)

    for d in range(1, SAMPLES):
        src = lax.rem(b + SAMPLES - d, SAMPLES)
        remote(latb.at[src], latb.at[src], in_s.at[0, d], in_r.at[0, d], samples=src).wait_recv()
        remote(selb.at[src], selb.at[src], in_s.at[1, d], in_r.at[1, d], samples=src).wait_recv()
    for db in range(SAMPLES):
        for dc in range(CHANS):
            if db or dc:
                bs, cs = lax.rem(b + SAMPLES - db, SAMPLES), lax.rem(c + CHANS - dc, CHANS)
                remote(
                    st.at[bs, cs], st.at[bs, cs], st_s.at[db, dc], st_r.at[db, dc], samples=bs, chan=cs
                ).wait_recv()

    diagonal = lax.broadcasted_iota(jnp.int32, (ib, 128), 0) == lane_iota((ib, 128))
    style_sum = jnp.zeros((1, 128), F32)
    affine = jnp.zeros(awg_ref.shape, F32)
    for s in range(SAMPLES):
        row = st[s, 0] + st[s, 1] + st[s, 2] + st[s, 3]
        style_sum = style_sum + row
        column = jnp.sum(jnp.where(diagonal, row, 0.0), axis=1, keepdims=True)
        affine = affine + column * latb[s][0:1]
    awg_ref[...] = affine
    abg_ref[...] = style_sum[:, :ib]

    for d in range(1, SAMPLES):
        src = lax.rem(b + SAMPLES - d, SAMPLES)
        remote(kg.at[src], kg.at[src], kg_s.at[d], kg_r.at[d], samples=src).wait_recv()

    for kw in range(3):
        each = [kg[s, kw].astype(F32) for s in range(SAMPLES)]
        for k in range(nb):
            total = sum(selb[s][0:1, k : k + 1] * each[s] for s in range(SAMPLES))
            for kh in range(3):
                bg_ref[k, 3 * kh + kw] = total[:, (2 - kh) * ch : (3 - kh) * ch]

    for copy in sent:
        copy.wait_send()
    for part in range(2):
        @pl.when(2 * c + part != r)
        def _():
            remote(gs.at[0, part], gbuf.at[r], g_s.at[0, part], g_r.at[r], rows=2 * c + part).wait_send()

    @pl.when(not_first)
    def _():
        edge(f_ref.at[0], fhalo, fh_s, fh_r, True).wait_send()
        edge(dsend.at[0], dhalo, dh_s, dh_r, True).wait_send()

    @pl.when(not_last)
    def _():
        edge(f_ref.at[0], fhalo, fh_s, fh_r, False).wait_send()
        edge(dsend.at[1], dhalo, dh_s, dh_r, False).wait_send()


def on_device(feature, out_grad, bank, select, latent, affine_w, affine_b):
    x = jnp.transpose(out_grad[0], (1, 0, 2))
    f = jnp.transpose(feature[0], (1, 0, 2))
    height, ch, width = x.shape
    nb, taps, _, ib = bank.shape
    z = latent.shape[1]
    lanes = 4 * ch
    vmem = pl.BlockSpec(memory_space=pltpu.VMEM)
    dma = pltpu.SemaphoreType.DMA
    d, bg, awg, abg = pl.pallas_call(
        kernel,
        out_shape=(
            jax.ShapeDtypeStruct((height, ch, width), BF16),
            jax.ShapeDtypeStruct((nb, taps, ib, ch), F32),
            jax.ShapeDtypeStruct((ib, z), F32),
            jax.ShapeDtypeStruct((1, ib), F32),
        ),
        in_specs=[vmem] * 7,
        out_specs=(vmem,) * 4,
        scratch_shapes=[
            pltpu.VMEM((height + 5, CHANS, ch, width), BF16),
            pltpu.VMEM((height + 2, 3 * ch, width), BF16),
            pltpu.VMEM((2, ch, width), BF16),
            pltpu.VMEM((4, 3 * ib // 2, 128), BF16),
            pltpu.VMEM((ROWS, 3 * ib // 2, 128), BF16),
            pltpu.VMEM((CHANS, 2, 3 * ib // 2, 128), BF16),
            pltpu.VMEM((CHANS, 2, 3 * ib, lanes), BF16),
            pltpu.VMEM((CHANS, 2, 3 * ib, lanes), BF16),
            pltpu.VMEM((ROWS, 3 * ib, lanes), BF16),
            pltpu.VMEM((SAMPLES, 8, z), F32),
            pltpu.VMEM((SAMPLES, 8, 128), F32),
            pltpu.VMEM((ROWS, 1, 128), F32),
            pltpu.VMEM((ROWS, CHANS, 1, 128), F32),
            pltpu.VMEM((CHANS, 1, 128), F32),
            pltpu.VMEM((SAMPLES, 3, ib, lanes), BF16),
            pltpu.VMEM((SAMPLES, CHANS, 1, 128), F32),
            pltpu.VMEM((3, ib, lanes), F32),
            pltpu.VMEM((3, ib, lanes), F32),
            pltpu.VMEM((height + 2, ch, width), F32),
            pltpu.VMEM((2, ch, width), BF16),
            pltpu.VMEM((2, ch, width), BF16),
            dma((2, 4)), dma((2, 4)),
            dma((2,)), dma((2,)),
            dma((2,)), dma((2,)),
            dma,
            dma((2, SAMPLES)), dma((2, SAMPLES)),
            dma((ROWS,)), dma((ROWS,)),
            dma((ROWS,)), dma((ROWS,)), dma((CHANS,)), dma((CHANS,)), dma((4,)), dma((4,)),
            dma((CHANS, 2)), dma((ROWS,)),
            dma((ROWS, CHANS)), dma((ROWS, CHANS)),
            dma((SAMPLES,)), dma((SAMPLES,)),
            dma((SAMPLES, CHANS)), dma((SAMPLES, CHANS)),
        ],
        compiler_params=pltpu.CompilerParams(
            collective_id=0, has_side_effects=True, vmem_limit_bytes=48 * 1024 * 1024
        ),
    )(
        x, f, jnp.transpose(bank, (0, 1, 3, 2)), select, latent,
        jnp.transpose(affine_w), affine_b[None],
    )
    return (
        jnp.transpose(d, (1, 0, 2))[None],
        jnp.transpose(bg, (0, 1, 3, 2)),
        jnp.transpose(awg),
        abg[0],
    )


def solution(mesh):
    return jax.shard_map(
        on_device,
        mesh=mesh,
        in_specs=(
            P("samples", "chan", "rows", None),
            P("samples", "chan", "rows", None),
            P(None, None, "chan", "rows"),
            P("samples", None),
            P("samples", None),
            P(None, "rows"),
            P("rows"),
        ),
        out_specs=(
            P("samples", "chan", "rows", None),
            P(None, None, "chan", "rows"),
            P(None, "rows"),
            P("rows"),
        ),
        check_vma=False,
    )
```

```python
import jax
import jax.numpy as jnp
from jax import lax
from jax.experimental import pallas as pl
from jax.experimental.pallas import tpu as pltpu
from jax.sharding import PartitionSpec as P

EPS = 1e-08
MESH = pl.DeviceIdType.MESH
ROWS, SAMPLES, CHANS = 8, 4, 4
F32, BF16 = jnp.float32, jnp.bfloat16


def lane_iota(shape):
    return lax.broadcasted_iota(jnp.int32, shape, len(shape) - 1)


def moved_right(x):
    return jnp.where(lane_iota(x.shape) == 0, 0.0, pltpu.roll(x, 1, axis=1))


def moved_left(x):
    width = x.shape[1]
    return jnp.where(lane_iota(x.shape) == width - 1, 0.0, pltpu.roll(x, width - 1, axis=1))


def over_taps(x):
    flat = jnp.sum(x, axis=(0, 1))[None, :]
    half = flat[:, :128] + flat[:, 128:]
    return half + pltpu.roll(half, 64, axis=1)


def kernel(
    x_ref, f_ref, bank_ref, sel_ref, lat_ref, aw_ref, ab_ref,
    d_ref, bg_ref, awg_ref, abg_ref,
    xbuf, fs, fhalo, mown, ms, my, mm, gs, gbuf, latb, selb, en, slv, slo, kg, st, ker_ref, plain_ref, dacc, dsend, dhalo,
    ag_s, ag_r, fh_s, fh_r, dh_s, dh_r, own_s, in_s, in_r, en_s, en_r, ms_s, ms_r, my_s, my_r, mm_s, mm_r,
    g_s, g_r, sl_s, sl_r, kg_s, kg_r, st_s, st_r,
):
    r, b, c = lax.axis_index("rows"), lax.axis_index("samples"), lax.axis_index("chan")
    height, ch, width = x_ref.shape
    nb, ib = bank_ref.shape[0], bank_ref.shape[2]
    left, right, opp = lax.rem(c + 3, CHANS), lax.rem(c + 1, CHANS), lax.rem(c + 2, CHANS)
    tall = 6 * ib

    def remote(src, dst, send, recv, **where):
        return pltpu.make_async_remote_copy(
            src_ref=src, dst_ref=dst, send_sem=send, recv_sem=recv, device_id=where, device_id_type=MESH
        )

    sent = []

    def go(copy):
        copy.start()
        sent.append(copy)

    barrier = pltpu.get_barrier_semaphore()
    greeted = 0
    for dr in range(ROWS):
        for dc in range(CHANS):
            if dr or dc:
                pl.semaphore_signal(
                    barrier, inc=1,
                    device_id={"rows": lax.rem(r + dr, ROWS), "chan": lax.rem(c + dc, CHANS)},
                    device_id_type=MESH,
                )
                greeted += 1
    for db in range(1, SAMPLES):
        for dc in range(CHANS):
            pl.semaphore_signal(
                barrier, inc=1,
                device_id={"samples": lax.rem(b + db, SAMPLES), "chan": lax.rem(c + dc, CHANS)},
                device_id_type=MESH,
            )
            greeted += 1

    lat = lat_ref[...]
    latb[pl.ds(b, 1)] = jnp.broadcast_to(lat[None], (1, 8, lat.shape[1]))
    sel = sel_ref[...].astype(F32)
    selrow = jnp.zeros((8, 128), F32)
    for k in range(nb):
        selrow = jnp.where(lane_iota((8, 128)) == k, sel[:, k : k + 1], selrow)
    selb[pl.ds(b, 1)] = selrow[None]
    square = lax.broadcasted_iota(jnp.int32, (ib, ib), 0) == lane_iota((ib, ib))
    bias = jnp.sum(jnp.where(square, ab_ref[...], 0.0), axis=1, keepdims=True)
    style = jnp.sum(aw_ref[...] * lat, axis=1, keepdims=True) + bias
    ker_ref[...] = jnp.zeros_like(ker_ref)
    for kh in range(3):
        for kw in range(3):
            tap = sum(sel[:, k : k + 1] * bank_ref[k, 3 * kh + kw] for k in range(nb))
            ker_ref[kw, :, (2 - kh) * ch : (3 - kh) * ch] = tap
    ker = ker_ref[...]
    plain_ref[...] = ker * style[None]
    plain = plain_ref[...]
    en[pl.ds(r, 1)] = over_taps(plain * plain)[None]

    own = pltpu.make_async_copy(x_ref, xbuf.at[pl.ds(2, height), c], own_s)
    own.start()

    def shift_into(at, f):
        wide = f.astype(F32)
        for kw, moved in enumerate((moved_right(wide).astype(BF16), f, moved_left(wide).astype(BF16))):
            for part in range(2):
                first = (3 * part + kw) * ib
                fs[at, first : first + ib] = moved[part * ib : (part + 1) * ib]

    def shifted(h, carry):
        shift_into(h + 1, f_ref[h])
        return carry

    lax.fori_loop(0, height, shifted, 0)
    gs[...] = jnp.zeros_like(gs)
    for row in (0, 1, height + 2, height + 3, height + 4):
        xbuf[row] = jnp.zeros(xbuf.shape[1:], BF16)

    pl.semaphore_wait(barrier, greeted)

    for d in range(1, ROWS):
        go(remote(en.at[r], en.at[r], en_s.at[d], en_r.at[d], rows=lax.rem(r + d, ROWS)))
    half = height // 2

    def rows_of(shard, first, count):
        return xbuf.at[pl.ds(first + 2, count), shard]

    to_right, to_left = {"chan": right}, {"chan": left}
    go(remote(x_ref.at[pl.ds(0, half)], rows_of(c, 0, half), ag_s.at[0, 0], ag_r.at[0, 0], **to_right))
    go(remote(x_ref.at[pl.ds(half, half)], rows_of(c, half, half), ag_s.at[1, 0], ag_r.at[1, 0], **to_left))

    def edge(src, dst, send, recv, up):
        there = jnp.maximum(r - 1, 0) if up else jnp.minimum(r + 1, ROWS - 1)
        i = 0 if up else 1
        return remote(src, dst.at[1 - i], send.at[i], recv.at[1 - i], rows=there)

    not_first, not_last = r > 0, r < ROWS - 1

    @pl.when(not_first)
    def _():
        edge(f_ref.at[0], fhalo, fh_s, fh_r, True).start()

    @pl.when(not_last)
    def _():
        edge(f_ref.at[height - 1], fhalo, fh_s, fh_r, False).start()

    go(remote(x_ref.at[pl.ds(half, half)], rows_of(c, half, half), ag_s.at[0, 1], ag_r.at[0, 1], **to_right))
    go(remote(x_ref.at[pl.ds(0, half)], rows_of(c, 0, half), ag_s.at[1, 1], ag_r.at[1, 1], **to_left))
    for d in range(1, SAMPLES):
        there = lax.rem(b + d, SAMPLES)
        go(remote(latb.at[b], latb.at[b], in_s.at[0, d], in_r.at[0, d], samples=there))
        go(remote(selb.at[b], selb.at[b], in_s.at[1, d], in_r.at[1, d], samples=there))

    for d in range(1, ROWS):
        src = lax.rem(r + ROWS - d, ROWS)
        remote(en.at[src], en.at[src], en_s.at[d], en_r.at[d], rows=src).wait_recv()
    scale = lax.rsqrt(jnp.sum(en[...], axis=0) + EPS)
    scale = jnp.concatenate([scale, scale], axis=1)[None]

    side, level = r // 4, lax.rem(r, 4)
    tile, lanes = 3 * ib // 2, 128
    modulated = (plain * scale).astype(BF16).reshape(3 * ib, 4 * ch)
    for quarter in range(4):
        top, start = (quarter // 2) * tile, (quarter % 2) * lanes
        mown[quarter] = modulated[top : top + tile, start : start + lanes]
    ms[pl.ds(r, 1)] = mown[pl.ds(level, 1)]
    for d in range(1, ROWS):
        there = lax.rem(r + d, ROWS)
        go(remote(mown.at[lax.rem(there, 4)], ms.at[r], ms_s.at[d], ms_r.at[d], rows=there))

    @pl.when(not_first)
    def _():
        edge(f_ref.at[0], fhalo, fh_s, fh_r, False).wait_recv()
        shift_into(0, fhalo[0])

    @pl.when(r == 0)
    def _():
        fs[0] = jnp.zeros(fs.shape[1:], BF16)

    @pl.when(not_last)
    def _():
        edge(f_ref.at[0], fhalo, fh_s, fh_r, True).wait_recv()
        shift_into(height + 1, fhalo[1])

    @pl.when(r == ROWS - 1)
    def _():
        fs[height + 1] = jnp.zeros(fs.shape[1:], BF16)

    def grad_rows(acc, shard, first, count):
        def step(q, acc):
            around = xbuf[pl.ds(q, 3), shard].reshape(3 * ch, width)
            return acc + lax.dot_general(
                fs[q], around, (((1,), (1,)), ((), ())), preferred_element_type=F32
            )

        return lax.fori_loop(first, first + count, step, acc)

    no_grad = jnp.zeros((tall, 3 * ch), F32)

    def send_grad(i, shard, acc):
        gs[i, :, :, : 3 * ch] = acc.reshape(2, 3 * ib, 3 * ch).astype(BF16)
        for part in range(2):
            src = gs.at[i, part]
            target = 2 * c + part
            if i == 0:
                @pl.when(target == r)
                def _():
                    pltpu.make_async_copy(src, gbuf.at[r], g_r.at[r]).start()

                @pl.when(target != r)
                def _():
                    remote(src, gbuf.at[r], g_s.at[i, part], g_r.at[r], rows=target).start()
            else:
                go(remote(src, gbuf.at[r], g_s.at[i, part], g_r.at[r], rows=target, chan=shard))

    own.wait()
    send_grad(0, c, grad_rows(no_grad, c, 0, height + 2))

    most = half - 1

    def from_left(k, first, count, shard):
        return remote(rows_of(shard, first, count), rows_of(shard, first, count), ag_s.at[0, k], ag_r.at[0, k], **to_right)

    def from_right(k, first, count, shard):
        return remote(rows_of(shard, first, count), rows_of(shard, first, count), ag_s.at[1, k], ag_r.at[1, k], **to_left)

    for d in range(1, ROWS):
        src = lax.rem(r + ROWS - d, ROWS)
        remote(mown.at[0], ms.at[src], ms_s.at[d], ms_r.at[d], rows=src).wait_recv()
    my[pl.ds(c, 1)] = ms[pl.ds(2 * c, 2)][None]
    for d in (1, 3, 2):
        there = lax.rem(c + d, CHANS)
        go(remote(ms.at[pl.ds(2 * there, 2)], my.at[c], my_s.at[d], my_r.at[d], chan=there))

    from_left(0, 0, half, left).wait_recv()
    go(from_left(2, 0, most, left))
    go(from_left(3, most, 1, left))
    from_right(0, half, half, right).wait_recv()
    go(from_right(2, half + 1, most, right))
    go(from_right(3, half, 1, right))

    from_left(1, half, half, left).wait_recv()

    for d in range(1, CHANS):
        src = lax.rem(c + CHANS - d, CHANS)
        remote(ms.at[pl.ds(0, 2)], my.at[src], my_s.at[d], my_r.at[d], chan=src).wait_recv()

    def quarter_of(level):
        top = pl.multiple_of((level // 2) * tile, tile)
        start = pl.multiple_of(lax.rem(level, 2) * lanes, lanes)
        return mm.at[:, :, pl.ds(top, tile), pl.ds(start, lanes)]

    def peer(d):
        return 4 * side + lax.rem(level + d, 4)

    mine = pltpu.make_async_copy(my, quarter_of(level), mm_r.at[0])
    mine.start()
    for d in (1, 3, 2):
        go(remote(my, quarter_of(level), mm_s.at[d], mm_r.at[d], rows=peer(d)))

    send_grad(1, left, grad_rows(no_grad, left, 0, height + 2))

    from_right(1, 0, half, right).wait_recv()

    send_grad(2, right, grad_rows(no_grad, right, 0, height + 2))

    def send_slope(i, k, shard):
        parts = gs[i].astype(F32) * mm[shard].astype(F32)
        slo[i] = over_taps(parts)
        for d in range(ROWS):
            if k == 0 and d == 0:
                slv[pl.ds(r, 1), pl.ds(c, 1)] = slo[0][None, None]
            else:
                go(remote(
                    slo.at[i], slv.at[r, c], sl_s.at[d, k], sl_r.at[d, k], rows=lax.rem(r + d, ROWS), chan=shard
                ))

    from_left(2, 0, most, opp).wait_recv()
    from_right(2, half + 1, most, opp).wait_recv()

    acc = grad_rows(no_grad, opp, 0, most)
    acc = grad_rows(acc, opp, height + 2 - most, most)

    for d in range(1, 4):
        src = peer(4 - d)
        remote(my, quarter_of(lax.rem(src, 4)), mm_s.at[d], mm_r.at[d], rows=src).wait_recv()
    mine.wait()
    send_slope(0, 0, c)
    send_slope(1, 3, left)
    send_slope(2, 1, right)

    from_left(3, most, 1, opp).wait_recv()
    from_right(3, half, 1, opp).wait_recv()

    send_grad(3, opp, grad_rows(acc, opp, most, height + 2 - 2 * most))
    send_slope(3, 2, opp)

    def rows_out(q, carry):
        total = jnp.zeros((tall, width), F32)
        for shard in range(CHANS):
            around = xbuf[pl.ds(q, 4), shard].reshape(4 * ch, width)
            total = total + jnp.dot(mm[shard].reshape(tall, 4 * ch), around, preferred_element_type=F32)
        for part in range(2):
            t = total[3 * part * ib : 3 * (part + 1) * ib]
            dacc[q, part * ib : (part + 1) * ib] = t[ib : 2 * ib] + moved_left(t[:ib]) + moved_right(t[2 * ib :])
        return carry

    lax.fori_loop(0, height + 2, rows_out, 0)
    dsend[0] = dacc[0].astype(BF16)
    dsend[1] = dacc[height + 1].astype(BF16)

    @pl.when(not_first)
    def _():
        edge(dsend.at[0], dhalo, dh_s, dh_r, True).start()

    @pl.when(not_last)
    def _():
        edge(dsend.at[1], dhalo, dh_s, dh_r, False).start()

    for src in range(ROWS):
        remote(gs.at[0, 0], gbuf.at[src], g_s.at[0, 0], g_r.at[src], rows=lax.rem(r + 1, ROWS)).wait_recv()

    for d in range(ROWS):
        for k in range(CHANS):
            if d or k:
                rs, cs = lax.rem(r + ROWS - d, ROWS), lax.rem(c + CHANS - k, CHANS)
                remote(slo.at[0], slv.at[rs, cs], sl_s.at[d, k], sl_r.at[d, k], rows=rs, chan=cs).wait_recv()

    grad = gbuf[0].astype(F32)
    for src in range(1, ROWS):
        grad = grad + gbuf[src].astype(F32)
    grad = grad.reshape(3, ib, 4 * ch)
    slope = jnp.sum(slv[...], axis=(0, 1))
    slope = jnp.concatenate([slope, slope], axis=1)[None]
    plain_grad = grad * scale - plain * (slope * (scale * scale))
    by_input = jnp.sum(plain_grad * ker, axis=0)
    by_input = jnp.concatenate([by_input, jnp.zeros((128 - ib, by_input.shape[1]), F32)], axis=0)
    style_part = lax.dot_general(
        jnp.ones((8, by_input.shape[1]), F32), by_input, (((1,), (1,)), ((), ())),
        preferred_element_type=F32, precision=lax.Precision.HIGHEST,
    )
    st[pl.ds(b, 1), pl.ds(c, 1)] = style_part[0:1][None, None]
    for db in range(SAMPLES):
        for dc in range(CHANS):
            if db or dc:
                go(remote(
                    st.at[b, c], st.at[b, c], st_s.at[db, dc], st_r.at[db, dc],
                    samples=lax.rem(b + db, SAMPLES), chan=lax.rem(c + dc, CHANS),
                ))
    kg[pl.ds(b, 1)] = (plain_grad * style[None])[None].astype(BF16)
    for d in range(1, SAMPLES):
        go(remote(kg.at[b], kg.at[b], kg_s.at[d], kg_r.at[d], samples=lax.rem(b + d, SAMPLES)))

    for h in range(1, height - 1):
        d_ref[h] = dacc[h + 1].astype(BF16)

    @pl.when(r == 0)
    def _():
        d_ref[0] = dacc[1].astype(BF16)

    @pl.when(not_first)
    def _():
        edge(dsend.at[0], dhalo, dh_s, dh_r, False).wait_recv()
        d_ref[0] = (dacc[1] + dhalo[0].astype(F32)).astype(BF16)

    @pl.when(r == ROWS - 1)
    def _():
        d_ref[height - 1] = dacc[height].astype(BF16)

    @pl.when(not_last)
    def _():
        edge(dsend.at[0], dhalo, dh_s, dh_r, True).wait_recv()
        d_ref[height - 1] = (dacc[height] + dhalo[1].astype(F32)).astype(BF16)

    for d in range(1, SAMPLES):
        src = lax.rem(b + SAMPLES - d, SAMPLES)
        remote(latb.at[src], latb.at[src], in_s.at[0, d], in_r.at[0, d], samples=src).wait_recv()
        remote(selb.at[src], selb.at[src], in_s.at[1, d], in_r.at[1, d], samples=src).wait_recv()
    for db in range(SAMPLES):
        for dc in range(CHANS):
            if db or dc:
                bs, cs = lax.rem(b + SAMPLES - db, SAMPLES), lax.rem(c + CHANS - dc, CHANS)
                remote(
                    st.at[bs, cs], st.at[bs, cs], st_s.at[db, dc], st_r.at[db, dc], samples=bs, chan=cs
                ).wait_recv()

    diagonal = lax.broadcasted_iota(jnp.int32, (ib, 128), 0) == lane_iota((ib, 128))
    style_sum = jnp.zeros((1, 128), F32)
    affine = jnp.zeros(awg_ref.shape, F32)
    for s in range(SAMPLES):
        row = st[s, 0] + st[s, 1] + st[s, 2] + st[s, 3]
        style_sum = style_sum + row
        column = jnp.sum(jnp.where(diagonal, row, 0.0), axis=1, keepdims=True)
        affine = affine + column * latb[s][0:1]
    awg_ref[...] = affine
    abg_ref[...] = style_sum[:, :ib]

    for d in range(1, SAMPLES):
        src = lax.rem(b + SAMPLES - d, SAMPLES)
        remote(kg.at[src], kg.at[src], kg_s.at[d], kg_r.at[d], samples=src).wait_recv()

    for kw in range(3):
        each = [kg[s, kw].astype(F32) for s in range(SAMPLES)]
        for k in range(nb):
            total = sum(selb[s][0:1, k : k + 1] * each[s] for s in range(SAMPLES))
            for kh in range(3):
                bg_ref[k, 3 * kh + kw] = total[:, (2 - kh) * ch : (3 - kh) * ch]

    for copy in sent:
        copy.wait_send()
    for part in range(2):
        @pl.when(2 * c + part != r)
        def _():
            remote(gs.at[0, part], gbuf.at[r], g_s.at[0, part], g_r.at[r], rows=2 * c + part).wait_send()

    @pl.when(not_first)
    def _():
        edge(f_ref.at[0], fhalo, fh_s, fh_r, True).wait_send()
        edge(dsend.at[0], dhalo, dh_s, dh_r, True).wait_send()

    @pl.when(not_last)
    def _():
        edge(f_ref.at[0], fhalo, fh_s, fh_r, False).wait_send()
        edge(dsend.at[1], dhalo, dh_s, dh_r, False).wait_send()


def on_device(feature, out_grad, bank, select, latent, affine_w, affine_b):
    x = jnp.transpose(out_grad[0], (1, 0, 2))
    f = jnp.transpose(feature[0], (1, 0, 2))
    height, ch, width = x.shape
    nb, taps, _, ib = bank.shape
    z = latent.shape[1]
    lanes = 4 * ch
    vmem = pl.BlockSpec(memory_space=pltpu.VMEM)
    dma = pltpu.SemaphoreType.DMA
    d, bg, awg, abg = pl.pallas_call(
        kernel,
        out_shape=(
            jax.ShapeDtypeStruct((height, ch, width), BF16),
            jax.ShapeDtypeStruct((nb, taps, ib, ch), F32),
            jax.ShapeDtypeStruct((ib, z), F32),
            jax.ShapeDtypeStruct((1, ib), F32),
        ),
        in_specs=[vmem] * 7,
        out_specs=(vmem,) * 4,
        scratch_shapes=[
            pltpu.VMEM((height + 5, CHANS, ch, width), BF16),
            pltpu.VMEM((height + 2, 3 * ch, width), BF16),
            pltpu.VMEM((2, ch, width), BF16),
            pltpu.VMEM((4, 3 * ib // 2, 128), BF16),
            pltpu.VMEM((ROWS, 3 * ib // 2, 128), BF16),
            pltpu.VMEM((CHANS, 2, 3 * ib // 2, 128), BF16),
            pltpu.VMEM((CHANS, 2, 3 * ib, lanes), BF16),
            pltpu.VMEM((CHANS, 2, 3 * ib, lanes), BF16),
            pltpu.VMEM((ROWS, 3 * ib, lanes), BF16),
            pltpu.VMEM((SAMPLES, 8, z), F32),
            pltpu.VMEM((SAMPLES, 8, 128), F32),
            pltpu.VMEM((ROWS, 1, 128), F32),
            pltpu.VMEM((ROWS, CHANS, 1, 128), F32),
            pltpu.VMEM((CHANS, 1, 128), F32),
            pltpu.VMEM((SAMPLES, 3, ib, lanes), BF16),
            pltpu.VMEM((SAMPLES, CHANS, 1, 128), F32),
            pltpu.VMEM((3, ib, lanes), F32),
            pltpu.VMEM((3, ib, lanes), F32),
            pltpu.VMEM((height + 2, ch, width), F32),
            pltpu.VMEM((2, ch, width), BF16),
            pltpu.VMEM((2, ch, width), BF16),
            dma((2, 4)), dma((2, 4)),
            dma((2,)), dma((2,)),
            dma((2,)), dma((2,)),
            dma,
            dma((2, SAMPLES)), dma((2, SAMPLES)),
            dma((ROWS,)), dma((ROWS,)),
            dma((ROWS,)), dma((ROWS,)), dma((CHANS,)), dma((CHANS,)), dma((4,)), dma((4,)),
            dma((CHANS, 2)), dma((ROWS,)),
            dma((ROWS, CHANS)), dma((ROWS, CHANS)),
            dma((SAMPLES,)), dma((SAMPLES,)),
            dma((SAMPLES, CHANS)), dma((SAMPLES, CHANS)),
        ],
        compiler_params=pltpu.CompilerParams(
            collective_id=0, has_side_effects=True, vmem_limit_bytes=48 * 1024 * 1024
        ),
    )(
        x, f, jnp.transpose(bank, (0, 1, 3, 2)), select, latent,
        jnp.transpose(affine_w), affine_b[None],
    )
    return (
        jnp.transpose(d, (1, 0, 2))[None],
        jnp.transpose(bg, (0, 1, 3, 2)),
        jnp.transpose(awg),
        abg[0],
    )


def solution(mesh):
    return jax.shard_map(
        on_device,
        mesh=mesh,
        in_specs=(
            P("samples", "chan", "rows", None),
            P("samples", "chan", "rows", None),
            P(None, None, "chan", "rows"),
            P("samples", None),
            P("samples", None),
            P(None, "rows"),
            P("rows"),
        ),
        out_specs=(
            P("samples", "chan", "rows", None),
            P(None, None, "chan", "rows"),
            P(None, "rows"),
            P("rows"),
        ),
        check_vma=False,
    )
```

```python
import jax
import jax.numpy as jnp
from jax import lax
from jax.experimental import pallas as pl
from jax.experimental.pallas import tpu as pltpu
from jax.sharding import PartitionSpec as P

EPS = 1e-08
MESH = pl.DeviceIdType.MESH
ROWS, SAMPLES, CHANS = 8, 4, 4
F32, BF16 = jnp.float32, jnp.bfloat16


def lane_iota(shape):
    return lax.broadcasted_iota(jnp.int32, shape, len(shape) - 1)


def moved_right(x):
    return jnp.where(lane_iota(x.shape) == 0, 0.0, pltpu.roll(x, 1, axis=1))


def moved_left(x):
    width = x.shape[1]
    return jnp.where(lane_iota(x.shape) == width - 1, 0.0, pltpu.roll(x, width - 1, axis=1))


def over_taps(x):
    flat = jnp.sum(x, axis=(0, 1))[None, :]
    half = flat[:, :128] + flat[:, 128:]
    return half + pltpu.roll(half, 64, axis=1)


def kernel(
    x_hbm, f_hbm, bank_hbm, sel_hbm, lat_hbm, aw_hbm, ab_hbm,
    d_ref, kg, st, latb, selb,
    xraw, fraw, f_ref, bank_ref, sel_ref, lat_ref, aw_ref, ab_ref, xbuf, fs, fhalo, mown, ms, my, mm, gs, gbuf, en, slv, slo, ker_ref, plain_ref, dacc, dsend, dhalo,
    ag_s, ag_r, fh_s, fh_r, dh_s, dh_r, load_s, in_s, in_r, en_s, en_r, ms_s, ms_r, my_s, my_r, mm_s, mm_r,
    g_s, g_r, sl_s, sl_r, kg_s, kg_r, st_s, st_r,
):
    r, b, c = lax.axis_index("rows"), lax.axis_index("samples"), lax.axis_index("chan")
    ch, height, width = xraw.shape
    nb, ib = bank_ref.shape[0], bank_ref.shape[2]
    left, right, opp = lax.rem(c + 3, CHANS), lax.rem(c + 1, CHANS), lax.rem(c + 2, CHANS)
    tall = 6 * ib

    def remote(src, dst, send, recv, **where):
        return pltpu.make_async_remote_copy(
            src_ref=src, dst_ref=dst, send_sem=send, recv_sem=recv, device_id=where, device_id_type=MESH
        )

    sent = []

    def go(copy):
        copy.start()
        sent.append(copy)

    barrier = pltpu.get_barrier_semaphore()
    greeted = 0
    for dr in range(ROWS):
        for dc in range(CHANS):
            if dr or dc:
                pl.semaphore_signal(
                    barrier, inc=1,
                    device_id={"rows": lax.rem(r + dr, ROWS), "chan": lax.rem(c + dc, CHANS)},
                    device_id_type=MESH,
                )
                greeted += 1
    for db in range(1, SAMPLES):
        for dc in range(CHANS):
            pl.semaphore_signal(
                barrier, inc=1,
                device_id={"samples": lax.rem(b + db, SAMPLES), "chan": lax.rem(c + dc, CHANS)},
                device_id_type=MESH,
            )
            greeted += 1

    pairs = (
        (lat_hbm, lat_ref), (sel_hbm, sel_ref), (ab_hbm, ab_ref), (aw_hbm, aw_ref), (bank_hbm, bank_ref),
        (x_hbm, xraw), (f_hbm, fraw),
    )
    loads = [pltpu.make_async_copy(src, dst, load_s.at[i]) for i, (src, dst) in enumerate(pairs)]
    for load in loads:
        load.start()
    gs[...] = jnp.zeros_like(gs)
    ker_ref[...] = jnp.zeros_like(ker_ref)
    for row in (0, 1, height + 2, height + 3, height + 4):
        xbuf[row] = jnp.zeros(xbuf.shape[1:], BF16)
    for load in loads[:5]:
        load.wait()

    lat = lat_ref[...]
    latb[pl.ds(b, 1)] = jnp.broadcast_to(lat[None], (1, 8, lat.shape[1]))
    sel = sel_ref[...].astype(F32)
    selrow = jnp.zeros((8, 128), F32)
    for k in range(nb):
        selrow = jnp.where(lane_iota((8, 128)) == k, sel[:, k : k + 1], selrow)
    selb[pl.ds(b, 1)] = selrow[None]
    square = lax.broadcasted_iota(jnp.int32, (ib, ib), 0) == lane_iota((ib, ib))
    bias = jnp.sum(jnp.where(square, ab_ref[...], 0.0), axis=1, keepdims=True)
    style = jnp.sum(aw_ref[...] * lat, axis=1, keepdims=True) + bias
    for kh in range(3):
        for kw in range(3):
            tap = sum(sel[:, k : k + 1] * bank_ref[k, 3 * kh + kw] for k in range(nb))
            ker_ref[kw, :, (2 - kh) * ch : (3 - kh) * ch] = tap
    ker = ker_ref[...]
    plain_ref[...] = ker * style[None]
    plain = plain_ref[...]
    en[pl.ds(r, 1)] = over_taps(plain * plain)[None]

    loads[5].wait()
    group = 16

    def lay_x(g, carry):
        some = pl.ds(pl.multiple_of(g * group, group), group)
        xbuf[pl.ds(2, height), pl.ds(c, 1), some] = (
            jnp.transpose(xraw[some].astype(F32), (1, 0, 2)).astype(BF16)[:, None]
        )
        return carry

    lax.fori_loop(0, ch // group, lay_x, 0)

    pl.semaphore_wait(barrier, greeted)

    for d in range(1, ROWS):
        go(remote(en.at[r], en.at[r], en_s.at[d], en_r.at[d], rows=lax.rem(r + d, ROWS)))
    half = height // 2

    def rows_of(shard, first, count):
        return xbuf.at[pl.ds(first + 2, count), shard]

    to_right, to_left = {"chan": right}, {"chan": left}
    go(remote(rows_of(c, 0, half), rows_of(c, 0, half), ag_s.at[0, 0], ag_r.at[0, 0], **to_right))
    go(remote(rows_of(c, half, half), rows_of(c, half, half), ag_s.at[1, 0], ag_r.at[1, 0], **to_left))

    go(remote(rows_of(c, half, half), rows_of(c, half, half), ag_s.at[0, 1], ag_r.at[0, 1], **to_right))
    go(remote(rows_of(c, 0, half), rows_of(c, 0, half), ag_s.at[1, 1], ag_r.at[1, 1], **to_left))
    for d in range(1, SAMPLES):
        there = lax.rem(b + d, SAMPLES)
        go(remote(latb.at[b], latb.at[b], in_s.at[0, d], in_r.at[0, d], samples=there))
        go(remote(selb.at[b], selb.at[b], in_s.at[1, d], in_r.at[1, d], samples=there))

    loads[6].wait()

    def lay_f(g, carry):
        some = pl.ds(pl.multiple_of(g * group, group), group)
        f_ref[:, some] = jnp.transpose(fraw[some].astype(F32), (1, 0, 2)).astype(BF16)
        return carry

    lax.fori_loop(0, ch // group, lay_f, 0)

    def edge(src, dst, send, recv, up):
        there = jnp.maximum(r - 1, 0) if up else jnp.minimum(r + 1, ROWS - 1)
        i = 0 if up else 1
        return remote(src, dst.at[1 - i], send.at[i], recv.at[1 - i], rows=there)

    not_first, not_last = r > 0, r < ROWS - 1

    @pl.when(not_first)
    def _():
        edge(f_ref.at[0], fhalo, fh_s, fh_r, True).start()

    @pl.when(not_last)
    def _():
        edge(f_ref.at[height - 1], fhalo, fh_s, fh_r, False).start()

    def shift_into(at, f):
        wide = f.astype(F32)
        for kw, moved in enumerate((moved_right(wide).astype(BF16), f, moved_left(wide).astype(BF16))):
            for part in range(2):
                first = (3 * part + kw) * ib
                fs[at, first : first + ib] = moved[part * ib : (part + 1) * ib]

    def shifted(h, carry):
        shift_into(h + 1, f_ref[h])
        return carry

    lax.fori_loop(0, height, shifted, 0)

    for d in range(1, ROWS):
        src = lax.rem(r + ROWS - d, ROWS)
        remote(en.at[src], en.at[src], en_s.at[d], en_r.at[d], rows=src).wait_recv()
    scale = lax.rsqrt(jnp.sum(en[...], axis=0) + EPS)
    scale = jnp.concatenate([scale, scale], axis=1)[None]

    side, level = r // 4, lax.rem(r, 4)
    tile, lanes = 3 * ib // 2, 128
    modulated = (plain * scale).astype(BF16).reshape(3 * ib, 4 * ch)
    for quarter in range(4):
        top, start = (quarter // 2) * tile, (quarter % 2) * lanes
        mown[quarter] = modulated[top : top + tile, start : start + lanes]
    ms[pl.ds(r, 1)] = mown[pl.ds(level, 1)]
    for d in range(1, ROWS):
        there = lax.rem(r + d, ROWS)
        go(remote(mown.at[lax.rem(there, 4)], ms.at[r], ms_s.at[d], ms_r.at[d], rows=there))

    @pl.when(not_first)
    def _():
        edge(f_ref.at[0], fhalo, fh_s, fh_r, False).wait_recv()
        shift_into(0, fhalo[0])

    @pl.when(r == 0)
    def _():
        fs[0] = jnp.zeros(fs.shape[1:], BF16)

    @pl.when(not_last)
    def _():
        edge(f_ref.at[0], fhalo, fh_s, fh_r, True).wait_recv()
        shift_into(height + 1, fhalo[1])

    @pl.when(r == ROWS - 1)
    def _():
        fs[height + 1] = jnp.zeros(fs.shape[1:], BF16)

    def grad_rows(acc, shard, first, count):
        def step(q, acc):
            around = xbuf[pl.ds(q, 3), shard].reshape(3 * ch, width)
            return acc + lax.dot_general(
                fs[q], around, (((1,), (1,)), ((), ())), preferred_element_type=F32
            )

        return lax.fori_loop(first, first + count, step, acc)

    no_grad = jnp.zeros((tall, 3 * ch), F32)

    def send_grad(i, shard, acc):
        gs[i, :, :, : 3 * ch] = acc.reshape(2, 3 * ib, 3 * ch).astype(BF16)
        for part in range(2):
            src = gs.at[i, part]
            target = 2 * c + part
            if i == 0:
                @pl.when(target == r)
                def _():
                    pltpu.make_async_copy(src, gbuf.at[r], g_r.at[r]).start()

                @pl.when(target != r)
                def _():
                    remote(src, gbuf.at[r], g_s.at[i, part], g_r.at[r], rows=target).start()
            else:
                go(remote(src, gbuf.at[r], g_s.at[i, part], g_r.at[r], rows=target, chan=shard))

    send_grad(0, c, grad_rows(no_grad, c, 0, height + 2))

    most = half - 1

    def from_left(k, first, count, shard):
        return remote(rows_of(shard, first, count), rows_of(shard, first, count), ag_s.at[0, k], ag_r.at[0, k], **to_right)

    def from_right(k, first, count, shard):
        return remote(rows_of(shard, first, count), rows_of(shard, first, count), ag_s.at[1, k], ag_r.at[1, k], **to_left)

    for d in range(1, ROWS):
        src = lax.rem(r + ROWS - d, ROWS)
        remote(mown.at[0], ms.at[src], ms_s.at[d], ms_r.at[d], rows=src).wait_recv()
    my[pl.ds(c, 1)] = ms[pl.ds(2 * c, 2)][None]
    for d in (1, 3, 2):
        there = lax.rem(c + d, CHANS)
        go(remote(ms.at[pl.ds(2 * there, 2)], my.at[c], my_s.at[d], my_r.at[d], chan=there))

    from_left(0, 0, half, left).wait_recv()
    go(from_left(2, 0, most, left))
    go(from_left(3, most, 1, left))
    from_right(0, half, half, right).wait_recv()
    go(from_right(2, half + 1, most, right))
    go(from_right(3, half, 1, right))

    from_left(1, half, half, left).wait_recv()

    for d in range(1, CHANS):
        src = lax.rem(c + CHANS - d, CHANS)
        remote(ms.at[pl.ds(0, 2)], my.at[src], my_s.at[d], my_r.at[d], chan=src).wait_recv()

    def quarter_of(level):
        top = pl.multiple_of((level // 2) * tile, tile)
        start = pl.multiple_of(lax.rem(level, 2) * lanes, lanes)
        return mm.at[:, :, pl.ds(top, tile), pl.ds(start, lanes)]

    def peer(d):
        return 4 * side + lax.rem(level + d, 4)

    mine = pltpu.make_async_copy(my, quarter_of(level), mm_r.at[0])
    mine.start()
    for d in (1, 3, 2):
        go(remote(my, quarter_of(level), mm_s.at[d], mm_r.at[d], rows=peer(d)))

    send_grad(1, left, grad_rows(no_grad, left, 0, height + 2))

    from_right(1, 0, half, right).wait_recv()

    send_grad(2, right, grad_rows(no_grad, right, 0, height + 2))

    def send_slope(i, k, shard):
        parts = gs[i].astype(F32) * mm[shard].astype(F32)
        slo[i] = over_taps(parts)
        for d in range(ROWS):
            if k == 0 and d == 0:
                slv[pl.ds(r, 1), pl.ds(c, 1)] = slo[0][None, None]
            else:
                go(remote(
                    slo.at[i], slv.at[r, c], sl_s.at[d, k], sl_r.at[d, k], rows=lax.rem(r + d, ROWS), chan=shard
                ))

    from_left(2, 0, most, opp).wait_recv()
    from_right(2, half + 1, most, opp).wait_recv()

    acc = grad_rows(no_grad, opp, 0, most)
    acc = grad_rows(acc, opp, height + 2 - most, most)

    for d in range(1, 4):
        src = peer(4 - d)
        remote(my, quarter_of(lax.rem(src, 4)), mm_s.at[d], mm_r.at[d], rows=src).wait_recv()
    mine.wait()
    send_slope(0, 0, c)
    send_slope(1, 3, left)
    send_slope(2, 1, right)

    from_left(3, most, 1, opp).wait_recv()
    from_right(3, half, 1, opp).wait_recv()

    send_grad(3, opp, grad_rows(acc, opp, most, height + 2 - 2 * most))
    send_slope(3, 2, opp)

    def rows_out(q, carry):
        total = jnp.zeros((tall, width), F32)
        for shard in range(CHANS):
            around = xbuf[pl.ds(q, 4), shard].reshape(4 * ch, width)
            total = total + jnp.dot(mm[shard].reshape(tall, 4 * ch), around, preferred_element_type=F32)
        for part in range(2):
            t = total[3 * part * ib : 3 * (part + 1) * ib]
            dacc[q, part * ib : (part + 1) * ib] = t[ib : 2 * ib] + moved_left(t[:ib]) + moved_right(t[2 * ib :])
        return carry

    lax.fori_loop(0, height + 2, rows_out, 0)
    dsend[0] = dacc[0].astype(BF16)
    dsend[1] = dacc[height + 1].astype(BF16)

    @pl.when(not_first)
    def _():
        edge(dsend.at[0], dhalo, dh_s, dh_r, True).start()

    @pl.when(not_last)
    def _():
        edge(dsend.at[1], dhalo, dh_s, dh_r, False).start()

    for src in range(ROWS):
        remote(gs.at[0, 0], gbuf.at[src], g_s.at[0, 0], g_r.at[src], rows=lax.rem(r + 1, ROWS)).wait_recv()

    for d in range(ROWS):
        for k in range(CHANS):
            if d or k:
                rs, cs = lax.rem(r + ROWS - d, ROWS), lax.rem(c + CHANS - k, CHANS)
                remote(slo.at[0], slv.at[rs, cs], sl_s.at[d, k], sl_r.at[d, k], rows=rs, chan=cs).wait_recv()

    grad = gbuf[0].astype(F32)
    for src in range(1, ROWS):
        grad = grad + gbuf[src].astype(F32)
    grad = grad.reshape(3, ib, 4 * ch)
    slope = jnp.sum(slv[...], axis=(0, 1))
    slope = jnp.concatenate([slope, slope], axis=1)[None]
    plain_grad = grad * scale - plain * (slope * (scale * scale))
    by_input = jnp.sum(plain_grad * ker, axis=0)
    by_input = jnp.concatenate([by_input, jnp.zeros((128 - ib, by_input.shape[1]), F32)], axis=0)
    style_part = lax.dot_general(
        jnp.ones((8, by_input.shape[1]), F32), by_input, (((1,), (1,)), ((), ())),
        preferred_element_type=F32, precision=lax.Precision.HIGHEST,
    )
    st[pl.ds(b, 1), pl.ds(c, 1)] = style_part[0:1][None, None]
    for db in range(SAMPLES):
        for dc in range(CHANS):
            if db or dc:
                go(remote(
                    st.at[b, c], st.at[b, c], st_s.at[db, dc], st_r.at[db, dc],
                    samples=lax.rem(b + db, SAMPLES), chan=lax.rem(c + dc, CHANS),
                ))
    kg[pl.ds(b, 1)] = (plain_grad * style[None])[None].astype(BF16)
    for d in range(1, SAMPLES):
        go(remote(kg.at[b], kg.at[b], kg_s.at[d], kg_r.at[d], samples=lax.rem(b + d, SAMPLES)))

    @pl.when(not_first)
    def _():
        edge(dsend.at[0], dhalo, dh_s, dh_r, False).wait_recv()
        dacc[1] = dacc[1] + dhalo[0].astype(F32)

    @pl.when(not_last)
    def _():
        edge(dsend.at[0], dhalo, dh_s, dh_r, True).wait_recv()
        dacc[height] = dacc[height] + dhalo[1].astype(F32)

    def lay_d(g, carry):
        some = pl.ds(pl.multiple_of(g * group, group), group)
        d_ref[some] = jnp.transpose(dacc[pl.ds(1, height), some], (1, 0, 2)).astype(BF16)
        return carry

    lax.fori_loop(0, ch // group, lay_d, 0)

    for d in range(1, SAMPLES):
        src = lax.rem(b + SAMPLES - d, SAMPLES)
        remote(latb.at[src], latb.at[src], in_s.at[0, d], in_r.at[0, d], samples=src).wait_recv()
        remote(selb.at[src], selb.at[src], in_s.at[1, d], in_r.at[1, d], samples=src).wait_recv()
    for db in range(SAMPLES):
        for dc in range(CHANS):
            if db or dc:
                bs, cs = lax.rem(b + SAMPLES - db, SAMPLES), lax.rem(c + CHANS - dc, CHANS)
                remote(
                    st.at[bs, cs], st.at[bs, cs], st_s.at[db, dc], st_r.at[db, dc], samples=bs, chan=cs
                ).wait_recv()

    for d in range(1, SAMPLES):
        src = lax.rem(b + SAMPLES - d, SAMPLES)
        remote(kg.at[src], kg.at[src], kg_s.at[d], kg_r.at[d], samples=src).wait_recv()

    for copy in sent:
        copy.wait_send()
    for part in range(2):
        @pl.when(2 * c + part != r)
        def _():
            remote(gs.at[0, part], gbuf.at[r], g_s.at[0, part], g_r.at[r], rows=2 * c + part).wait_send()

    @pl.when(not_first)
    def _():
        edge(f_ref.at[0], fhalo, fh_s, fh_r, True).wait_send()
        edge(dsend.at[0], dhalo, dh_s, dh_r, True).wait_send()

    @pl.when(not_last)
    def _():
        edge(f_ref.at[0], fhalo, fh_s, fh_r, False).wait_send()
        edge(dsend.at[1], dhalo, dh_s, dh_r, False).wait_send()


def write_out(d_ref, kg, st, latb, selb, d_hbm, bg_hbm, awg_hbm, abg_hbm, bg_ref, awg_ref, abg_ref, sems):
    nb, _, ib, ch = bg_ref.shape
    copies = [pltpu.make_async_copy(d_ref, d_hbm, sems.at[0])]
    copies[0].start()
    for k in range(nb):
        for kw in range(3):
            total = sum(selb[s][0:1, k : k + 1] * kg[s, kw].astype(F32) for s in range(SAMPLES))
            for kh in range(3):
                bg_ref[k, 3 * kh + kw] = total[:, (2 - kh) * ch : (3 - kh) * ch]
        copies.append(pltpu.make_async_copy(bg_ref.at[k], bg_hbm.at[k], sems.at[3 + k]))
        copies[-1].start()
    diagonal = lax.broadcasted_iota(jnp.int32, (ib, 128), 0) == lane_iota((ib, 128))
    style_sum = jnp.zeros((1, 128), F32)
    affine = jnp.zeros(awg_ref.shape, F32)
    for s in range(SAMPLES):
        row = st[s, 0] + st[s, 1] + st[s, 2] + st[s, 3]
        style_sum = style_sum + row
        column = jnp.sum(jnp.where(diagonal, row, 0.0), axis=1, keepdims=True)
        affine = affine + column * latb[s][0:1]
    awg_ref[...] = affine
    abg_ref[...] = style_sum[:, :ib]
    copies.append(pltpu.make_async_copy(awg_ref, awg_hbm, sems.at[1]))
    copies[-1].start()
    copies.append(pltpu.make_async_copy(abg_ref, abg_hbm, sems.at[2]))
    copies[-1].start()
    for copy in copies:
        copy.wait()


def on_device(feature, out_grad, bank, select, latent, affine_w, affine_b):
    _, ch, height, width = out_grad.shape
    nb, taps, _, ib = bank.shape
    z = latent.shape[1]
    lanes = 4 * ch
    vmem, hbm = pl.BlockSpec(memory_space=pltpu.VMEM), pl.BlockSpec(memory_space=pltpu.HBM)
    dma = pltpu.SemaphoreType.DMA
    parts = pl.pallas_call(
        kernel,
        out_shape=(
            jax.ShapeDtypeStruct((ch, height, width), BF16),
            jax.ShapeDtypeStruct((SAMPLES, 3, ib, lanes), BF16),
            jax.ShapeDtypeStruct((SAMPLES, CHANS, 1, 128), F32),
            jax.ShapeDtypeStruct((SAMPLES, 8, z), F32),
            jax.ShapeDtypeStruct((SAMPLES, 8, 128), F32),
        ),
        in_specs=[hbm] * 7,
        out_specs=(vmem,) * 5,
        scratch_shapes=[
            pltpu.VMEM((ch, height, width), BF16),
            pltpu.VMEM((ch, height, width), BF16),
            pltpu.VMEM((height, ch, width), BF16),
            pltpu.VMEM((nb, taps, ib, ch), F32),
            pltpu.VMEM((1, nb), jnp.int32),
            pltpu.VMEM((1, z), F32),
            pltpu.VMEM((ib, z), F32),
            pltpu.VMEM((1, ib), F32),
            pltpu.VMEM((height + 5, CHANS, ch, width), BF16),
            pltpu.VMEM((height + 2, 3 * ch, width), BF16),
            pltpu.VMEM((2, ch, width), BF16),
            pltpu.VMEM((4, 3 * ib // 2, 128), BF16),
            pltpu.VMEM((ROWS, 3 * ib // 2, 128), BF16),
            pltpu.VMEM((CHANS, 2, 3 * ib // 2, 128), BF16),
            pltpu.VMEM((CHANS, 2, 3 * ib, lanes), BF16),
            pltpu.VMEM((CHANS, 2, 3 * ib, lanes), BF16),
            pltpu.VMEM((ROWS, 3 * ib, lanes), BF16),
            pltpu.VMEM((ROWS, 1, 128), F32),
            pltpu.VMEM((ROWS, CHANS, 1, 128), F32),
            pltpu.VMEM((CHANS, 1, 128), F32),
            pltpu.VMEM((3, ib, lanes), F32),
            pltpu.VMEM((3, ib, lanes), F32),
            pltpu.VMEM((height + 2, ch, width), F32),
            pltpu.VMEM((2, ch, width), BF16),
            pltpu.VMEM((2, ch, width), BF16),
            dma((2, 4)), dma((2, 4)),
            dma((2,)), dma((2,)),
            dma((2,)), dma((2,)),
            dma((7,)),
            dma((2, SAMPLES)), dma((2, SAMPLES)),
            dma((ROWS,)), dma((ROWS,)),
            dma((ROWS,)), dma((ROWS,)), dma((CHANS,)), dma((CHANS,)), dma((4,)), dma((4,)),
            dma((CHANS, 2)), dma((ROWS,)),
            dma((ROWS, CHANS)), dma((ROWS, CHANS)),
            dma((SAMPLES,)), dma((SAMPLES,)),
            dma((SAMPLES, CHANS)), dma((SAMPLES, CHANS)),
        ],
        compiler_params=pltpu.CompilerParams(
            collective_id=0, has_side_effects=True, vmem_limit_bytes=48 * 1024 * 1024
        ),
    )(
        *(pltpu.with_memory_space_constraint(a, pltpu.HBM) for a in (
            out_grad[0], feature[0], jnp.transpose(bank, (0, 1, 3, 2)), select, latent,
            jnp.transpose(affine_w), affine_b[None],
        ))
    )
    d, bg, awg, abg = pl.pallas_call(
        write_out,
        out_shape=(
            jax.ShapeDtypeStruct((ch, height, width), BF16),
            jax.ShapeDtypeStruct((nb, taps, ib, ch), F32),
            jax.ShapeDtypeStruct((ib, z), F32),
            jax.ShapeDtypeStruct((1, ib), F32),
        ),
        in_specs=[vmem] * 5,
        out_specs=(hbm,) * 4,
        scratch_shapes=[
            pltpu.VMEM((nb, taps, ib, ch), F32),
            pltpu.VMEM((ib, z), F32),
            pltpu.VMEM((1, ib), F32),
            dma((3 + nb,)),
        ],
        compiler_params=pltpu.CompilerParams(vmem_limit_bytes=16 * 1024 * 1024),
    )(*parts)
    return d[None], jnp.transpose(bg, (0, 1, 3, 2)), jnp.transpose(awg), abg[0]


def solution(mesh):
    return jax.shard_map(
        on_device,
        mesh=mesh,
        in_specs=(
            P("samples", "chan", "rows", None),
            P("samples", "chan", "rows", None),
            P(None, None, "chan", "rows"),
            P("samples", None),
            P("samples", None),
            P(None, "rows"),
            P("rows"),
        ),
        out_specs=(
            P("samples", "chan", "rows", None),
            P(None, None, "chan", "rows"),
            P(None, "rows"),
            P("rows"),
        ),
        check_vma=False,
    )
```

```python
import jax
import jax.numpy as jnp
from jax import lax
from jax.experimental import pallas as pl
from jax.experimental.pallas import tpu as pltpu
from jax.sharding import PartitionSpec as P

EPS = 1e-08
MESH = pl.DeviceIdType.MESH
ROWS, SAMPLES, CHANS = 8, 4, 4
F32, BF16 = jnp.float32, jnp.bfloat16


def lane_iota(shape):
    return lax.broadcasted_iota(jnp.int32, shape, len(shape) - 1)


def moved_right(x):
    return jnp.where(lane_iota(x.shape) == 0, 0.0, pltpu.roll(x, 1, axis=1))


def moved_left(x):
    width = x.shape[1]
    return jnp.where(lane_iota(x.shape) == width - 1, 0.0, pltpu.roll(x, width - 1, axis=1))


def over_taps(x):
    flat = jnp.sum(x, axis=(0, 1))[None, :]
    half = flat[:, :128] + flat[:, 128:]
    return half + pltpu.roll(half, 64, axis=1)


def packed(x):
    half = x.shape[0] // 2
    return jnp.concatenate(
        [x[:, :128], jnp.concatenate([x[:half, 128:192], x[half:, 128:192]], axis=1)], axis=0
    )


def unpacked(x):
    third = x.shape[0] // 3
    tail = x[2 * third :]
    return jnp.concatenate(
        [x[: 2 * third], jnp.concatenate([tail, pltpu.roll(tail, 64, axis=1)], axis=0)], axis=1
    )


def kernel(
    x_hbm, f_hbm, bank_hbm, sel_hbm, lat_hbm, aw_hbm, ab_hbm,
    d_ref, kg, st, latb, selb,
    xraw, fraw, f_ref, bank_ref, sel_ref, lat_ref, aw_ref, ab_ref, xbuf, fs, fhalo, mown, ms, my, mm, mall, gs, gp, gbuf, en, sc, slv, slo, ker_ref, plain_ref, dacc, dsend, dhalo,
    ag_s, ag_r, fh_s, fh_r, dh_s, dh_r, load_s, in_s, in_r, en_s, en_r, sc_s, sc_r, ms_s, ms_r, my_s, my_r, mm_s, mm_r,
    g_s, g_r, sl_s, sl_r, kg_s, kg_r, st_s, st_r,
):
    r, b, c = lax.axis_index("rows"), lax.axis_index("samples"), lax.axis_index("chan")
    ch, height, width = xraw.shape
    nb, ib = bank_ref.shape[0], bank_ref.shape[2]
    left, right, opp = lax.rem(c + 3, CHANS), lax.rem(c + 1, CHANS), lax.rem(c + 2, CHANS)
    tall = 6 * ib

    def remote(src, dst, send, recv, **where):
        return pltpu.make_async_remote_copy(
            src_ref=src, dst_ref=dst, send_sem=send, recv_sem=recv, device_id=where, device_id_type=MESH
        )

    sent = []

    def go(copy):
        copy.start()
        sent.append(copy)

    group = 16
    pairs = [
        (lat_hbm, lat_ref), (sel_hbm, sel_ref), (ab_hbm, ab_ref), (aw_hbm, aw_ref), (bank_hbm, bank_ref),
        *((x_hbm.at[pl.ds(g, group)], xraw.at[pl.ds(g, group)]) for g in range(0, ch, group)),
        (f_hbm, fraw),
    ]
    loads = [pltpu.make_async_copy(src, dst, load_s.at[i]) for i, (src, dst) in enumerate(pairs)]
    for load in loads:
        load.start()

    barrier = pltpu.get_barrier_semaphore()
    greeted = 0
    for dr in range(ROWS):
        for dc in range(CHANS):
            if dr or dc:
                pl.semaphore_signal(
                    barrier, inc=1,
                    device_id={"rows": lax.rem(r + dr, ROWS), "chan": lax.rem(c + dc, CHANS)},
                    device_id_type=MESH,
                )
                greeted += 1
    for db in range(1, SAMPLES):
        for dc in range(CHANS):
            pl.semaphore_signal(
                barrier, inc=1,
                device_id={"samples": lax.rem(b + db, SAMPLES), "chan": lax.rem(c + dc, CHANS)},
                device_id_type=MESH,
            )
            greeted += 1

    gs[...] = jnp.zeros_like(gs)
    ker_ref[...] = jnp.zeros_like(ker_ref)
    for row in (0, 1, height + 2, height + 3, height + 4):
        xbuf[row] = jnp.zeros(xbuf.shape[1:], BF16)
    for load in loads[:5]:
        load.wait()

    lat = lat_ref[...]
    latb[pl.ds(b, 1)] = jnp.broadcast_to(lat[None], (1, 8, lat.shape[1]))
    sel = sel_ref[...].astype(F32)
    selrow = jnp.zeros((8, 128), F32)
    for k in range(nb):
        selrow = jnp.where(lane_iota((8, 128)) == k, sel[:, k : k + 1], selrow)
    selb[pl.ds(b, 1)] = selrow[None]
    square = lax.broadcasted_iota(jnp.int32, (ib, ib), 0) == lane_iota((ib, ib))
    bias = jnp.sum(jnp.where(square, ab_ref[...], 0.0), axis=1, keepdims=True)
    style = jnp.sum(aw_ref[...] * lat, axis=1, keepdims=True) + bias
    for kh in range(3):
        for kw in range(3):
            tap = sum(sel[:, k : k + 1] * bank_ref[k, 3 * kh + kw] for k in range(nb))
            ker_ref[kw, :, (2 - kh) * ch : (3 - kh) * ch] = tap
    ker = ker_ref[...]
    plain_ref[...] = ker * style[None]
    plain = plain_ref[...]
    en[pl.ds(r, 1)] = over_taps(plain * plain)[None]

    side, level = r // 4, lax.rem(r, 4)
    tile, lanes = 3 * ib // 2, 128
    styled = plain.astype(BF16).reshape(3 * ib, 4 * ch)
    for quarter in range(4):
        top, start = (quarter // 2) * tile, (quarter % 2) * lanes
        mown[quarter] = styled[top : top + tile, start : start + lanes]
    ms[pl.ds(r, 1)] = mown[pl.ds(level, 1)]

    for g in range(0, ch, group):
        loads[5 + g // group].wait()
        xbuf[2 : 2 + height, pl.ds(c, 1), g : g + group] = (
            jnp.transpose(xraw[g : g + group].astype(F32), (1, 0, 2)).astype(BF16)[:, None]
        )

    pl.semaphore_wait(barrier, greeted)

    for d in range(1, ROWS):
        there = lax.rem(r + d, ROWS)
        go(remote(mown.at[lax.rem(there, 4)], ms.at[r], ms_s.at[d], ms_r.at[d], rows=there))
    for d in range(1, ROWS):
        go(remote(en.at[r], en.at[r], en_s.at[d], en_r.at[d], rows=lax.rem(r + d, ROWS)))
    half = height // 2

    def rows_of(shard, first, count):
        return xbuf.at[pl.ds(first + 2, count), shard]

    to_right, to_left = {"chan": right}, {"chan": left}
    go(remote(rows_of(c, 0, half), rows_of(c, 0, half), ag_s.at[0, 0], ag_r.at[0, 0], **to_right))
    go(remote(rows_of(c, half, half), rows_of(c, half, half), ag_s.at[1, 0], ag_r.at[1, 0], **to_left))

    most = half - 1
    for d in range(1, SAMPLES):
        there = lax.rem(b + d, SAMPLES)
        go(remote(latb.at[b], latb.at[b], in_s.at[0, d], in_r.at[0, d], samples=there))
        go(remote(selb.at[b], selb.at[b], in_s.at[1, d], in_r.at[1, d], samples=there))

    loads[-1].wait()

    def lay_f(g, carry):
        some = pl.ds(pl.multiple_of(g * group, group), group)
        f_ref[:, some] = jnp.transpose(fraw[some].astype(F32), (1, 0, 2)).astype(BF16)
        return carry

    lax.fori_loop(0, ch // group, lay_f, 0)

    def edge(src, dst, send, recv, up):
        there = jnp.maximum(r - 1, 0) if up else jnp.minimum(r + 1, ROWS - 1)
        i = 0 if up else 1
        return remote(src, dst.at[1 - i], send.at[i], recv.at[1 - i], rows=there)

    not_first, not_last = r > 0, r < ROWS - 1

    @pl.when(not_first)
    def _():
        edge(f_ref.at[0], fhalo, fh_s, fh_r, True).start()

    @pl.when(not_last)
    def _():
        edge(f_ref.at[height - 1], fhalo, fh_s, fh_r, False).start()

    def shift_into(at, f):
        wide = f.astype(F32)
        for kw, moved in enumerate((moved_right(wide).astype(BF16), f, moved_left(wide).astype(BF16))):
            for part in range(2):
                first = (3 * part + kw) * ib
                fs[at, first : first + ib] = moved[part * ib : (part + 1) * ib]

    def shifted(h, carry):
        shift_into(h + 1, f_ref[h])
        return carry

    lax.fori_loop(0, height, shifted, 0)

    for d in range(1, ROWS):
        src = lax.rem(r + ROWS - d, ROWS)
        remote(mown.at[0], ms.at[src], ms_s.at[d], ms_r.at[d], rows=src).wait_recv()
    my[pl.ds(c, 1)] = ms[pl.ds(2 * c, 2)][None]
    for d in (1, 3, 2):
        there = lax.rem(c + d, CHANS)
        go(remote(ms.at[pl.ds(2 * there, 2)], my.at[c], my_s.at[d], my_r.at[d], chan=there))
    go(remote(rows_of(c, half, half), rows_of(c, half, half), ag_s.at[0, 1], ag_r.at[0, 1], **to_right))
    go(remote(rows_of(c, 0, half), rows_of(c, 0, half), ag_s.at[1, 1], ag_r.at[1, 1], **to_left))

    for d in range(1, ROWS):
        src = lax.rem(r + ROWS - d, ROWS)
        remote(en.at[src], en.at[src], en_s.at[d], en_r.at[d], rows=src).wait_recv()
    scale = lax.rsqrt(jnp.sum(en[...], axis=0) + EPS)
    sc[pl.ds(c, 1)] = scale[None]
    for d in range(1, CHANS):
        go(remote(sc.at[c], sc.at[c], sc_s.at[d], sc_r.at[d], chan=lax.rem(c + d, CHANS)))
    scale = jnp.concatenate([scale, scale], axis=1)[None]

    @pl.when(not_first)
    def _():
        edge(f_ref.at[0], fhalo, fh_s, fh_r, False).wait_recv()
        shift_into(0, fhalo[0])

    @pl.when(r == 0)
    def _():
        fs[0] = jnp.zeros(fs.shape[1:], BF16)

    @pl.when(not_last)
    def _():
        edge(f_ref.at[0], fhalo, fh_s, fh_r, True).wait_recv()
        shift_into(height + 1, fhalo[1])

    @pl.when(r == ROWS - 1)
    def _():
        fs[height + 1] = jnp.zeros(fs.shape[1:], BF16)

    def grad_step(acc, shard, q):
        around = xbuf[q : q + 3, pl.ds(shard, 1)].reshape(3 * ch, width)
        return acc + lax.dot_general(
            fs[q], around, (((1,), (1,)), ((), ())), preferred_element_type=F32
        )

    def grad_rows(acc, shard, steps):
        for q in steps:
            acc = grad_step(acc, shard, q)
        return acc

    no_grad = jnp.zeros((tall, 3 * ch), F32)

    def send_grad(i, shard, acc, slope_first=None):
        gs[i, :, :, : 3 * ch] = acc.reshape(2, 3 * ib, 3 * ch).astype(BF16)
        for part in range(2):
            gp[i, part] = packed(acc[part * 3 * ib : (part + 1) * 3 * ib]).astype(BF16)
        if slope_first:
            send_slope(i, *slope_first)
        for part in range(2):
            src = gp.at[i, part]
            target = 2 * c + part
            if i == 0:
                @pl.when(target == r)
                def _():
                    pltpu.make_async_copy(src, gbuf.at[r], g_r.at[r]).start()

                @pl.when(target != r)
                def _():
                    remote(src, gbuf.at[r], g_s.at[i, part], g_r.at[r], rows=target).start()
            else:
                go(remote(src, gbuf.at[r], g_s.at[i, part], g_r.at[r], rows=target, chan=shard))

    send_grad(0, c, grad_rows(no_grad, c, range(height + 2)))

    most = half - 1

    def from_left(k, first, count, shard):
        return remote(rows_of(shard, first, count), rows_of(shard, first, count), ag_s.at[0, k], ag_r.at[0, k], **to_right)

    def from_right(k, first, count, shard):
        return remote(rows_of(shard, first, count), rows_of(shard, first, count), ag_s.at[1, k], ag_r.at[1, k], **to_left)

    def from_left(k, first, count, shard):
        return remote(rows_of(shard, first, count), rows_of(shard, first, count), ag_s.at[0, k], ag_r.at[0, k], **to_right)

    def from_right(k, first, count, shard):
        return remote(rows_of(shard, first, count), rows_of(shard, first, count), ag_s.at[1, k], ag_r.at[1, k], **to_left)

    from_left(0, 0, half, left).wait_recv()
    go(from_left(2, 0, most, left))
    go(from_left(3, most, 1, left))
    from_right(0, half, half, right).wait_recv()
    go(from_right(2, half + 1, most, right))
    go(from_right(3, half, 1, right))

    def both_steps(acc_left, acc_right, steps):
        for q in steps:
            acc_left = grad_step(acc_left, left, q)
            acc_right = grad_step(acc_right, right, height + 1 - q)
        return acc_left, acc_right

    acc_left, acc_right = both_steps(no_grad, no_grad, range(half))

    for d in range(1, CHANS):
        src = lax.rem(c + CHANS - d, CHANS)
        remote(ms.at[pl.ds(0, 2)], my.at[src], my_s.at[d], my_r.at[d], chan=src).wait_recv()

    def quarter_of(level, shards=slice(None)):
        top = pl.multiple_of((level // 2) * tile, tile)
        start = pl.multiple_of(lax.rem(level, 2) * lanes, lanes)
        return mm.at[shards, :, pl.ds(top, tile), pl.ds(start, lanes)]

    def peer(d):
        return 4 * side + lax.rem(level + d, 4)

    mine = pltpu.make_async_copy(my, quarter_of(level), mm_r.at[0])
    mine.start()
    for d in (1, 3):
        go(remote(my, quarter_of(level), mm_s.at[d], mm_r.at[d], rows=peer(d)))

    from_left(1, half, half, left).wait_recv()
    from_right(1, 0, half, right).wait_recv()

    acc_left, acc_right = both_steps(acc_left, acc_right, range(half, height + 2))
    send_grad(1, left, acc_left)
    send_grad(2, right, acc_right)

    def passed(d, level):
        part = quarter_of(level, slice(0, 2) if d == 1 else slice(2, 4))
        return remote(part, part, mm_s.at[1 + d // 2 * 2 + 1], mm_r.at[1 + d // 2 * 2 + 1], rows=peer(d))

    for d in (1, 3):
        src = lax.rem(level + 4 - d, 4)
        remote(my, quarter_of(src), mm_s.at[d], mm_r.at[d], rows=peer(4 - d)).wait_recv()
        go(passed(d, src))

    from_left(2, 0, most, opp).wait_recv()
    from_right(2, half + 1, most, opp).wait_recv()

    early = list(range(most)) + list(range(height + 2 - most, height + 2))
    acc_opp = grad_rows(no_grad, opp, early)

    for d in (1, 3):
        passed(d, lax.rem(level + 2, 4)).wait_recv()
    mine.wait()

    def send_slope(i, k, shard):
        slo[i] = over_taps(gs[i].astype(F32) * mm[shard].astype(F32))
        for d in range(ROWS):
            if k == 0 and d == 0:
                slv[pl.ds(r, 1), pl.ds(c, 1)] = slo[0][None, None]
            else:
                go(remote(
                    slo.at[i], slv.at[r, c], sl_s.at[d, k], sl_r.at[d, k], rows=lax.rem(r + d, ROWS), chan=shard
                ))

    send_slope(0, 0, c)
    send_slope(1, 3, left)
    send_slope(2, 1, right)

    from_left(3, most, 1, opp).wait_recv()
    from_right(3, half, 1, opp).wait_recv()

    send_grad(3, opp, grad_rows(acc_opp, opp, range(most, height + 2 - most)), slope_first=(2, opp))

    for d in range(1, CHANS):
        src = lax.rem(c + CHANS - d, CHANS)
        remote(sc.at[src], sc.at[src], sc_s.at[d], sc_r.at[d], chan=src).wait_recv()
    for shard in range(CHANS):
        modulated = mm[shard].reshape(tall, 4 * ch).astype(F32)
        modulated = (modulated * jnp.concatenate([sc[shard], sc[shard]], axis=1)).astype(BF16)
        for kh in range(3):
            at = (kh * CHANS + shard) * ch
            mall[:, at : at + ch] = modulated[:, kh * ch : (kh + 1) * ch]

    def row_out(q):
        first, last = max(q, 2), min(q + 3, height + 2)
        deep = CHANS * ch
        total = jnp.dot(
            mall[:, (first - q) * deep : (last - q) * deep],
            xbuf[first:last].reshape((last - first) * deep, width),
            preferred_element_type=F32,
        )
        for part in range(2):
            t = total[3 * part * ib : 3 * (part + 1) * ib]
            dacc[q, part * ib : (part + 1) * ib] = t[ib : 2 * ib] + moved_left(t[:ib]) + moved_right(t[2 * ib :])

    row_out(0)
    row_out(height + 1)
    dsend[0] = dacc[0].astype(BF16)
    dsend[1] = dacc[height + 1].astype(BF16)

    @pl.when(not_first)
    def _():
        edge(dsend.at[0], dhalo, dh_s, dh_r, True).start()

    @pl.when(not_last)
    def _():
        edge(dsend.at[1], dhalo, dh_s, dh_r, False).start()

    for q in range(1, height + 1):
        row_out(q)

    for src in range(ROWS):
        remote(gp.at[0, 0], gbuf.at[src], g_s.at[0, 0], g_r.at[src], rows=lax.rem(r + 1, ROWS)).wait_recv()

    for d in range(ROWS):
        for k in range(CHANS):
            if d or k:
                rs, cs = lax.rem(r + ROWS - d, ROWS), lax.rem(c + CHANS - k, CHANS)
                remote(slo.at[0], slv.at[rs, cs], sl_s.at[d, k], sl_r.at[d, k], rows=rs, chan=cs).wait_recv()

    grad = gbuf[0].astype(F32)
    for src in range(1, ROWS):
        grad = grad + gbuf[src].astype(F32)
    grad = unpacked(grad).reshape(3, ib, 4 * ch)
    slope = jnp.sum(slv[...], axis=(0, 1))
    slope = jnp.concatenate([slope, slope], axis=1)[None]
    plain_grad = grad * scale - plain * (slope * (scale * scale * scale))
    by_input = jnp.sum(plain_grad * ker, axis=0)
    by_input = jnp.concatenate([by_input, jnp.zeros((128 - ib, by_input.shape[1]), F32)], axis=0)
    style_part = lax.dot_general(
        jnp.ones((8, by_input.shape[1]), F32), by_input, (((1,), (1,)), ((), ())),
        preferred_element_type=F32, precision=lax.Precision.HIGHEST,
    )
    st[pl.ds(b, 1), pl.ds(c, 1)] = style_part[0:1][None, None]
    for db in range(SAMPLES):
        for dc in range(CHANS):
            if db or dc:
                go(remote(
                    st.at[b, c], st.at[b, c], st_s.at[db, dc], st_r.at[db, dc],
                    samples=lax.rem(b + db, SAMPLES), chan=lax.rem(c + dc, CHANS),
                ))
    kg[pl.ds(b, 1)] = packed((plain_grad * style[None]).reshape(3 * ib, 4 * ch))[None].astype(BF16)
    for d in range(1, SAMPLES):
        go(remote(kg.at[b], kg.at[b], kg_s.at[d], kg_r.at[d], samples=lax.rem(b + d, SAMPLES)))

    @pl.when(not_first)
    def _():
        edge(dsend.at[0], dhalo, dh_s, dh_r, False).wait_recv()
        dacc[1] = dacc[1] + dhalo[0].astype(F32)

    @pl.when(not_last)
    def _():
        edge(dsend.at[0], dhalo, dh_s, dh_r, True).wait_recv()
        dacc[height] = dacc[height] + dhalo[1].astype(F32)

    def lay_d(g, carry):
        some = pl.ds(pl.multiple_of(g * group, group), group)
        d_ref[some] = jnp.transpose(dacc[pl.ds(1, height), some], (1, 0, 2)).astype(BF16)
        return carry

    lax.fori_loop(0, ch // group, lay_d, 0)

    for d in range(1, SAMPLES):
        src = lax.rem(b + SAMPLES - d, SAMPLES)
        remote(latb.at[src], latb.at[src], in_s.at[0, d], in_r.at[0, d], samples=src).wait_recv()
        remote(selb.at[src], selb.at[src], in_s.at[1, d], in_r.at[1, d], samples=src).wait_recv()
    for db in range(SAMPLES):
        for dc in range(CHANS):
            if db or dc:
                bs, cs = lax.rem(b + SAMPLES - db, SAMPLES), lax.rem(c + CHANS - dc, CHANS)
                remote(
                    st.at[bs, cs], st.at[bs, cs], st_s.at[db, dc], st_r.at[db, dc], samples=bs, chan=cs
                ).wait_recv()

    for d in range(1, SAMPLES):
        src = lax.rem(b + SAMPLES - d, SAMPLES)
        remote(kg.at[src], kg.at[src], kg_s.at[d], kg_r.at[d], samples=src).wait_recv()

    for copy in sent:
        copy.wait_send()
    for part in range(2):
        @pl.when(2 * c + part != r)
        def _():
            remote(gp.at[0, part], gbuf.at[r], g_s.at[0, part], g_r.at[r], rows=2 * c + part).wait_send()

    @pl.when(not_first)
    def _():
        edge(f_ref.at[0], fhalo, fh_s, fh_r, True).wait_send()
        edge(dsend.at[0], dhalo, dh_s, dh_r, True).wait_send()

    @pl.when(not_last)
    def _():
        edge(f_ref.at[0], fhalo, fh_s, fh_r, False).wait_send()
        edge(dsend.at[1], dhalo, dh_s, dh_r, False).wait_send()


def write_out(d_ref, kg, st, latb, selb, d_hbm, bg_hbm, awg_hbm, abg_hbm, bg_ref, awg_ref, abg_ref, sems):
    nb, _, ib, ch = bg_ref.shape
    quarter = d_ref.shape[0] // 4
    copies = []
    for i in range(4):
        some = pl.ds(i * quarter, quarter)
        copies.append(pltpu.make_async_copy(d_ref.at[some], d_hbm.at[some], sems.at[2 + nb + i]))
        copies[-1].start()
    each = [kg[s].astype(F32) for s in range(SAMPLES)]
    for k in range(nb):
        total = unpacked(sum(selb[s][0:1, k : k + 1] * each[s] for s in range(SAMPLES)))
        for kw in range(3):
            for kh in range(3):
                bg_ref[k, 3 * kh + kw] = total[kw * ib : (kw + 1) * ib, (2 - kh) * ch : (3 - kh) * ch]
        copies.append(pltpu.make_async_copy(bg_ref.at[k], bg_hbm.at[k], sems.at[2 + k]))
        copies[-1].start()
    diagonal = lax.broadcasted_iota(jnp.int32, (ib, 128), 0) == lane_iota((ib, 128))
    style_sum = jnp.zeros((1, 128), F32)
    affine = jnp.zeros(awg_ref.shape, F32)
    for s in range(SAMPLES):
        row = st[s, 0] + st[s, 1] + st[s, 2] + st[s, 3]
        style_sum = style_sum + row
        column = jnp.sum(jnp.where(diagonal, row, 0.0), axis=1, keepdims=True)
        affine = affine + column * latb[s][0:1]
    awg_ref[...] = affine
    abg_ref[...] = style_sum[:, :ib]
    copies.append(pltpu.make_async_copy(awg_ref, awg_hbm, sems.at[0]))
    copies[-1].start()
    copies.append(pltpu.make_async_copy(abg_ref, abg_hbm, sems.at[1]))
    copies[-1].start()
    for copy in copies:
        copy.wait()


def on_device(feature, out_grad, bank, select, latent, affine_w, affine_b):
    _, ch, height, width = out_grad.shape
    nb, taps, _, ib = bank.shape
    z = latent.shape[1]
    lanes = 4 * ch
    vmem, hbm = pl.BlockSpec(memory_space=pltpu.VMEM), pl.BlockSpec(memory_space=pltpu.HBM)
    dma = pltpu.SemaphoreType.DMA
    parts = pl.pallas_call(
        kernel,
        out_shape=(
            jax.ShapeDtypeStruct((ch, height, width), BF16),
            jax.ShapeDtypeStruct((SAMPLES, 9 * ib // 2, 128), BF16),
            jax.ShapeDtypeStruct((SAMPLES, CHANS, 1, 128), F32),
            jax.ShapeDtypeStruct((SAMPLES, 8, z), F32),
            jax.ShapeDtypeStruct((SAMPLES, 8, 128), F32),
        ),
        in_specs=[hbm] * 7,
        out_specs=(vmem,) * 5,
        scratch_shapes=[
            pltpu.VMEM((ch, height, width), BF16),
            pltpu.VMEM((ch, height, width), BF16),
            pltpu.VMEM((height, ch, width), BF16),
            pltpu.VMEM((nb, taps, ib, ch), F32),
            pltpu.VMEM((1, nb), jnp.int32),
            pltpu.VMEM((1, z), F32),
            pltpu.VMEM((ib, z), F32),
            pltpu.VMEM((1, ib), F32),
            pltpu.VMEM((height + 5, CHANS, ch, width), BF16),
            pltpu.VMEM((height + 2, 3 * ch, width), BF16),
            pltpu.VMEM((2, ch, width), BF16),
            pltpu.VMEM((4, 3 * ib // 2, 128), BF16),
            pltpu.VMEM((ROWS, 3 * ib // 2, 128), BF16),
            pltpu.VMEM((CHANS, 2, 3 * ib // 2, 128), BF16),
            pltpu.VMEM((CHANS, 2, 3 * ib, lanes), BF16),
            pltpu.VMEM((6 * ib, 3 * CHANS * ch), BF16),
            pltpu.VMEM((CHANS, 2, 3 * ib, lanes), BF16),
            pltpu.VMEM((CHANS, 2, 9 * ib // 2, 128), BF16),
            pltpu.VMEM((ROWS, 9 * ib // 2, 128), BF16),
            pltpu.VMEM((ROWS, 1, 128), F32),
            pltpu.VMEM((CHANS, 1, 128), F32),
            pltpu.VMEM((ROWS, CHANS, 1, 128), F32),
            pltpu.VMEM((CHANS, 1, 128), F32),
            pltpu.VMEM((3, ib, lanes), F32),
            pltpu.VMEM((3, ib, lanes), F32),
            pltpu.VMEM((height + 2, ch, width), F32),
            pltpu.VMEM((2, ch, width), BF16),
            pltpu.VMEM((2, ch, width), BF16),
            dma((2, 5)), dma((2, 5)),
            dma((2,)), dma((2,)),
            dma((2,)), dma((2,)),
            dma((6 + ch // 16,)),
            dma((2, SAMPLES)), dma((2, SAMPLES)),
            dma((ROWS,)), dma((ROWS,)),
            dma((CHANS,)), dma((CHANS,)),
            dma((ROWS,)), dma((ROWS,)), dma((CHANS,)), dma((CHANS,)), dma((5,)), dma((5,)),
            dma((CHANS, 2)), dma((ROWS,)),
            dma((ROWS, CHANS)), dma((ROWS, CHANS)),
            dma((SAMPLES,)), dma((SAMPLES,)),
            dma((SAMPLES, CHANS)), dma((SAMPLES, CHANS)),
        ],
        compiler_params=pltpu.CompilerParams(
            collective_id=0, has_side_effects=True, vmem_limit_bytes=48 * 1024 * 1024
        ),
    )(
        *(pltpu.with_memory_space_constraint(a, pltpu.HBM) for a in (
            out_grad[0], feature[0], jnp.transpose(bank, (0, 1, 3, 2)), select, latent,
            jnp.transpose(affine_w), affine_b[None],
        ))
    )
    d, bg, awg, abg = pl.pallas_call(
        write_out,
        out_shape=(
            jax.ShapeDtypeStruct((ch, height, width), BF16),
            jax.ShapeDtypeStruct((nb, taps, ib, ch), F32),
            jax.ShapeDtypeStruct((ib, z), F32),
            jax.ShapeDtypeStruct((1, ib), F32),
        ),
        in_specs=[vmem] * 5,
        out_specs=(hbm,) * 4,
        scratch_shapes=[
            pltpu.VMEM((nb, taps, ib, ch), F32),
            pltpu.VMEM((ib, z), F32),
            pltpu.VMEM((1, ib), F32),
            dma((6 + nb,)),
        ],
        compiler_params=pltpu.CompilerParams(vmem_limit_bytes=16 * 1024 * 1024),
    )(*parts)
    return d[None], jnp.transpose(bg, (0, 1, 3, 2)), jnp.transpose(awg), abg[0]


def solution(mesh):
    return jax.shard_map(
        on_device,
        mesh=mesh,
        in_specs=(
            P("samples", "chan", "rows", None),
            P("samples", "chan", "rows", None),
            P(None, None, "chan", "rows"),
            P("samples", None),
            P("samples", None),
            P(None, "rows"),
            P("rows"),
        ),
        out_specs=(
            P("samples", "chan", "rows", None),
            P(None, None, "chan", "rows"),
            P(None, "rows"),
            P("rows"),
        ),
        check_vma=False,
    )
```

```python
import jax
import jax.numpy as jnp
from jax import lax
from jax.experimental import pallas as pl
from jax.experimental.pallas import tpu as pltpu
from jax.sharding import PartitionSpec as P

EPS = 1e-08
MESH = pl.DeviceIdType.MESH
ROWS, SAMPLES, CHANS = 8, 4, 4
F32, BF16 = jnp.float32, jnp.bfloat16
FAR_ROWS, FAR_SAMPLES, FAR_CHANS = (2, 6, 3, 5, 1, 7, 4), (2, 3, 1), (2, 1, 3)


def lane_iota(shape):
    return lax.broadcasted_iota(jnp.int32, shape, len(shape) - 1)


def moved_right(x):
    return jnp.where(lane_iota(x.shape) == 0, 0.0, pltpu.roll(x, 1, axis=1))


def moved_left(x):
    width = x.shape[1]
    return jnp.where(lane_iota(x.shape) == width - 1, 0.0, pltpu.roll(x, width - 1, axis=1))


def over_taps(x):
    flat = jnp.sum(x, axis=(0, 1))[None, :]
    half = flat[:, :128] + flat[:, 128:]
    return half + pltpu.roll(half, 64, axis=1)


def packed(x):
    half = x.shape[0] // 2
    return jnp.concatenate(
        [x[:, :128], jnp.concatenate([x[:half, 128:192], x[half:, 128:192]], axis=1)], axis=0
    )


def unpacked(x):
    third = x.shape[0] // 3
    tail = x[2 * third :]
    return jnp.concatenate(
        [x[: 2 * third], jnp.concatenate([tail, pltpu.roll(tail, 64, axis=1)], axis=0)], axis=1
    )


def kernel(
    x_hbm, f_hbm, bank_hbm, sel_hbm, lat_hbm, aw_hbm, ab_hbm,
    d_ref, kg, st, latb, selb,
    xraw, fraw, f_ref, bank_ref, sel_ref, lat_ref, aw_ref, ab_ref, xbuf, fs, fhalo, mown, ms, my, mm, mall, gs, gp, gw, gx, gk, gbuf, en, sc, slv, slo, ker_ref, plain_ref, dacc, dsend, dhalo,
    ag_s, ag_r, fh_s, fh_r, dh_s, dh_r, load_s, in_s, in_r, en_s, en_r, sc_s, sc_r, ms_s, ms_r, my_s, my_r, mm_s, mm_r,
    gx_s, gx_r, g_s, gf_s, g_r, sl_s, sl_r, kg_s, kg_r, st_s, st_r,
):
    r, b, c = lax.axis_index("rows"), lax.axis_index("samples"), lax.axis_index("chan")
    ch, height, width = xraw.shape
    nb, ib = bank_ref.shape[0], bank_ref.shape[2]
    left, right, opp = lax.rem(c + 3, CHANS), lax.rem(c + 1, CHANS), lax.rem(c + 2, CHANS)
    tall = 6 * ib

    def remote(src, dst, send, recv, **where):
        return pltpu.make_async_remote_copy(
            src_ref=src, dst_ref=dst, send_sem=send, recv_sem=recv, device_id=where, device_id_type=MESH
        )

    sent = []

    def go(copy):
        copy.start()
        sent.append(copy)

    group = 16
    pairs = [
        (lat_hbm, lat_ref), (sel_hbm, sel_ref), (ab_hbm, ab_ref), (aw_hbm, aw_ref), (bank_hbm, bank_ref),
        *((x_hbm.at[pl.ds(g, group)], xraw.at[pl.ds(g, group)]) for g in range(0, ch, group)),
        (f_hbm, fraw),
    ]
    loads = [pltpu.make_async_copy(src, dst, load_s.at[i]) for i, (src, dst) in enumerate(pairs)]
    for load in loads:
        load.start()

    barrier = pltpu.get_barrier_semaphore()
    greeted = 0
    for dc in (*FAR_CHANS, 0):
        for dr in (*FAR_ROWS, 0):
            if dr or dc:
                pl.semaphore_signal(
                    barrier, inc=1,
                    device_id={"rows": lax.rem(r + dr, ROWS), "chan": lax.rem(c + dc, CHANS)},
                    device_id_type=MESH,
                )
                greeted += 1
    for db in FAR_SAMPLES:
        for dc in (*FAR_CHANS, 0):
            pl.semaphore_signal(
                barrier, inc=1,
                device_id={"samples": lax.rem(b + db, SAMPLES), "chan": lax.rem(c + dc, CHANS)},
                device_id_type=MESH,
            )
            greeted += 1

    gs[...] = jnp.zeros_like(gs)
    gbuf[ROWS // 2 :] = jnp.zeros((ROWS // 2, *gbuf.shape[1:]), BF16)
    ker_ref[...] = jnp.zeros_like(ker_ref)
    for row in (0, 1, height + 2, height + 3, height + 4):
        xbuf[row] = jnp.zeros(xbuf.shape[1:], BF16)
    for load in loads[:5]:
        load.wait()

    lat = lat_ref[...]
    latb[pl.ds(b, 1)] = jnp.broadcast_to(lat[None], (1, 8, lat.shape[1]))
    sel = sel_ref[...].astype(F32)
    selrow = jnp.zeros((8, 128), F32)
    for k in range(nb):
        selrow = jnp.where(lane_iota((8, 128)) == k, sel[:, k : k + 1], selrow)
    selb[pl.ds(b, 1)] = selrow[None]
    square = lax.broadcasted_iota(jnp.int32, (ib, ib), 0) == lane_iota((ib, ib))
    bias = jnp.sum(jnp.where(square, ab_ref[...], 0.0), axis=1, keepdims=True)
    style = jnp.sum(aw_ref[...] * lat, axis=1, keepdims=True) + bias
    for kh in range(3):
        for kw in range(3):
            tap = sum(sel[:, k : k + 1] * bank_ref[k, 3 * kh + kw] for k in range(nb))
            ker_ref[kw, :, (2 - kh) * ch : (3 - kh) * ch] = tap
    ker = ker_ref[...]
    plain_ref[...] = ker * style[None]
    plain = plain_ref[...]
    en[pl.ds(r, 1)] = over_taps(plain * plain)[None]

    side, level = r // 4, lax.rem(r, 4)
    tile, lanes = 3 * ib // 2, 128
    styled = plain.astype(BF16).reshape(3 * ib, 4 * ch)
    for quarter in range(4):
        top, start = (quarter // 2) * tile, (quarter % 2) * lanes
        mown[quarter] = styled[top : top + tile, start : start + lanes]
    ms[pl.ds(r, 1)] = mown[pl.ds(level, 1)]

    for g in range(0, ch, group):
        loads[5 + g // group].wait()
        xbuf[2 : 2 + height, pl.ds(c, 1), g : g + group] = (
            jnp.transpose(xraw[g : g + group].astype(F32), (1, 0, 2)).astype(BF16)[:, None]
        )

    pl.semaphore_wait(barrier, greeted)

    for d in FAR_ROWS:
        there = lax.rem(r + d, ROWS)
        go(remote(mown.at[lax.rem(there, 4)], ms.at[r], ms_s.at[d], ms_r.at[d], rows=there))
    for d in FAR_ROWS:
        go(remote(en.at[r], en.at[r], en_s.at[d], en_r.at[d], rows=lax.rem(r + d, ROWS)))
    half = height // 2

    def rows_of(shard, first, count):
        return xbuf.at[pl.ds(first + 2, count), shard]

    to_right, to_left = {"chan": right}, {"chan": left}
    go(remote(rows_of(c, 0, half), rows_of(c, 0, half), ag_s.at[0, 0], ag_r.at[0, 0], **to_right))
    go(remote(rows_of(c, half, half), rows_of(c, half, half), ag_s.at[1, 0], ag_r.at[1, 0], **to_left))

    most = half - 1
    go(remote(rows_of(c, half, 1), rows_of(c, half, 1), ag_s.at[0, 4], ag_r.at[0, 4], **to_right))
    go(remote(rows_of(c, most, 1), rows_of(c, most, 1), ag_s.at[1, 4], ag_r.at[1, 4], **to_left))
    for d in range(1, SAMPLES):
        there = lax.rem(b + d, SAMPLES)
        go(remote(latb.at[b], latb.at[b], in_s.at[0, d], in_r.at[0, d], samples=there))
        go(remote(selb.at[b], selb.at[b], in_s.at[1, d], in_r.at[1, d], samples=there))

    loads[-1].wait()

    def lay_f(g, carry):
        some = pl.ds(pl.multiple_of(g * group, group), group)
        f_ref[:, some] = jnp.transpose(fraw[some].astype(F32), (1, 0, 2)).astype(BF16)
        return carry

    lax.fori_loop(0, ch // group, lay_f, 0)

    def edge(src, dst, send, recv, up):
        there = jnp.maximum(r - 1, 0) if up else jnp.minimum(r + 1, ROWS - 1)
        i = 0 if up else 1
        return remote(src, dst.at[1 - i], send.at[i], recv.at[1 - i], rows=there)

    not_first, not_last = r > 0, r < ROWS - 1

    @pl.when(not_first)
    def _():
        edge(f_ref.at[0], fhalo, fh_s, fh_r, True).start()

    @pl.when(not_last)
    def _():
        edge(f_ref.at[height - 1], fhalo, fh_s, fh_r, False).start()

    def shift_into(at, f):
        wide = f.astype(F32)
        for kw, moved in enumerate((moved_right(wide).astype(BF16), f, moved_left(wide).astype(BF16))):
            for part in range(2):
                first = (3 * part + kw) * ib
                fs[at, first : first + ib] = moved[part * ib : (part + 1) * ib]

    def shifted(h, carry):
        shift_into(h + 1, f_ref[h])
        return carry

    lax.fori_loop(0, height, shifted, 0)

    for d in range(1, ROWS):
        src = lax.rem(r + ROWS - d, ROWS)
        remote(mown.at[0], ms.at[src], ms_s.at[d], ms_r.at[d], rows=src).wait_recv()
    my[pl.ds(c, 1)] = ms[pl.ds(2 * c, 2)][None]
    for d in (1, 3, 2):
        there = lax.rem(c + d, CHANS)
        go(remote(ms.at[pl.ds(2 * there, 2)], my.at[c], my_s.at[d], my_r.at[d], chan=there))
    go(remote(rows_of(c, half + 1, most), rows_of(c, half + 1, most), ag_s.at[0, 1], ag_r.at[0, 1], **to_right))
    go(remote(rows_of(c, 0, most), rows_of(c, 0, most), ag_s.at[1, 1], ag_r.at[1, 1], **to_left))

    for d in range(1, ROWS):
        src = lax.rem(r + ROWS - d, ROWS)
        remote(en.at[src], en.at[src], en_s.at[d], en_r.at[d], rows=src).wait_recv()
    scale = lax.rsqrt(jnp.sum(en[...], axis=0) + EPS)
    sc[pl.ds(c, 1)] = scale[None]
    for d in range(1, CHANS):
        go(remote(sc.at[c], sc.at[c], sc_s.at[d], sc_r.at[d], chan=lax.rem(c + d, CHANS)))
    scale = jnp.concatenate([scale, scale], axis=1)[None]

    @pl.when(not_first)
    def _():
        edge(f_ref.at[0], fhalo, fh_s, fh_r, False).wait_recv()
        shift_into(0, fhalo[0])

    @pl.when(r == 0)
    def _():
        fs[0] = jnp.zeros(fs.shape[1:], BF16)

    @pl.when(not_last)
    def _():
        edge(f_ref.at[0], fhalo, fh_s, fh_r, True).wait_recv()
        shift_into(height + 1, fhalo[1])

    @pl.when(r == ROWS - 1)
    def _():
        fs[height + 1] = jnp.zeros(fs.shape[1:], BF16)

    def grad_step(acc, shard, q):
        around = xbuf[q : q + 3, pl.ds(shard, 1)].reshape(3 * ch, width)
        return acc + lax.dot_general(
            fs[q], around, (((1,), (1,)), ((), ())), preferred_element_type=F32
        )

    def grad_rows(acc, shard, steps):
        for q in steps:
            acc = grad_step(acc, shard, q)
        return acc

    no_grad = jnp.zeros((tall, 3 * ch), F32)

    keep = lax.rem(r, 2)
    partner = r + 1 - 2 * keep

    def swap(i):
        return remote(gp.at[i, 1 - keep], gx.at[i], gx_s.at[i], gx_r.at[i], rows=partner)

    def send_grad(i, acc):
        gs[i, :, :, : 3 * ch] = acc.reshape(2, 3 * ib, 3 * ch).astype(BF16)
        for part in range(2):
            wide = packed(acc[part * 3 * ib : (part + 1) * 3 * ib])
            gw[i, part] = wide
            gp[i, part] = wide.astype(BF16)
        if i < 3:
            go(swap(i))

    def block(i, shard):
        return remote(gk.at[i], gbuf.at[r // 2], g_s.at[i], g_r.at[r // 2], rows=2 * c + keep, chan=shard)

    def send_block(i, shard):
        swap(i).wait_recv()
        gk[i] = (gw[i, keep] + gx[i].astype(F32)).astype(BF16)
        if i == 0:
            @pl.when(r // 2 == c)
            def _():
                pltpu.make_async_copy(gk.at[0], gbuf.at[r // 2], g_r.at[r // 2]).start()

            @pl.when(r // 2 != c)
            def _():
                block(0, c).start()
        else:
            go(block(i, shard))

    send_grad(0, grad_rows(no_grad, c, range(height + 2)))

    most = half - 1

    def from_left(k, first, count, shard):
        return remote(rows_of(shard, first, count), rows_of(shard, first, count), ag_s.at[0, k], ag_r.at[0, k], **to_right)

    def from_right(k, first, count, shard):
        return remote(rows_of(shard, first, count), rows_of(shard, first, count), ag_s.at[1, k], ag_r.at[1, k], **to_left)

    def from_left(k, first, count, shard):
        return remote(rows_of(shard, first, count), rows_of(shard, first, count), ag_s.at[0, k], ag_r.at[0, k], **to_right)

    def from_right(k, first, count, shard):
        return remote(rows_of(shard, first, count), rows_of(shard, first, count), ag_s.at[1, k], ag_r.at[1, k], **to_left)

    from_left(0, 0, half, left).wait_recv()
    go(from_left(2, 0, most, left))
    go(from_left(3, most, 1, left))
    from_right(0, half, half, right).wait_recv()
    go(from_right(2, half + 1, most, right))
    go(from_right(3, half, 1, right))

    def both_steps(acc_left, acc_right, steps):
        for q in steps:
            acc_left = grad_step(acc_left, left, q)
            acc_right = grad_step(acc_right, right, height + 1 - q)
        return acc_left, acc_right

    acc_left, acc_right = both_steps(no_grad, no_grad, range(half))

    send_block(0, c)

    for d in range(1, CHANS):
        src = lax.rem(c + CHANS - d, CHANS)
        remote(ms.at[pl.ds(0, 2)], my.at[src], my_s.at[d], my_r.at[d], chan=src).wait_recv()

    def quarter_of(level, shards=slice(None)):
        top = pl.multiple_of((level // 2) * tile, tile)
        start = pl.multiple_of(lax.rem(level, 2) * lanes, lanes)
        return mm.at[shards, :, pl.ds(top, tile), pl.ds(start, lanes)]

    def peer(d):
        return 4 * side + lax.rem(level + d, 4)

    mine = pltpu.make_async_copy(my, quarter_of(level), mm_r.at[0])
    mine.start()
    for d in (1, 3):
        go(remote(my, quarter_of(level), mm_s.at[d], mm_r.at[d], rows=peer(d)))

    from_left(4, half, 1, left).wait_recv()
    from_right(4, most, 1, right).wait_recv()
    from_left(1, half + 1, most, left).wait_recv()
    from_right(1, 0, most, right).wait_recv()

    acc_left, acc_right = both_steps(acc_left, acc_right, range(half, height + 2))
    send_grad(1, acc_left)
    send_grad(2, acc_right)

    def passed(d, level):
        part = quarter_of(level, slice(0, 2) if d == 1 else slice(2, 4))
        return remote(part, part, mm_s.at[1 + d // 2 * 2 + 1], mm_r.at[1 + d // 2 * 2 + 1], rows=peer(d))

    for d in (1, 3):
        src = lax.rem(level + 4 - d, 4)
        remote(my, quarter_of(src), mm_s.at[d], mm_r.at[d], rows=peer(4 - d)).wait_recv()
        go(passed(d, src))

    from_left(2, 0, most, opp).wait_recv()
    from_right(2, half + 1, most, opp).wait_recv()

    early = list(range(most)) + list(range(height + 2 - most, height + 2))
    acc_opp = grad_rows(no_grad, opp, early)

    send_block(1, left)
    send_block(2, right)

    for d in (1, 3):
        passed(d, lax.rem(level + 2, 4)).wait_recv()
    mine.wait()

    def send_slope(i, k, shard):
        slo[i] = over_taps(gs[i].astype(F32) * mm[shard].astype(F32))
        for d in (*FAR_ROWS, 0):
            if k == 0 and d == 0:
                slv[pl.ds(r, 1), pl.ds(c, 1)] = slo[0][None, None]
            else:
                go(remote(
                    slo.at[i], slv.at[r, c], sl_s.at[d, k], sl_r.at[d, k], rows=lax.rem(r + d, ROWS), chan=shard
                ))

    send_slope(0, 0, c)
    send_slope(1, 3, left)
    send_slope(2, 1, right)

    from_left(3, most, 1, opp).wait_recv()
    from_right(3, half, 1, opp).wait_recv()

    send_grad(3, grad_rows(acc_opp, opp, range(most, height + 2 - most)))
    for part in range(2):
        go(remote(gp.at[3, part], gbuf.at[r], gf_s.at[part], g_r.at[r], rows=2 * c + part, chan=opp))
    send_slope(3, 2, opp)

    for d in range(1, CHANS):
        src = lax.rem(c + CHANS - d, CHANS)
        remote(sc.at[src], sc.at[src], sc_s.at[d], sc_r.at[d], chan=src).wait_recv()
    for shard in range(CHANS):
        modulated = mm[shard].reshape(tall, 4 * ch).astype(F32)
        modulated = (modulated * jnp.concatenate([sc[shard], sc[shard]], axis=1)).astype(BF16)
        for kh in range(3):
            at = (kh * CHANS + shard) * ch
            mall[:, at : at + ch] = modulated[:, kh * ch : (kh + 1) * ch]

    def row_out(q):
        first, last = max(q, 2), min(q + 3, height + 2)
        deep = CHANS * ch
        total = jnp.dot(
            mall[:, (first - q) * deep : (last - q) * deep],
            xbuf[first:last].reshape((last - first) * deep, width),
            preferred_element_type=F32,
        )
        for part in range(2):
            t = total[3 * part * ib : 3 * (part + 1) * ib]
            dacc[q, part * ib : (part + 1) * ib] = t[ib : 2 * ib] + moved_left(t[:ib]) + moved_right(t[2 * ib :])

    row_out(0)
    row_out(height + 1)
    dsend[0] = dacc[0].astype(BF16)
    dsend[1] = dacc[height + 1].astype(BF16)

    @pl.when(not_first)
    def _():
        edge(dsend.at[0], dhalo, dh_s, dh_r, True).start()

    @pl.when(not_last)
    def _():
        edge(dsend.at[1], dhalo, dh_s, dh_r, False).start()

    for q in range(1, height + 1):
        row_out(q)

    for src in range(ROWS // 2):
        remote(gk.at[0], gbuf.at[src], g_s.at[0], g_r.at[src], rows=partner).wait_recv()

    @pl.when(lax.rem(c + CHANS - r // 2, CHANS) == 2)
    def _():
        for src in range(ROWS // 2, ROWS):
            remote(gk.at[0], gbuf.at[src], g_s.at[0], g_r.at[src], rows=partner).wait_recv()

    for d in range(ROWS):
        for k in range(CHANS):
            if d or k:
                rs, cs = lax.rem(r + ROWS - d, ROWS), lax.rem(c + CHANS - k, CHANS)
                remote(slo.at[0], slv.at[rs, cs], sl_s.at[d, k], sl_r.at[d, k], rows=rs, chan=cs).wait_recv()

    grad = gbuf[0].astype(F32)
    for src in range(1, ROWS):
        grad = grad + gbuf[src].astype(F32)
    grad = unpacked(grad).reshape(3, ib, 4 * ch)
    slope = jnp.sum(slv[...], axis=(0, 1))
    slope = jnp.concatenate([slope, slope], axis=1)[None]
    plain_grad = grad * scale - plain * (slope * (scale * scale * scale))
    by_input = jnp.sum(plain_grad * ker, axis=0)
    by_input = jnp.concatenate([by_input, jnp.zeros((128 - ib, by_input.shape[1]), F32)], axis=0)
    style_part = lax.dot_general(
        jnp.ones((8, by_input.shape[1]), F32), by_input, (((1,), (1,)), ((), ())),
        preferred_element_type=F32, precision=lax.Precision.HIGHEST,
    )
    st[pl.ds(b, 1), pl.ds(c, 1)] = style_part[0:1][None, None]
    for dc in (*FAR_CHANS, 0):
        for db in (*FAR_SAMPLES, 0):
            if db or dc:
                go(remote(
                    st.at[b, c], st.at[b, c], st_s.at[db, dc], st_r.at[db, dc],
                    samples=lax.rem(b + db, SAMPLES), chan=lax.rem(c + dc, CHANS),
                ))
    kg[pl.ds(b, 1)] = packed((plain_grad * style[None]).reshape(3 * ib, 4 * ch))[None].astype(BF16)
    for d in FAR_SAMPLES:
        go(remote(kg.at[b], kg.at[b], kg_s.at[d], kg_r.at[d], samples=lax.rem(b + d, SAMPLES)))

    @pl.when(not_first)
    def _():
        edge(dsend.at[0], dhalo, dh_s, dh_r, False).wait_recv()
        dacc[1] = dacc[1] + dhalo[0].astype(F32)

    @pl.when(not_last)
    def _():
        edge(dsend.at[0], dhalo, dh_s, dh_r, True).wait_recv()
        dacc[height] = dacc[height] + dhalo[1].astype(F32)

    def lay_d(g, carry):
        some = pl.ds(pl.multiple_of(g * group, group), group)
        d_ref[some] = jnp.transpose(dacc[pl.ds(1, height), some], (1, 0, 2)).astype(BF16)
        return carry

    lax.fori_loop(0, ch // group, lay_d, 0)

    for d in range(1, SAMPLES):
        src = lax.rem(b + SAMPLES - d, SAMPLES)
        remote(latb.at[src], latb.at[src], in_s.at[0, d], in_r.at[0, d], samples=src).wait_recv()
        remote(selb.at[src], selb.at[src], in_s.at[1, d], in_r.at[1, d], samples=src).wait_recv()
    for db in range(SAMPLES):
        for dc in range(CHANS):
            if db or dc:
                bs, cs = lax.rem(b + SAMPLES - db, SAMPLES), lax.rem(c + CHANS - dc, CHANS)
                remote(
                    st.at[bs, cs], st.at[bs, cs], st_s.at[db, dc], st_r.at[db, dc], samples=bs, chan=cs
                ).wait_recv()

    for d in range(1, SAMPLES):
        src = lax.rem(b + SAMPLES - d, SAMPLES)
        remote(kg.at[src], kg.at[src], kg_s.at[d], kg_r.at[d], samples=src).wait_recv()

    for copy in sent:
        copy.wait_send()

    @pl.when(r // 2 != c)
    def _():
        block(0, c).wait_send()

    @pl.when(not_first)
    def _():
        edge(f_ref.at[0], fhalo, fh_s, fh_r, True).wait_send()
        edge(dsend.at[0], dhalo, dh_s, dh_r, True).wait_send()

    @pl.when(not_last)
    def _():
        edge(f_ref.at[0], fhalo, fh_s, fh_r, False).wait_send()
        edge(dsend.at[1], dhalo, dh_s, dh_r, False).wait_send()


def write_out(d_ref, kg, st, latb, selb, d_hbm, bg_hbm, awg_hbm, abg_hbm, bg_ref, awg_ref, abg_ref, sems):
    nb, _, ib, ch = bg_ref.shape
    quarter = d_ref.shape[0] // 4
    copies = []
    for i in range(4):
        some = pl.ds(i * quarter, quarter)
        copies.append(pltpu.make_async_copy(d_ref.at[some], d_hbm.at[some], sems.at[2 + nb + i]))
        copies[-1].start()
    each = [kg[s].astype(F32) for s in range(SAMPLES)]
    for k in range(nb):
        total = unpacked(sum(selb[s][0:1, k : k + 1] * each[s] for s in range(SAMPLES)))
        for kw in range(3):
            for kh in range(3):
                bg_ref[k, 3 * kh + kw] = total[kw * ib : (kw + 1) * ib, (2 - kh) * ch : (3 - kh) * ch]
        copies.append(pltpu.make_async_copy(bg_ref.at[k], bg_hbm.at[k], sems.at[2 + k]))
        copies[-1].start()
    diagonal = lax.broadcasted_iota(jnp.int32, (ib, 128), 0) == lane_iota((ib, 128))
    style_sum = jnp.zeros((1, 128), F32)
    affine = jnp.zeros(awg_ref.shape, F32)
    for s in range(SAMPLES):
        row = st[s, 0] + st[s, 1] + st[s, 2] + st[s, 3]
        style_sum = style_sum + row
        column = jnp.sum(jnp.where(diagonal, row, 0.0), axis=1, keepdims=True)
        affine = affine + column * latb[s][0:1]
    awg_ref[...] = affine
    abg_ref[...] = style_sum[:, :ib]
    copies.append(pltpu.make_async_copy(awg_ref, awg_hbm, sems.at[0]))
    copies[-1].start()
    copies.append(pltpu.make_async_copy(abg_ref, abg_hbm, sems.at[1]))
    copies[-1].start()
    for copy in copies:
        copy.wait()


def on_device(feature, out_grad, bank, select, latent, affine_w, affine_b):
    _, ch, height, width = out_grad.shape
    nb, taps, _, ib = bank.shape
    z = latent.shape[1]
    lanes = 4 * ch
    vmem, hbm = pl.BlockSpec(memory_space=pltpu.VMEM), pl.BlockSpec(memory_space=pltpu.HBM)
    dma = pltpu.SemaphoreType.DMA
    parts = pl.pallas_call(
        kernel,
        out_shape=(
            jax.ShapeDtypeStruct((ch, height, width), BF16),
            jax.ShapeDtypeStruct((SAMPLES, 9 * ib // 2, 128), BF16),
            jax.ShapeDtypeStruct((SAMPLES, CHANS, 1, 128), F32),
            jax.ShapeDtypeStruct((SAMPLES, 8, z), F32),
            jax.ShapeDtypeStruct((SAMPLES, 8, 128), F32),
        ),
        in_specs=[hbm] * 7,
        out_specs=(vmem,) * 5,
        scratch_shapes=[
            pltpu.VMEM((ch, height, width), BF16),
            pltpu.VMEM((ch, height, width), BF16),
            pltpu.VMEM((height, ch, width), BF16),
            pltpu.VMEM((nb, taps, ib, ch), F32),
            pltpu.VMEM((1, nb), jnp.int32),
            pltpu.VMEM((1, z), F32),
            pltpu.VMEM((ib, z), F32),
            pltpu.VMEM((1, ib), F32),
            pltpu.VMEM((height + 5, CHANS, ch, width), BF16),
            pltpu.VMEM((height + 2, 3 * ch, width), BF16),
            pltpu.VMEM((2, ch, width), BF16),
            pltpu.VMEM((4, 3 * ib // 2, 128), BF16),
            pltpu.VMEM((ROWS, 3 * ib // 2, 128), BF16),
            pltpu.VMEM((CHANS, 2, 3 * ib // 2, 128), BF16),
            pltpu.VMEM((CHANS, 2, 3 * ib, lanes), BF16),
            pltpu.VMEM((6 * ib, 3 * CHANS * ch), BF16),
            pltpu.VMEM((CHANS, 2, 3 * ib, lanes), BF16),
            pltpu.VMEM((CHANS, 2, 9 * ib // 2, 128), BF16),
            pltpu.VMEM((CHANS, 2, 9 * ib // 2, 128), F32),
            pltpu.VMEM((CHANS, 9 * ib // 2, 128), BF16),
            pltpu.VMEM((CHANS, 9 * ib // 2, 128), BF16),
            pltpu.VMEM((ROWS, 9 * ib // 2, 128), BF16),
            pltpu.VMEM((ROWS, 1, 128), F32),
            pltpu.VMEM((CHANS, 1, 128), F32),
            pltpu.VMEM((ROWS, CHANS, 1, 128), F32),
            pltpu.VMEM((CHANS, 1, 128), F32),
            pltpu.VMEM((3, ib, lanes), F32),
            pltpu.VMEM((3, ib, lanes), F32),
            pltpu.VMEM((height + 2, ch, width), F32),
            pltpu.VMEM((2, ch, width), BF16),
            pltpu.VMEM((2, ch, width), BF16),
            dma((2, 5)), dma((2, 5)),
            dma((2,)), dma((2,)),
            dma((2,)), dma((2,)),
            dma((6 + ch // 16,)),
            dma((2, SAMPLES)), dma((2, SAMPLES)),
            dma((ROWS,)), dma((ROWS,)),
            dma((CHANS,)), dma((CHANS,)),
            dma((ROWS,)), dma((ROWS,)), dma((CHANS,)), dma((CHANS,)), dma((5,)), dma((5,)),
            dma((CHANS,)), dma((CHANS,)), dma((CHANS,)), dma((2,)), dma((ROWS,)),
            dma((ROWS, CHANS)), dma((ROWS, CHANS)),
            dma((SAMPLES,)), dma((SAMPLES,)),
            dma((SAMPLES, CHANS)), dma((SAMPLES, CHANS)),
        ],
        compiler_params=pltpu.CompilerParams(
            collective_id=0, has_side_effects=True, vmem_limit_bytes=48 * 1024 * 1024
        ),
    )(
        *(pltpu.with_memory_space_constraint(a, pltpu.HBM) for a in (
            out_grad[0], feature[0], jnp.transpose(bank, (0, 1, 3, 2)), select, latent,
            jnp.transpose(affine_w), affine_b[None],
        ))
    )
    d, bg, awg, abg = pl.pallas_call(
        write_out,
        out_shape=(
            jax.ShapeDtypeStruct((ch, height, width), BF16),
            jax.ShapeDtypeStruct((nb, taps, ib, ch), F32),
            jax.ShapeDtypeStruct((ib, z), F32),
            jax.ShapeDtypeStruct((1, ib), F32),
        ),
        in_specs=[vmem] * 5,
        out_specs=(hbm,) * 4,
        scratch_shapes=[
            pltpu.VMEM((nb, taps, ib, ch), F32),
            pltpu.VMEM((ib, z), F32),
            pltpu.VMEM((1, ib), F32),
            dma((6 + nb,)),
        ],
        compiler_params=pltpu.CompilerParams(vmem_limit_bytes=16 * 1024 * 1024),
    )(*parts)
    return d[None], jnp.transpose(bg, (0, 1, 3, 2)), jnp.transpose(awg), abg[0]


def solution(mesh):
    return jax.shard_map(
        on_device,
        mesh=mesh,
        in_specs=(
            P("samples", "chan", "rows", None),
            P("samples", "chan", "rows", None),
            P(None, None, "chan", "rows"),
            P("samples", None),
            P("samples", None),
            P(None, "rows"),
            P("rows"),
        ),
        out_specs=(
            P("samples", "chan", "rows", None),
            P(None, None, "chan", "rows"),
            P(None, "rows"),
            P("rows"),
        ),
        check_vma=False,
    )
```

```python
import jax
import jax.numpy as jnp
from jax import lax
from jax.experimental import pallas as pl
from jax.experimental.pallas import tpu as pltpu
from jax.sharding import PartitionSpec as P

EPS = 1e-08
MESH = pl.DeviceIdType.MESH
ROWS, SAMPLES, CHANS = 8, 4, 4
F32, BF16 = jnp.float32, jnp.bfloat16
FAR_ROWS, FAR_SAMPLES, FAR_CHANS = (2, 6, 3, 5, 1, 7, 4), (2, 3, 1), (2, 1, 3)


def lane_iota(shape):
    return lax.broadcasted_iota(jnp.int32, shape, len(shape) - 1)


def moved_right(x):
    return jnp.where(lane_iota(x.shape) == 0, 0.0, pltpu.roll(x, 1, axis=1))


def moved_left(x):
    width = x.shape[1]
    return jnp.where(lane_iota(x.shape) == width - 1, 0.0, pltpu.roll(x, width - 1, axis=1))


def over_taps(x):
    flat = jnp.sum(x, axis=(0, 1))[None, :]
    half = flat[:, :128] + flat[:, 128:]
    return half + pltpu.roll(half, 64, axis=1)


def packed(x):
    half = x.shape[0] // 2
    return jnp.concatenate(
        [x[:, :128], jnp.concatenate([x[:half, 128:192], x[half:, 128:192]], axis=1)], axis=0
    )


def unpacked(x):
    third = x.shape[0] // 3
    tail = x[2 * third :]
    return jnp.concatenate(
        [x[: 2 * third], jnp.concatenate([tail, pltpu.roll(tail, 64, axis=1)], axis=0)], axis=1
    )


def kernel(
    x_hbm, f_hbm, bank_hbm, sel_hbm, lat_hbm, aw_hbm, ab_hbm,
    d_ref, kg, st, latb, selb,
    xraw, fraw, f_ref, bank_ref, sel_ref, lat_ref, aw_ref, ab_ref, xbuf, fs, fhalo, mown, ms, my, mm, mall, gs, gp, gw, gx, gk, gbuf, en, sc, slv, slo, ker_ref, plain_ref, dacc, dsend, dhalo,
    ag_s, ag_r, fh_s, fh_r, dh_s, dh_r, load_s, in_s, in_r, en_s, en_r, sc_s, sc_r, ms_s, ms_r, my_s, my_r, mm_s, mm_r,
    gx_s, gx_r, g_s, gf_s, g_r, sl_s, sl_r, kg_s, kg_r, st_s, st_r,
):
    r, b, c = lax.axis_index("rows"), lax.axis_index("samples"), lax.axis_index("chan")
    ch, height, width = xraw.shape
    nb, ib = bank_ref.shape[0], bank_ref.shape[2]
    left, right, opp = lax.rem(c + 3, CHANS), lax.rem(c + 1, CHANS), lax.rem(c + 2, CHANS)
    tall = 6 * ib

    def remote(src, dst, send, recv, **where):
        return pltpu.make_async_remote_copy(
            src_ref=src, dst_ref=dst, send_sem=send, recv_sem=recv, device_id=where, device_id_type=MESH
        )

    sent = []

    def go(copy):
        copy.start()
        sent.append(copy)

    group = 16
    pairs = [
        (lat_hbm, lat_ref), (sel_hbm, sel_ref), (ab_hbm, ab_ref), (aw_hbm, aw_ref), (bank_hbm, bank_ref),
        *((x_hbm.at[pl.ds(g, group)], xraw.at[pl.ds(g, group)]) for g in range(0, ch, group)),
        (f_hbm, fraw),
    ]
    loads = [pltpu.make_async_copy(src, dst, load_s.at[i]) for i, (src, dst) in enumerate(pairs)]
    for load in loads:
        load.start()

    barrier = pltpu.get_barrier_semaphore()
    greeted = 0
    for dc in (*FAR_CHANS, 0):
        for dr in (*FAR_ROWS, 0):
            if dr or dc:
                pl.semaphore_signal(
                    barrier, inc=1,
                    device_id={"rows": lax.rem(r + dr, ROWS), "chan": lax.rem(c + dc, CHANS)},
                    device_id_type=MESH,
                )
                greeted += 1
    for db in FAR_SAMPLES:
        for dc in (*FAR_CHANS, 0):
            pl.semaphore_signal(
                barrier, inc=1,
                device_id={"samples": lax.rem(b + db, SAMPLES), "chan": lax.rem(c + dc, CHANS)},
                device_id_type=MESH,
            )
            greeted += 1

    gs[...] = jnp.zeros_like(gs)
    gbuf[ROWS // 2 :] = jnp.zeros((ROWS // 2, *gbuf.shape[1:]), BF16)
    ker_ref[...] = jnp.zeros_like(ker_ref)
    for row in (0, 1, height + 2, height + 3, height + 4):
        xbuf[row] = jnp.zeros(xbuf.shape[1:], BF16)
    for load in loads[:5]:
        load.wait()

    lat = lat_ref[...]
    latb[pl.ds(b, 1)] = jnp.broadcast_to(lat[None], (1, 8, lat.shape[1]))
    sel = sel_ref[...].astype(F32)
    selrow = jnp.zeros((8, 128), F32)
    for k in range(nb):
        selrow = jnp.where(lane_iota((8, 128)) == k, sel[:, k : k + 1], selrow)
    selb[pl.ds(b, 1)] = selrow[None]
    square = lax.broadcasted_iota(jnp.int32, (ib, ib), 0) == lane_iota((ib, ib))
    bias = jnp.sum(jnp.where(square, ab_ref[...], 0.0), axis=1, keepdims=True)
    style = jnp.sum(aw_ref[...] * lat, axis=1, keepdims=True) + bias
    for kh in range(3):
        for kw in range(3):
            tap = sum(sel[:, k : k + 1] * bank_ref[k, 3 * kh + kw] for k in range(nb))
            ker_ref[kw, :, (2 - kh) * ch : (3 - kh) * ch] = tap
    ker = ker_ref[...]
    plain_ref[...] = ker * style[None]
    plain = plain_ref[...]
    en[pl.ds(r, 1)] = over_taps(plain * plain)[None]

    side, level = r // 4, lax.rem(r, 4)
    tile, lanes = 3 * ib // 2, 128
    styled = plain.astype(BF16).reshape(3 * ib, 4 * ch)
    for quarter in range(4):
        top, start = (quarter // 2) * tile, (quarter % 2) * lanes
        mown[quarter] = styled[top : top + tile, start : start + lanes]
    ms[pl.ds(r, 1)] = mown[pl.ds(level, 1)]

    for g in range(0, ch, group):
        loads[5 + g // group].wait()
        xbuf[2 : 2 + height, pl.ds(c, 1), g : g + group] = (
            jnp.transpose(xraw[g : g + group].astype(F32), (1, 0, 2)).astype(BF16)[:, None]
        )

    pl.semaphore_wait(barrier, greeted)

    for d in FAR_ROWS:
        there = lax.rem(r + d, ROWS)
        go(remote(mown.at[lax.rem(there, 4)], ms.at[r], ms_s.at[d], ms_r.at[d], rows=there))
    for d in FAR_ROWS:
        go(remote(en.at[r], en.at[r], en_s.at[d], en_r.at[d], rows=lax.rem(r + d, ROWS)))
    half = height // 2

    def rows_of(shard, first, count):
        return xbuf.at[pl.ds(first + 2, count), shard]

    to_right, to_left = {"chan": right}, {"chan": left}
    go(remote(rows_of(c, 0, half), rows_of(c, 0, half), ag_s.at[0, 0], ag_r.at[0, 0], **to_right))
    go(remote(rows_of(c, half, half), rows_of(c, half, half), ag_s.at[1, 0], ag_r.at[1, 0], **to_left))

    most = half - 1
    go(remote(rows_of(c, half, 1), rows_of(c, half, 1), ag_s.at[0, 4], ag_r.at[0, 4], **to_right))
    go(remote(rows_of(c, most, 1), rows_of(c, most, 1), ag_s.at[1, 4], ag_r.at[1, 4], **to_left))
    for d in range(1, SAMPLES):
        there = lax.rem(b + d, SAMPLES)
        go(remote(latb.at[b], latb.at[b], in_s.at[0, d], in_r.at[0, d], samples=there))
        go(remote(selb.at[b], selb.at[b], in_s.at[1, d], in_r.at[1, d], samples=there))

    loads[-1].wait()

    def lay_f(g, carry):
        some = pl.ds(pl.multiple_of(g * group, group), group)
        f_ref[:, some] = jnp.transpose(fraw[some].astype(F32), (1, 0, 2)).astype(BF16)
        return carry

    lax.fori_loop(0, ch // group, lay_f, 0)

    def edge(src, dst, send, recv, up):
        there = jnp.maximum(r - 1, 0) if up else jnp.minimum(r + 1, ROWS - 1)
        i = 0 if up else 1
        return remote(src, dst.at[1 - i], send.at[i], recv.at[1 - i], rows=there)

    not_first, not_last = r > 0, r < ROWS - 1

    @pl.when(not_first)
    def _():
        edge(f_ref.at[0], fhalo, fh_s, fh_r, True).start()

    @pl.when(not_last)
    def _():
        edge(f_ref.at[height - 1], fhalo, fh_s, fh_r, False).start()

    def shift_into(at, f):
        wide = f.astype(F32)
        for kw, moved in enumerate((moved_right(wide).astype(BF16), f, moved_left(wide).astype(BF16))):
            for part in range(2):
                first = (3 * part + kw) * ib
                fs[at, first : first + ib] = moved[part * ib : (part + 1) * ib]

    def shifted(h, carry):
        shift_into(h + 1, f_ref[h])
        return carry

    lax.fori_loop(0, height, shifted, 0)

    for d in range(1, ROWS):
        src = lax.rem(r + ROWS - d, ROWS)
        remote(mown.at[0], ms.at[src], ms_s.at[d], ms_r.at[d], rows=src).wait_recv()
    my[pl.ds(c, 1)] = ms[pl.ds(2 * c, 2)][None]
    for d in (1, 3, 2):
        there = lax.rem(c + d, CHANS)
        go(remote(ms.at[pl.ds(2 * there, 2)], my.at[c], my_s.at[d], my_r.at[d], chan=there))
    go(remote(rows_of(c, half + 1, most), rows_of(c, half + 1, most), ag_s.at[0, 1], ag_r.at[0, 1], **to_right))
    go(remote(rows_of(c, 0, most), rows_of(c, 0, most), ag_s.at[1, 1], ag_r.at[1, 1], **to_left))

    for d in range(1, ROWS):
        src = lax.rem(r + ROWS - d, ROWS)
        remote(en.at[src], en.at[src], en_s.at[d], en_r.at[d], rows=src).wait_recv()
    scale = lax.rsqrt(jnp.sum(en[...], axis=0) + EPS)
    sc[pl.ds(c, 1)] = scale[None]
    for d in range(1, CHANS):
        go(remote(sc.at[c], sc.at[c], sc_s.at[d], sc_r.at[d], chan=lax.rem(c + d, CHANS)))
    scale = jnp.concatenate([scale, scale], axis=1)[None]

    @pl.when(not_first)
    def _():
        edge(f_ref.at[0], fhalo, fh_s, fh_r, False).wait_recv()
        shift_into(0, fhalo[0])

    @pl.when(r == 0)
    def _():
        fs[0] = jnp.zeros(fs.shape[1:], BF16)

    @pl.when(not_last)
    def _():
        edge(f_ref.at[0], fhalo, fh_s, fh_r, True).wait_recv()
        shift_into(height + 1, fhalo[1])

    @pl.when(r == ROWS - 1)
    def _():
        fs[height + 1] = jnp.zeros(fs.shape[1:], BF16)

    def grad_step(acc, shard, q):
        around = xbuf[q : q + 3, pl.ds(shard, 1)].reshape(3 * ch, width)
        return acc + lax.dot_general(
            fs[q], around, (((1,), (1,)), ((), ())), preferred_element_type=F32
        )

    def grad_rows(acc, shard, steps):
        for q in steps:
            acc = grad_step(acc, shard, q)
        return acc

    no_grad = jnp.zeros((tall, 3 * ch), F32)

    keep = lax.rem(r, 2)
    partner = r + 1 - 2 * keep

    def swap(i):
        return remote(gp.at[i, 1 - keep], gx.at[i], gx_s.at[i], gx_r.at[i], rows=partner)

    def send_grad(i, acc):
        gs[i, :, :, : 3 * ch] = acc.reshape(2, 3 * ib, 3 * ch).astype(BF16)
        for part in range(2):
            wide = packed(acc[part * 3 * ib : (part + 1) * 3 * ib])
            gw[i, part] = wide
            gp[i, part] = wide.astype(BF16)
        if i < 3:
            go(swap(i))

    def block(i, shard):
        return remote(gk.at[i], gbuf.at[r // 2], g_s.at[i], g_r.at[r // 2], rows=2 * c + keep, chan=shard)

    def send_block(i, shard):
        swap(i).wait_recv()
        gk[i] = (gw[i, keep] + gx[i].astype(F32)).astype(BF16)
        if i == 0:
            @pl.when(r // 2 == c)
            def _():
                pltpu.make_async_copy(gk.at[0], gbuf.at[r // 2], g_r.at[r // 2]).start()

            @pl.when(r // 2 != c)
            def _():
                block(0, c).start()
        else:
            go(block(i, shard))

    send_grad(0, grad_rows(no_grad, c, range(height + 2)))

    most = half - 1

    def from_left(k, first, count, shard):
        return remote(rows_of(shard, first, count), rows_of(shard, first, count), ag_s.at[0, k], ag_r.at[0, k], **to_right)

    def from_right(k, first, count, shard):
        return remote(rows_of(shard, first, count), rows_of(shard, first, count), ag_s.at[1, k], ag_r.at[1, k], **to_left)

    def from_left(k, first, count, shard):
        return remote(rows_of(shard, first, count), rows_of(shard, first, count), ag_s.at[0, k], ag_r.at[0, k], **to_right)

    def from_right(k, first, count, shard):
        return remote(rows_of(shard, first, count), rows_of(shard, first, count), ag_s.at[1, k], ag_r.at[1, k], **to_left)

    from_left(0, 0, half, left).wait_recv()
    go(from_left(2, 0, most, left))
    go(from_left(3, most, 1, left))
    from_right(0, half, half, right).wait_recv()
    go(from_right(2, half + 1, most, right))
    go(from_right(3, half, 1, right))

    def both_steps(acc_left, acc_right, steps):
        for q in steps:
            acc_left = grad_step(acc_left, left, q)
            acc_right = grad_step(acc_right, right, height + 1 - q)
        return acc_left, acc_right

    acc_left, acc_right = both_steps(no_grad, no_grad, range(half))

    send_block(0, c)

    for d in range(1, CHANS):
        src = lax.rem(c + CHANS - d, CHANS)
        remote(ms.at[pl.ds(0, 2)], my.at[src], my_s.at[d], my_r.at[d], chan=src).wait_recv()

    def quarter_of(level, shards=slice(None)):
        top = pl.multiple_of((level // 2) * tile, tile)
        start = pl.multiple_of(lax.rem(level, 2) * lanes, lanes)
        return mm.at[shards, :, pl.ds(top, tile), pl.ds(start, lanes)]

    def peer(d):
        return 4 * side + lax.rem(level + d, 4)

    mine = pltpu.make_async_copy(my, quarter_of(level), mm_r.at[0])
    mine.start()
    for d in (2, 1, 3):
        go(remote(my, quarter_of(level), mm_s.at[d], mm_r.at[d], rows=peer(d)))

    from_left(4, half, 1, left).wait_recv()
    from_right(4, most, 1, right).wait_recv()
    from_left(1, half + 1, most, left).wait_recv()
    from_right(1, 0, most, right).wait_recv()

    acc_left, acc_right = both_steps(acc_left, acc_right, range(half, height + 2))
    send_grad(1, acc_left)
    send_grad(2, acc_right)


    from_left(2, 0, most, opp).wait_recv()
    from_right(2, half + 1, most, opp).wait_recv()

    early = list(range(most)) + list(range(height + 2 - most, height + 2))
    acc_opp = grad_rows(no_grad, opp, early)

    send_block(1, left)
    send_block(2, right)

    for d in range(1, 4):
        src = lax.rem(level + 4 - d, 4)
        remote(my, quarter_of(src), mm_s.at[d], mm_r.at[d], rows=peer(4 - d)).wait_recv()
    mine.wait()

    def send_slope(i, k, shard):
        slo[i] = over_taps(gs[i].astype(F32) * mm[shard].astype(F32))
        for d in (*FAR_ROWS, 0):
            if k == 0 and d == 0:
                slv[pl.ds(r, 1), pl.ds(c, 1)] = slo[0][None, None]
            else:
                go(remote(
                    slo.at[i], slv.at[r, c], sl_s.at[d, k], sl_r.at[d, k], rows=lax.rem(r + d, ROWS), chan=shard
                ))

    send_slope(0, 0, c)
    send_slope(1, 3, left)
    send_slope(2, 1, right)

    from_left(3, most, 1, opp).wait_recv()
    from_right(3, half, 1, opp).wait_recv()

    send_grad(3, grad_rows(acc_opp, opp, range(most, height + 2 - most)))
    for part in range(2):
        go(remote(gp.at[3, part], gbuf.at[r], gf_s.at[part], g_r.at[r], rows=2 * c + part, chan=opp))
    send_slope(3, 2, opp)

    for d in range(1, CHANS):
        src = lax.rem(c + CHANS - d, CHANS)
        remote(sc.at[src], sc.at[src], sc_s.at[d], sc_r.at[d], chan=src).wait_recv()
    for shard in range(CHANS):
        modulated = mm[shard].reshape(tall, 4 * ch).astype(F32)
        modulated = (modulated * jnp.concatenate([sc[shard], sc[shard]], axis=1)).astype(BF16)
        for kh in range(3):
            at = (kh * CHANS + shard) * ch
            mall[:, at : at + ch] = modulated[:, kh * ch : (kh + 1) * ch]

    def row_out(q):
        first, last = max(q, 2), min(q + 3, height + 2)
        deep = CHANS * ch
        total = jnp.dot(
            mall[:, (first - q) * deep : (last - q) * deep],
            xbuf[first:last].reshape((last - first) * deep, width),
            preferred_element_type=F32,
        )
        for part in range(2):
            t = total[3 * part * ib : 3 * (part + 1) * ib]
            dacc[q, part * ib : (part + 1) * ib] = t[ib : 2 * ib] + moved_left(t[:ib]) + moved_right(t[2 * ib :])

    row_out(0)
    row_out(height + 1)
    dsend[0] = dacc[0].astype(BF16)
    dsend[1] = dacc[height + 1].astype(BF16)

    @pl.when(not_first)
    def _():
        edge(dsend.at[0], dhalo, dh_s, dh_r, True).start()

    @pl.when(not_last)
    def _():
        edge(dsend.at[1], dhalo, dh_s, dh_r, False).start()

    for q in range(1, height + 1):
        row_out(q)

    for src in range(ROWS // 2):
        remote(gk.at[0], gbuf.at[src], g_s.at[0], g_r.at[src], rows=partner).wait_recv()

    @pl.when(lax.rem(c + CHANS - r // 2, CHANS) == 2)
    def _():
        for src in range(ROWS // 2, ROWS):
            remote(gk.at[0], gbuf.at[src], g_s.at[0], g_r.at[src], rows=partner).wait_recv()

    for d in range(ROWS):
        for k in range(CHANS):
            if d or k:
                rs, cs = lax.rem(r + ROWS - d, ROWS), lax.rem(c + CHANS - k, CHANS)
                remote(slo.at[0], slv.at[rs, cs], sl_s.at[d, k], sl_r.at[d, k], rows=rs, chan=cs).wait_recv()

    grad = gbuf[0].astype(F32)
    for src in range(1, ROWS):
        grad = grad + gbuf[src].astype(F32)
    grad = unpacked(grad).reshape(3, ib, 4 * ch)
    slope = jnp.sum(slv[...], axis=(0, 1))
    slope = jnp.concatenate([slope, slope], axis=1)[None]
    plain_grad = grad * scale - plain * (slope * (scale * scale * scale))
    by_input = jnp.sum(plain_grad * ker, axis=0)
    by_input = jnp.concatenate([by_input, jnp.zeros((128 - ib, by_input.shape[1]), F32)], axis=0)
    style_part = lax.dot_general(
        jnp.ones((8, by_input.shape[1]), F32), by_input, (((1,), (1,)), ((), ())),
        preferred_element_type=F32, precision=lax.Precision.HIGHEST,
    )
    st[pl.ds(b, 1), pl.ds(c, 1)] = style_part[0:1][None, None]
    for dc in (*FAR_CHANS, 0):
        for db in (*FAR_SAMPLES, 0):
            if db or dc:
                go(remote(
                    st.at[b, c], st.at[b, c], st_s.at[db, dc], st_r.at[db, dc],
                    samples=lax.rem(b + db, SAMPLES), chan=lax.rem(c + dc, CHANS),
                ))
    kg[pl.ds(b, 1)] = packed((plain_grad * style[None]).reshape(3 * ib, 4 * ch))[None].astype(BF16)
    for d in FAR_SAMPLES:
        go(remote(kg.at[b], kg.at[b], kg_s.at[d], kg_r.at[d], samples=lax.rem(b + d, SAMPLES)))

    @pl.when(not_first)
    def _():
        edge(dsend.at[0], dhalo, dh_s, dh_r, False).wait_recv()
        dacc[1] = dacc[1] + dhalo[0].astype(F32)

    @pl.when(not_last)
    def _():
        edge(dsend.at[0], dhalo, dh_s, dh_r, True).wait_recv()
        dacc[height] = dacc[height] + dhalo[1].astype(F32)

    def lay_d(g, carry):
        some = pl.ds(pl.multiple_of(g * group, group), group)
        d_ref[some] = jnp.transpose(dacc[pl.ds(1, height), some], (1, 0, 2)).astype(BF16)
        return carry

    lax.fori_loop(0, ch // group, lay_d, 0)

    for d in range(1, SAMPLES):
        src = lax.rem(b + SAMPLES - d, SAMPLES)
        remote(latb.at[src], latb.at[src], in_s.at[0, d], in_r.at[0, d], samples=src).wait_recv()
        remote(selb.at[src], selb.at[src], in_s.at[1, d], in_r.at[1, d], samples=src).wait_recv()
    for db in range(SAMPLES):
        for dc in range(CHANS):
            if db or dc:
                bs, cs = lax.rem(b + SAMPLES - db, SAMPLES), lax.rem(c + CHANS - dc, CHANS)
                remote(
                    st.at[bs, cs], st.at[bs, cs], st_s.at[db, dc], st_r.at[db, dc], samples=bs, chan=cs
                ).wait_recv()

    for d in range(1, SAMPLES):
        src = lax.rem(b + SAMPLES - d, SAMPLES)
        remote(kg.at[src], kg.at[src], kg_s.at[d], kg_r.at[d], samples=src).wait_recv()

    for copy in sent:
        copy.wait_send()

    @pl.when(r // 2 != c)
    def _():
        block(0, c).wait_send()

    @pl.when(not_first)
    def _():
        edge(f_ref.at[0], fhalo, fh_s, fh_r, True).wait_send()
        edge(dsend.at[0], dhalo, dh_s, dh_r, True).wait_send()

    @pl.when(not_last)
    def _():
        edge(f_ref.at[0], fhalo, fh_s, fh_r, False).wait_send()
        edge(dsend.at[1], dhalo, dh_s, dh_r, False).wait_send()


def write_out(d_ref, kg, st, latb, selb, d_hbm, bg_hbm, awg_hbm, abg_hbm, bg_ref, awg_ref, abg_ref, sems):
    nb, _, ib, ch = bg_ref.shape
    quarter = d_ref.shape[0] // 4
    copies = []
    for i in range(4):
        some = pl.ds(i * quarter, quarter)
        copies.append(pltpu.make_async_copy(d_ref.at[some], d_hbm.at[some], sems.at[2 + nb + i]))
        copies[-1].start()
    each = [kg[s].astype(F32) for s in range(SAMPLES)]
    for k in range(nb):
        total = unpacked(sum(selb[s][0:1, k : k + 1] * each[s] for s in range(SAMPLES)))
        for kw in range(3):
            for kh in range(3):
                bg_ref[k, 3 * kh + kw] = total[kw * ib : (kw + 1) * ib, (2 - kh) * ch : (3 - kh) * ch]
        copies.append(pltpu.make_async_copy(bg_ref.at[k], bg_hbm.at[k], sems.at[2 + k]))
        copies[-1].start()
    diagonal = lax.broadcasted_iota(jnp.int32, (ib, 128), 0) == lane_iota((ib, 128))
    style_sum = jnp.zeros((1, 128), F32)
    affine = jnp.zeros(awg_ref.shape, F32)
    for s in range(SAMPLES):
        row = st[s, 0] + st[s, 1] + st[s, 2] + st[s, 3]
        style_sum = style_sum + row
        column = jnp.sum(jnp.where(diagonal, row, 0.0), axis=1, keepdims=True)
        affine = affine + column * latb[s][0:1]
    awg_ref[...] = affine
    abg_ref[...] = style_sum[:, :ib]
    copies.append(pltpu.make_async_copy(awg_ref, awg_hbm, sems.at[0]))
    copies[-1].start()
    copies.append(pltpu.make_async_copy(abg_ref, abg_hbm, sems.at[1]))
    copies[-1].start()
    for copy in copies:
        copy.wait()


def on_device(feature, out_grad, bank, select, latent, affine_w, affine_b):
    _, ch, height, width = out_grad.shape
    nb, taps, _, ib = bank.shape
    z = latent.shape[1]
    lanes = 4 * ch
    vmem, hbm = pl.BlockSpec(memory_space=pltpu.VMEM), pl.BlockSpec(memory_space=pltpu.HBM)
    dma = pltpu.SemaphoreType.DMA
    parts = pl.pallas_call(
        kernel,
        out_shape=(
            jax.ShapeDtypeStruct((ch, height, width), BF16),
            jax.ShapeDtypeStruct((SAMPLES, 9 * ib // 2, 128), BF16),
            jax.ShapeDtypeStruct((SAMPLES, CHANS, 1, 128), F32),
            jax.ShapeDtypeStruct((SAMPLES, 8, z), F32),
            jax.ShapeDtypeStruct((SAMPLES, 8, 128), F32),
        ),
        in_specs=[hbm] * 7,
        out_specs=(vmem,) * 5,
        scratch_shapes=[
            pltpu.VMEM((ch, height, width), BF16),
            pltpu.VMEM((ch, height, width), BF16),
            pltpu.VMEM((height, ch, width), BF16),
            pltpu.VMEM((nb, taps, ib, ch), F32),
            pltpu.VMEM((1, nb), jnp.int32),
            pltpu.VMEM((1, z), F32),
            pltpu.VMEM((ib, z), F32),
            pltpu.VMEM((1, ib), F32),
            pltpu.VMEM((height + 5, CHANS, ch, width), BF16),
            pltpu.VMEM((height + 2, 3 * ch, width), BF16),
            pltpu.VMEM((2, ch, width), BF16),
            pltpu.VMEM((4, 3 * ib // 2, 128), BF16),
            pltpu.VMEM((ROWS, 3 * ib // 2, 128), BF16),
            pltpu.VMEM((CHANS, 2, 3 * ib // 2, 128), BF16),
            pltpu.VMEM((CHANS, 2, 3 * ib, lanes), BF16),
            pltpu.VMEM((6 * ib, 3 * CHANS * ch), BF16),
            pltpu.VMEM((CHANS, 2, 3 * ib, lanes), BF16),
            pltpu.VMEM((CHANS, 2, 9 * ib // 2, 128), BF16),
            pltpu.VMEM((CHANS, 2, 9 * ib // 2, 128), F32),
            pltpu.VMEM((CHANS, 9 * ib // 2, 128), BF16),
            pltpu.VMEM((CHANS, 9 * ib // 2, 128), BF16),
            pltpu.VMEM((ROWS, 9 * ib // 2, 128), BF16),
            pltpu.VMEM((ROWS, 1, 128), F32),
            pltpu.VMEM((CHANS, 1, 128), F32),
            pltpu.VMEM((ROWS, CHANS, 1, 128), F32),
            pltpu.VMEM((CHANS, 1, 128), F32),
            pltpu.VMEM((3, ib, lanes), F32),
            pltpu.VMEM((3, ib, lanes), F32),
            pltpu.VMEM((height + 2, ch, width), F32),
            pltpu.VMEM((2, ch, width), BF16),
            pltpu.VMEM((2, ch, width), BF16),
            dma((2, 5)), dma((2, 5)),
            dma((2,)), dma((2,)),
            dma((2,)), dma((2,)),
            dma((6 + ch // 16,)),
            dma((2, SAMPLES)), dma((2, SAMPLES)),
            dma((ROWS,)), dma((ROWS,)),
            dma((CHANS,)), dma((CHANS,)),
            dma((ROWS,)), dma((ROWS,)), dma((CHANS,)), dma((CHANS,)), dma((5,)), dma((5,)),
            dma((CHANS,)), dma((CHANS,)), dma((CHANS,)), dma((2,)), dma((ROWS,)),
            dma((ROWS, CHANS)), dma((ROWS, CHANS)),
            dma((SAMPLES,)), dma((SAMPLES,)),
            dma((SAMPLES, CHANS)), dma((SAMPLES, CHANS)),
        ],
        compiler_params=pltpu.CompilerParams(
            collective_id=0, has_side_effects=True, vmem_limit_bytes=48 * 1024 * 1024
        ),
    )(
        *(pltpu.with_memory_space_constraint(a, pltpu.HBM) for a in (
            out_grad[0], feature[0], jnp.transpose(bank, (0, 1, 3, 2)), select, latent,
            jnp.transpose(affine_w), affine_b[None],
        ))
    )
    d, bg, awg, abg = pl.pallas_call(
        write_out,
        out_shape=(
            jax.ShapeDtypeStruct((ch, height, width), BF16),
            jax.ShapeDtypeStruct((nb, taps, ib, ch), F32),
            jax.ShapeDtypeStruct((ib, z), F32),
            jax.ShapeDtypeStruct((1, ib), F32),
        ),
        in_specs=[vmem] * 5,
        out_specs=(hbm,) * 4,
        scratch_shapes=[
            pltpu.VMEM((nb, taps, ib, ch), F32),
            pltpu.VMEM((ib, z), F32),
            pltpu.VMEM((1, ib), F32),
            dma((6 + nb,)),
        ],
        compiler_params=pltpu.CompilerParams(vmem_limit_bytes=16 * 1024 * 1024),
    )(*parts)
    return d[None], jnp.transpose(bg, (0, 1, 3, 2)), jnp.transpose(awg), abg[0]


def solution(mesh):
    return jax.shard_map(
        on_device,
        mesh=mesh,
        in_specs=(
            P("samples", "chan", "rows", None),
            P("samples", "chan", "rows", None),
            P(None, None, "chan", "rows"),
            P("samples", None),
            P("samples", None),
            P(None, "rows"),
            P("rows"),
        ),
        out_specs=(
            P("samples", "chan", "rows", None),
            P(None, None, "chan", "rows"),
            P(None, "rows"),
            P("rows"),
        ),
        check_vma=False,
    )
```

```python
import jax
import jax.numpy as jnp
from jax import lax
from jax.experimental import pallas as pl
from jax.experimental.pallas import tpu as pltpu
from jax.sharding import PartitionSpec as P

EPS = 1e-08
MESH = pl.DeviceIdType.MESH
ROWS, SAMPLES, CHANS = 8, 4, 4
F32, BF16 = jnp.float32, jnp.bfloat16
FAR_ROWS, FAR_SAMPLES, FAR_CHANS = (2, 6, 3, 5, 1, 7, 4), (2, 3, 1), (2, 1, 3)


def lane_iota(shape):
    return lax.broadcasted_iota(jnp.int32, shape, len(shape) - 1)


def moved_right(x):
    return jnp.where(lane_iota(x.shape) == 0, 0.0, pltpu.roll(x, 1, axis=1))


def moved_left(x):
    width = x.shape[1]
    return jnp.where(lane_iota(x.shape) == width - 1, 0.0, pltpu.roll(x, width - 1, axis=1))


def over_taps(x):
    flat = jnp.sum(x, axis=(0, 1))[None, :]
    half = flat[:, :128] + flat[:, 128:]
    return half + pltpu.roll(half, 64, axis=1)


def packed(x):
    half = x.shape[0] // 2
    return jnp.concatenate(
        [x[:, :128], jnp.concatenate([x[:half, 128:192], x[half:, 128:192]], axis=1)], axis=0
    )


def unpacked(x):
    third = x.shape[0] // 3
    tail = x[2 * third :]
    return jnp.concatenate(
        [x[: 2 * third], jnp.concatenate([tail, pltpu.roll(tail, 64, axis=1)], axis=0)], axis=1
    )


def kernel(
    x_hbm, f_hbm, bank_hbm, sel_hbm, lat_hbm, aw_hbm, ab_hbm,
    d_ref, bg_ref, st, latb,
    xraw, fraw, f_ref, bank_ref, sel_ref, lat_ref, aw_ref, ab_ref, xbuf, fs, fhalo, mown, ms, my, mm, mall, gs, gp, gw, gx, gk, gbuf, en, sc, slv, slo, kg, selb, ker_ref, plain_ref, dacc, dsend, dhalo,
    ag_s, ag_r, fh_s, fh_r, dh_s, dh_r, load_s, in_s, in_r, en_s, en_r, sc_s, sc_r, ms_s, ms_r, my_s, my_r, mm_s, mm_r,
    gx_s, gx_r, g_s, gf_s, g_r, sl_s, sl_r, kg_s, kg_r, st_s, st_r,
):
    r, b, c = lax.axis_index("rows"), lax.axis_index("samples"), lax.axis_index("chan")
    ch, height, width = xraw.shape
    nb, ib = bank_ref.shape[0], bank_ref.shape[2]
    left, right, opp = lax.rem(c + 3, CHANS), lax.rem(c + 1, CHANS), lax.rem(c + 2, CHANS)
    tall = 6 * ib

    def remote(src, dst, send, recv, **where):
        return pltpu.make_async_remote_copy(
            src_ref=src, dst_ref=dst, send_sem=send, recv_sem=recv, device_id=where, device_id_type=MESH
        )

    sent = []

    def go(copy):
        copy.start()
        sent.append(copy)

    group = 16
    pairs = [
        (lat_hbm, lat_ref), (sel_hbm, sel_ref), (ab_hbm, ab_ref), (aw_hbm, aw_ref), (bank_hbm, bank_ref),
        *((x_hbm.at[pl.ds(g, group)], xraw.at[pl.ds(g, group)]) for g in range(0, ch, group)),
        (f_hbm, fraw),
    ]
    loads = [pltpu.make_async_copy(src, dst, load_s.at[i]) for i, (src, dst) in enumerate(pairs)]
    for load in loads:
        load.start()

    barrier = pltpu.get_barrier_semaphore()
    greeted = 0
    for dc in (*FAR_CHANS, 0):
        for dr in (*FAR_ROWS, 0):
            if dr or dc:
                pl.semaphore_signal(
                    barrier, inc=1,
                    device_id={"rows": lax.rem(r + dr, ROWS), "chan": lax.rem(c + dc, CHANS)},
                    device_id_type=MESH,
                )
                greeted += 1
    for db in FAR_SAMPLES:
        for dc in (*FAR_CHANS, 0):
            pl.semaphore_signal(
                barrier, inc=1,
                device_id={"samples": lax.rem(b + db, SAMPLES), "chan": lax.rem(c + dc, CHANS)},
                device_id_type=MESH,
            )
            greeted += 1

    gs[...] = jnp.zeros_like(gs)
    gbuf[ROWS // 2 :] = jnp.zeros((ROWS // 2, *gbuf.shape[1:]), BF16)
    ker_ref[...] = jnp.zeros_like(ker_ref)
    for row in (0, 1, height + 2, height + 3, height + 4):
        xbuf[row] = jnp.zeros(xbuf.shape[1:], BF16)
    for load in loads[:5]:
        load.wait()

    lat = lat_ref[...]
    latb[pl.ds(b, 1)] = jnp.broadcast_to(lat[None], (1, 8, lat.shape[1]))
    sel = sel_ref[...].astype(F32)
    selrow = jnp.zeros((8, 128), F32)
    for k in range(nb):
        selrow = jnp.where(lane_iota((8, 128)) == k, sel[:, k : k + 1], selrow)
    selb[pl.ds(b, 1)] = selrow[None]
    square = lax.broadcasted_iota(jnp.int32, (ib, ib), 0) == lane_iota((ib, ib))
    bias = jnp.sum(jnp.where(square, ab_ref[...], 0.0), axis=1, keepdims=True)
    style = jnp.sum(aw_ref[...] * lat, axis=1, keepdims=True) + bias
    for kh in range(3):
        for kw in range(3):
            tap = sum(sel[:, k : k + 1] * bank_ref[k, 3 * kh + kw] for k in range(nb))
            ker_ref[kw, :, (2 - kh) * ch : (3 - kh) * ch] = tap
    ker = ker_ref[...]
    plain_ref[...] = ker * style[None]
    plain = plain_ref[...]
    en[pl.ds(r, 1)] = over_taps(plain * plain)[None]

    side, level = r // 4, lax.rem(r, 4)
    tile, lanes = 3 * ib // 2, 128
    styled = plain.astype(BF16).reshape(3 * ib, 4 * ch)
    for quarter in range(4):
        top, start = (quarter // 2) * tile, (quarter % 2) * lanes
        mown[quarter] = styled[top : top + tile, start : start + lanes]
    ms[pl.ds(r, 1)] = mown[pl.ds(level, 1)]

    for g in range(0, ch, group):
        loads[5 + g // group].wait()
        xbuf[2 : 2 + height, pl.ds(c, 1), g : g + group] = (
            jnp.transpose(xraw[g : g + group].astype(F32), (1, 0, 2)).astype(BF16)[:, None]
        )

    pl.semaphore_wait(barrier, greeted)

    for d in FAR_ROWS:
        there = lax.rem(r + d, ROWS)
        go(remote(mown.at[lax.rem(there, 4)], ms.at[r], ms_s.at[d], ms_r.at[d], rows=there))
    for d in FAR_ROWS:
        go(remote(en.at[r], en.at[r], en_s.at[d], en_r.at[d], rows=lax.rem(r + d, ROWS)))
    half = height // 2

    def rows_of(shard, first, count):
        return xbuf.at[pl.ds(first + 2, count), shard]

    to_right, to_left = {"chan": right}, {"chan": left}
    go(remote(rows_of(c, 0, half), rows_of(c, 0, half), ag_s.at[0, 0], ag_r.at[0, 0], **to_right))
    go(remote(rows_of(c, half, half), rows_of(c, half, half), ag_s.at[1, 0], ag_r.at[1, 0], **to_left))

    most = half - 1
    go(remote(rows_of(c, half, 1), rows_of(c, half, 1), ag_s.at[0, 4], ag_r.at[0, 4], **to_right))
    go(remote(rows_of(c, most, 1), rows_of(c, most, 1), ag_s.at[1, 4], ag_r.at[1, 4], **to_left))
    for d in range(1, SAMPLES):
        there = lax.rem(b + d, SAMPLES)
        go(remote(latb.at[b], latb.at[b], in_s.at[0, d], in_r.at[0, d], samples=there))
        go(remote(selb.at[b], selb.at[b], in_s.at[1, d], in_r.at[1, d], samples=there))

    loads[-1].wait()

    def lay_f(g, carry):
        some = pl.ds(pl.multiple_of(g * group, group), group)
        f_ref[:, some] = jnp.transpose(fraw[some].astype(F32), (1, 0, 2)).astype(BF16)
        return carry

    lax.fori_loop(0, ch // group, lay_f, 0)

    def edge(src, dst, send, recv, up):
        there = jnp.maximum(r - 1, 0) if up else jnp.minimum(r + 1, ROWS - 1)
        i = 0 if up else 1
        return remote(src, dst.at[1 - i], send.at[i], recv.at[1 - i], rows=there)

    not_first, not_last = r > 0, r < ROWS - 1

    @pl.when(not_first)
    def _():
        edge(f_ref.at[0], fhalo, fh_s, fh_r, True).start()

    @pl.when(not_last)
    def _():
        edge(f_ref.at[height - 1], fhalo, fh_s, fh_r, False).start()

    def shift_into(at, f):
        wide = f.astype(F32)
        for kw, moved in enumerate((moved_right(wide).astype(BF16), f, moved_left(wide).astype(BF16))):
            for part in range(2):
                first = (3 * part + kw) * ib
                fs[at, first : first + ib] = moved[part * ib : (part + 1) * ib]

    def shifted(h, carry):
        shift_into(h + 1, f_ref[h])
        return carry

    lax.fori_loop(0, height, shifted, 0)

    for d in range(1, ROWS):
        src = lax.rem(r + ROWS - d, ROWS)
        remote(mown.at[0], ms.at[src], ms_s.at[d], ms_r.at[d], rows=src).wait_recv()
    my[pl.ds(c, 1)] = ms[pl.ds(2 * c, 2)][None]
    for d in (1, 3, 2):
        there = lax.rem(c + d, CHANS)
        go(remote(ms.at[pl.ds(2 * there, 2)], my.at[c], my_s.at[d], my_r.at[d], chan=there))
    go(remote(rows_of(c, half + 1, most), rows_of(c, half + 1, most), ag_s.at[0, 1], ag_r.at[0, 1], **to_right))
    go(remote(rows_of(c, 0, most), rows_of(c, 0, most), ag_s.at[1, 1], ag_r.at[1, 1], **to_left))

    for d in range(1, ROWS):
        src = lax.rem(r + ROWS - d, ROWS)
        remote(en.at[src], en.at[src], en_s.at[d], en_r.at[d], rows=src).wait_recv()
    scale = lax.rsqrt(jnp.sum(en[...], axis=0) + EPS)
    sc[pl.ds(c, 1)] = scale[None]
    for d in range(1, CHANS):
        go(remote(sc.at[c], sc.at[c], sc_s.at[d], sc_r.at[d], chan=lax.rem(c + d, CHANS)))
    scale = jnp.concatenate([scale, scale], axis=1)[None]

    @pl.when(not_first)
    def _():
        edge(f_ref.at[0], fhalo, fh_s, fh_r, False).wait_recv()
        shift_into(0, fhalo[0])

    @pl.when(r == 0)
    def _():
        fs[0] = jnp.zeros(fs.shape[1:], BF16)

    @pl.when(not_last)
    def _():
        edge(f_ref.at[0], fhalo, fh_s, fh_r, True).wait_recv()
        shift_into(height + 1, fhalo[1])

    @pl.when(r == ROWS - 1)
    def _():
        fs[height + 1] = jnp.zeros(fs.shape[1:], BF16)

    def grad_step(acc, shard, q):
        around = xbuf[q : q + 3, pl.ds(shard, 1)].reshape(3 * ch, width)
        return acc + lax.dot_general(
            fs[q], around, (((1,), (1,)), ((), ())), preferred_element_type=F32
        )

    def grad_rows(acc, shard, steps):
        for q in steps:
            acc = grad_step(acc, shard, q)
        return acc

    no_grad = jnp.zeros((tall, 3 * ch), F32)

    keep = lax.rem(r, 2)
    partner = r + 1 - 2 * keep

    def swap(i):
        return remote(gp.at[i, 1 - keep], gx.at[i], gx_s.at[i], gx_r.at[i], rows=partner)

    def send_grad(i, acc):
        gs[i, :, :, : 3 * ch] = acc.reshape(2, 3 * ib, 3 * ch).astype(BF16)
        for part in range(2):
            wide = packed(acc[part * 3 * ib : (part + 1) * 3 * ib])
            gw[i, part] = wide
            gp[i, part] = wide.astype(BF16)
        if i < 3:
            go(swap(i))

    def block(i, shard):
        return remote(gk.at[i], gbuf.at[r // 2], g_s.at[i], g_r.at[r // 2], rows=2 * c + keep, chan=shard)

    def send_block(i, shard):
        swap(i).wait_recv()
        gk[i] = (gw[i, keep] + gx[i].astype(F32)).astype(BF16)
        if i == 0:
            @pl.when(r // 2 == c)
            def _():
                pltpu.make_async_copy(gk.at[0], gbuf.at[r // 2], g_r.at[r // 2]).start()

            @pl.when(r // 2 != c)
            def _():
                block(0, c).start()
        else:
            go(block(i, shard))

    send_grad(0, grad_rows(no_grad, c, range(height + 2)))

    most = half - 1

    def from_left(k, first, count, shard):
        return remote(rows_of(shard, first, count), rows_of(shard, first, count), ag_s.at[0, k], ag_r.at[0, k], **to_right)

    def from_right(k, first, count, shard):
        return remote(rows_of(shard, first, count), rows_of(shard, first, count), ag_s.at[1, k], ag_r.at[1, k], **to_left)

    def from_left(k, first, count, shard):
        return remote(rows_of(shard, first, count), rows_of(shard, first, count), ag_s.at[0, k], ag_r.at[0, k], **to_right)

    def from_right(k, first, count, shard):
        return remote(rows_of(shard, first, count), rows_of(shard, first, count), ag_s.at[1, k], ag_r.at[1, k], **to_left)

    from_left(0, 0, half, left).wait_recv()
    go(from_left(2, 0, most, left))
    go(from_left(3, most, 1, left))
    from_right(0, half, half, right).wait_recv()
    go(from_right(2, half + 1, most, right))
    go(from_right(3, half, 1, right))

    def both_steps(acc_left, acc_right, steps):
        for q in steps:
            acc_left = grad_step(acc_left, left, q)
            acc_right = grad_step(acc_right, right, height + 1 - q)
        return acc_left, acc_right

    acc_left, acc_right = both_steps(no_grad, no_grad, range(half))

    send_block(0, c)

    for d in range(1, CHANS):
        src = lax.rem(c + CHANS - d, CHANS)
        remote(ms.at[pl.ds(0, 2)], my.at[src], my_s.at[d], my_r.at[d], chan=src).wait_recv()

    def quarter_of(level, shards=slice(None)):
        top = pl.multiple_of((level // 2) * tile, tile)
        start = pl.multiple_of(lax.rem(level, 2) * lanes, lanes)
        return mm.at[shards, :, pl.ds(top, tile), pl.ds(start, lanes)]

    def peer(d):
        return 4 * side + lax.rem(level + d, 4)

    mine = pltpu.make_async_copy(my, quarter_of(level), mm_r.at[0])
    mine.start()
    for d in (2, 1, 3):
        go(remote(my, quarter_of(level), mm_s.at[d], mm_r.at[d], rows=peer(d)))

    from_left(4, half, 1, left).wait_recv()
    from_right(4, most, 1, right).wait_recv()
    from_left(1, half + 1, most, left).wait_recv()
    from_right(1, 0, most, right).wait_recv()

    acc_left, acc_right = both_steps(acc_left, acc_right, range(half, height + 2))
    send_grad(1, acc_left)
    send_grad(2, acc_right)


    from_left(2, 0, most, opp).wait_recv()
    from_right(2, half + 1, most, opp).wait_recv()

    early = list(range(most)) + list(range(height + 2 - most, height + 2))
    acc_opp = grad_rows(no_grad, opp, early)

    send_block(1, left)
    send_block(2, right)

    for d in range(1, 4):
        src = lax.rem(level + 4 - d, 4)
        remote(my, quarter_of(src), mm_s.at[d], mm_r.at[d], rows=peer(4 - d)).wait_recv()
    mine.wait()

    def send_slope(i, k, shard):
        slo[i] = over_taps(gs[i].astype(F32) * mm[shard].astype(F32))
        for d in (*FAR_ROWS, 0):
            if k == 0 and d == 0:
                slv[pl.ds(r, 1), pl.ds(c, 1)] = slo[0][None, None]
            else:
                go(remote(
                    slo.at[i], slv.at[r, c], sl_s.at[d, k], sl_r.at[d, k], rows=lax.rem(r + d, ROWS), chan=shard
                ))

    send_slope(0, 0, c)
    send_slope(1, 3, left)
    send_slope(2, 1, right)

    from_left(3, most, 1, opp).wait_recv()
    from_right(3, half, 1, opp).wait_recv()

    send_grad(3, grad_rows(acc_opp, opp, range(most, height + 2 - most)))
    for part in range(2):
        go(remote(gp.at[3, part], gbuf.at[r], gf_s.at[part], g_r.at[r], rows=2 * c + part, chan=opp))
    send_slope(3, 2, opp)

    for d in range(1, CHANS):
        src = lax.rem(c + CHANS - d, CHANS)
        remote(sc.at[src], sc.at[src], sc_s.at[d], sc_r.at[d], chan=src).wait_recv()
    for shard in range(CHANS):
        modulated = mm[shard].reshape(tall, 4 * ch).astype(F32)
        modulated = (modulated * jnp.concatenate([sc[shard], sc[shard]], axis=1)).astype(BF16)
        for kh in range(3):
            at = (kh * CHANS + shard) * ch
            mall[:, at : at + ch] = modulated[:, kh * ch : (kh + 1) * ch]

    def row_out(q):
        first, last = max(q, 2), min(q + 3, height + 2)
        deep = CHANS * ch
        total = jnp.dot(
            mall[:, (first - q) * deep : (last - q) * deep],
            xbuf[first:last].reshape((last - first) * deep, width),
            preferred_element_type=F32,
        )
        for part in range(2):
            t = total[3 * part * ib : 3 * (part + 1) * ib]
            dacc[q, part * ib : (part + 1) * ib] = t[ib : 2 * ib] + moved_left(t[:ib]) + moved_right(t[2 * ib :])

    row_out(0)
    row_out(height + 1)
    dsend[0] = dacc[0].astype(BF16)
    dsend[1] = dacc[height + 1].astype(BF16)

    @pl.when(not_first)
    def _():
        edge(dsend.at[0], dhalo, dh_s, dh_r, True).start()

    @pl.when(not_last)
    def _():
        edge(dsend.at[1], dhalo, dh_s, dh_r, False).start()

    for q in range(1, height + 1):
        row_out(q)

    for src in range(ROWS // 2):
        remote(gk.at[0], gbuf.at[src], g_s.at[0], g_r.at[src], rows=partner).wait_recv()

    @pl.when(lax.rem(c + CHANS - r // 2, CHANS) == 2)
    def _():
        for src in range(ROWS // 2, ROWS):
            remote(gk.at[0], gbuf.at[src], g_s.at[0], g_r.at[src], rows=partner).wait_recv()

    for d in range(ROWS):
        for k in range(CHANS):
            if d or k:
                rs, cs = lax.rem(r + ROWS - d, ROWS), lax.rem(c + CHANS - k, CHANS)
                remote(slo.at[0], slv.at[rs, cs], sl_s.at[d, k], sl_r.at[d, k], rows=rs, chan=cs).wait_recv()

    grad = gbuf[0].astype(F32)
    for src in range(1, ROWS):
        grad = grad + gbuf[src].astype(F32)
    grad = unpacked(grad).reshape(3, ib, 4 * ch)
    slope = jnp.sum(slv[...], axis=(0, 1))
    slope = jnp.concatenate([slope, slope], axis=1)[None]
    plain_grad = grad * scale - plain * (slope * (scale * scale * scale))
    by_input = jnp.sum(plain_grad * ker, axis=0)
    by_input = jnp.concatenate([by_input, jnp.zeros((128 - ib, by_input.shape[1]), F32)], axis=0)
    style_part = lax.dot_general(
        jnp.ones((8, by_input.shape[1]), F32), by_input, (((1,), (1,)), ((), ())),
        preferred_element_type=F32, precision=lax.Precision.HIGHEST,
    )
    st[pl.ds(b, 1), pl.ds(c, 1)] = style_part[0:1][None, None]
    for dc in (*FAR_CHANS, 0):
        for db in (*FAR_SAMPLES, 0):
            if db or dc:
                go(remote(
                    st.at[b, c], st.at[b, c], st_s.at[db, dc], st_r.at[db, dc],
                    samples=lax.rem(b + db, SAMPLES), chan=lax.rem(c + dc, CHANS),
                ))
    kg[pl.ds(b, 1)] = packed((plain_grad * style[None]).reshape(3 * ib, 4 * ch))[None].astype(BF16)
    for d in FAR_SAMPLES:
        go(remote(kg.at[b], kg.at[b], kg_s.at[d], kg_r.at[d], samples=lax.rem(b + d, SAMPLES)))

    @pl.when(not_first)
    def _():
        edge(dsend.at[0], dhalo, dh_s, dh_r, False).wait_recv()
        dacc[1] = dacc[1] + dhalo[0].astype(F32)

    @pl.when(not_last)
    def _():
        edge(dsend.at[0], dhalo, dh_s, dh_r, True).wait_recv()
        dacc[height] = dacc[height] + dhalo[1].astype(F32)

    def lay_d(g, carry):
        some = pl.ds(pl.multiple_of(g * group, group), group)
        d_ref[some] = jnp.transpose(dacc[pl.ds(1, height), some], (1, 0, 2)).astype(BF16)
        return carry

    lax.fori_loop(0, ch // group, lay_d, 0)

    for d in range(1, SAMPLES):
        src = lax.rem(b + SAMPLES - d, SAMPLES)
        remote(kg.at[src], kg.at[src], kg_s.at[d], kg_r.at[d], samples=src).wait_recv()
    for d in range(1, SAMPLES):
        src = lax.rem(b + SAMPLES - d, SAMPLES)
        remote(latb.at[src], latb.at[src], in_s.at[0, d], in_r.at[0, d], samples=src).wait_recv()
        remote(selb.at[src], selb.at[src], in_s.at[1, d], in_r.at[1, d], samples=src).wait_recv()

    each = [kg[s].astype(F32) for s in range(SAMPLES)]
    for k in range(nb):
        total = unpacked(sum(selb[s][0:1, k : k + 1] * each[s] for s in range(SAMPLES)))
        for kw in range(3):
            for kh in range(3):
                bg_ref[k, 3 * kh + kw] = total[kw * ib : (kw + 1) * ib, (2 - kh) * ch : (3 - kh) * ch]

    for db in range(SAMPLES):
        for dc in range(CHANS):
            if db or dc:
                bs, cs = lax.rem(b + SAMPLES - db, SAMPLES), lax.rem(c + CHANS - dc, CHANS)
                remote(
                    st.at[bs, cs], st.at[bs, cs], st_s.at[db, dc], st_r.at[db, dc], samples=bs, chan=cs
                ).wait_recv()

    for copy in sent:
        copy.wait_send()

    @pl.when(r // 2 != c)
    def _():
        block(0, c).wait_send()

    @pl.when(not_first)
    def _():
        edge(f_ref.at[0], fhalo, fh_s, fh_r, True).wait_send()
        edge(dsend.at[0], dhalo, dh_s, dh_r, True).wait_send()

    @pl.when(not_last)
    def _():
        edge(f_ref.at[0], fhalo, fh_s, fh_r, False).wait_send()
        edge(dsend.at[1], dhalo, dh_s, dh_r, False).wait_send()


def write_out(d_ref, bg_ref, st, latb, d_hbm, bg_hbm, awg_hbm, abg_hbm, awg_ref, abg_ref, sems):
    nb, _, ib, _ = bg_ref.shape
    quarter = d_ref.shape[0] // 4
    copies = []
    for i in range(4):
        some = pl.ds(i * quarter, quarter)
        copies.append(pltpu.make_async_copy(d_ref.at[some], d_hbm.at[some], sems.at[2 + nb + i]))
        copies[-1].start()
    for k in range(nb):
        copies.append(pltpu.make_async_copy(bg_ref.at[k], bg_hbm.at[k], sems.at[2 + k]))
        copies[-1].start()
    diagonal = lax.broadcasted_iota(jnp.int32, (ib, 128), 0) == lane_iota((ib, 128))
    style_sum = jnp.zeros((1, 128), F32)
    affine = jnp.zeros(awg_ref.shape, F32)
    for s in range(SAMPLES):
        row = st[s, 0] + st[s, 1] + st[s, 2] + st[s, 3]
        style_sum = style_sum + row
        column = jnp.sum(jnp.where(diagonal, row, 0.0), axis=1, keepdims=True)
        affine = affine + column * latb[s][0:1]
    awg_ref[...] = affine
    abg_ref[...] = style_sum[:, :ib]
    copies.append(pltpu.make_async_copy(awg_ref, awg_hbm, sems.at[0]))
    copies[-1].start()
    copies.append(pltpu.make_async_copy(abg_ref, abg_hbm, sems.at[1]))
    copies[-1].start()
    for copy in copies:
        copy.wait()


def on_device(feature, out_grad, bank, select, latent, affine_w, affine_b):
    _, ch, height, width = out_grad.shape
    nb, taps, _, ib = bank.shape
    z = latent.shape[1]
    lanes = 4 * ch
    vmem, hbm = pl.BlockSpec(memory_space=pltpu.VMEM), pl.BlockSpec(memory_space=pltpu.HBM)
    dma = pltpu.SemaphoreType.DMA
    parts = pl.pallas_call(
        kernel,
        out_shape=(
            jax.ShapeDtypeStruct((ch, height, width), BF16),
            jax.ShapeDtypeStruct((nb, taps, ib, ch), F32),
            jax.ShapeDtypeStruct((SAMPLES, CHANS, 1, 128), F32),
            jax.ShapeDtypeStruct((SAMPLES, 8, z), F32),
        ),
        in_specs=[hbm] * 7,
        out_specs=(vmem,) * 4,
        scratch_shapes=[
            pltpu.VMEM((ch, height, width), BF16),
            pltpu.VMEM((ch, height, width), BF16),
            pltpu.VMEM((height, ch, width), BF16),
            pltpu.VMEM((nb, taps, ib, ch), F32),
            pltpu.VMEM((1, nb), jnp.int32),
            pltpu.VMEM((1, z), F32),
            pltpu.VMEM((ib, z), F32),
            pltpu.VMEM((1, ib), F32),
            pltpu.VMEM((height + 5, CHANS, ch, width), BF16),
            pltpu.VMEM((height + 2, 3 * ch, width), BF16),
            pltpu.VMEM((2, ch, width), BF16),
            pltpu.VMEM((4, 3 * ib // 2, 128), BF16),
            pltpu.VMEM((ROWS, 3 * ib // 2, 128), BF16),
            pltpu.VMEM((CHANS, 2, 3 * ib // 2, 128), BF16),
            pltpu.VMEM((CHANS, 2, 3 * ib, lanes), BF16),
            pltpu.VMEM((6 * ib, 3 * CHANS * ch), BF16),
            pltpu.VMEM((CHANS, 2, 3 * ib, lanes), BF16),
            pltpu.VMEM((CHANS, 2, 9 * ib // 2, 128), BF16),
            pltpu.VMEM((CHANS, 2, 9 * ib // 2, 128), F32),
            pltpu.VMEM((CHANS, 9 * ib // 2, 128), BF16),
            pltpu.VMEM((CHANS, 9 * ib // 2, 128), BF16),
            pltpu.VMEM((ROWS, 9 * ib // 2, 128), BF16),
            pltpu.VMEM((ROWS, 1, 128), F32),
            pltpu.VMEM((CHANS, 1, 128), F32),
            pltpu.VMEM((ROWS, CHANS, 1, 128), F32),
            pltpu.VMEM((CHANS, 1, 128), F32),
            pltpu.VMEM((SAMPLES, 9 * ib // 2, 128), BF16),
            pltpu.VMEM((SAMPLES, 8, 128), F32),
            pltpu.VMEM((3, ib, lanes), F32),
            pltpu.VMEM((3, ib, lanes), F32),
            pltpu.VMEM((height + 2, ch, width), F32),
            pltpu.VMEM((2, ch, width), BF16),
            pltpu.VMEM((2, ch, width), BF16),
            dma((2, 5)), dma((2, 5)),
            dma((2,)), dma((2,)),
            dma((2,)), dma((2,)),
            dma((6 + ch // 16,)),
            dma((2, SAMPLES)), dma((2, SAMPLES)),
            dma((ROWS,)), dma((ROWS,)),
            dma((CHANS,)), dma((CHANS,)),
            dma((ROWS,)), dma((ROWS,)), dma((CHANS,)), dma((CHANS,)), dma((5,)), dma((5,)),
            dma((CHANS,)), dma((CHANS,)), dma((CHANS,)), dma((2,)), dma((ROWS,)),
            dma((ROWS, CHANS)), dma((ROWS, CHANS)),
            dma((SAMPLES,)), dma((SAMPLES,)),
            dma((SAMPLES, CHANS)), dma((SAMPLES, CHANS)),
        ],
        compiler_params=pltpu.CompilerParams(
            collective_id=0, has_side_effects=True, vmem_limit_bytes=48 * 1024 * 1024
        ),
    )(
        *(pltpu.with_memory_space_constraint(a, pltpu.HBM) for a in (
            out_grad[0], feature[0], jnp.transpose(bank, (0, 1, 3, 2)), select, latent,
            jnp.transpose(affine_w), affine_b[None],
        ))
    )
    d, bg, awg, abg = pl.pallas_call(
        write_out,
        out_shape=(
            jax.ShapeDtypeStruct((ch, height, width), BF16),
            jax.ShapeDtypeStruct((nb, taps, ib, ch), F32),
            jax.ShapeDtypeStruct((ib, z), F32),
            jax.ShapeDtypeStruct((1, ib), F32),
        ),
        in_specs=[vmem] * 4,
        out_specs=(hbm,) * 4,
        scratch_shapes=[
            pltpu.VMEM((ib, z), F32),
            pltpu.VMEM((1, ib), F32),
            dma((6 + nb,)),
        ],
        compiler_params=pltpu.CompilerParams(vmem_limit_bytes=16 * 1024 * 1024),
    )(*parts)
    return d[None], jnp.transpose(bg, (0, 1, 3, 2)), jnp.transpose(awg), abg[0]


def solution(mesh):
    return jax.shard_map(
        on_device,
        mesh=mesh,
        in_specs=(
            P("samples", "chan", "rows", None),
            P("samples", "chan", "rows", None),
            P(None, None, "chan", "rows"),
            P("samples", None),
            P("samples", None),
            P(None, "rows"),
            P("rows"),
        ),
        out_specs=(
            P("samples", "chan", "rows", None),
            P(None, None, "chan", "rows"),
            P(None, "rows"),
            P("rows"),
        ),
        check_vma=False,
    )
```

```python
import jax
import jax.numpy as jnp
from jax import lax
from jax.experimental import pallas as pl
from jax.experimental.pallas import tpu as pltpu
from jax.sharding import PartitionSpec as P

EPS = 1e-08
MESH = pl.DeviceIdType.MESH
ROWS, SAMPLES, CHANS = 8, 4, 4
F32, BF16 = jnp.float32, jnp.bfloat16
FAR_ROWS, FAR_SAMPLES, FAR_CHANS = (2, 6, 3, 5, 1, 7, 4), (2, 3, 1), (2, 1, 3)


def lane_iota(shape):
    return lax.broadcasted_iota(jnp.int32, shape, len(shape) - 1)


def moved_right(x):
    return jnp.where(lane_iota(x.shape) == 0, 0.0, pltpu.roll(x, 1, axis=1))


def moved_left(x):
    width = x.shape[1]
    return jnp.where(lane_iota(x.shape) == width - 1, 0.0, pltpu.roll(x, width - 1, axis=1))


def over_taps(x):
    flat = jnp.sum(x, axis=(0, 1))[None, :]
    half = flat[:, :128] + flat[:, 128:]
    return half + pltpu.roll(half, 64, axis=1)


def packed(x):
    half = x.shape[0] // 2
    return jnp.concatenate(
        [x[:, :128], jnp.concatenate([x[:half, 128:192], x[half:, 128:192]], axis=1)], axis=0
    )


def unpacked(x):
    third = x.shape[0] // 3
    tail = x[2 * third :]
    return jnp.concatenate(
        [x[: 2 * third], jnp.concatenate([tail, pltpu.roll(tail, 64, axis=1)], axis=0)], axis=1
    )


def kernel(
    x_hbm, f_hbm, bank_hbm, sel_hbm, lat_hbm, aw_hbm, ab_hbm,
    d_ref, kg, st, latb, selb,
    xraw, fraw, f_ref, bank_ref, sel_ref, lat_ref, aw_ref, ab_ref, xbuf, fs, fhalo, mown, ms, my, mm, mall, gs, gp, gw, gx, gk, gbuf, en, sc, slv, slo, ker_ref, plain_ref, dacc, dsend, dhalo,
    ag_s, ag_r, fh_s, fh_r, dh_s, dh_r, load_s, in_s, in_r, en_s, en_r, sc_s, sc_r, ms_s, ms_r, my_s, my_r, mm_s, mm_r,
    gx_s, gx_r, g_s, gf_s, g_r, sl_s, sl_r, kg_s, kg_r, st_s, st_r,
):
    r, b, c = lax.axis_index("rows"), lax.axis_index("samples"), lax.axis_index("chan")
    ch, height, width = xraw.shape
    nb, ib = bank_ref.shape[0], bank_ref.shape[2]
    left, right, opp = lax.rem(c + 3, CHANS), lax.rem(c + 1, CHANS), lax.rem(c + 2, CHANS)
    tall = 6 * ib

    def remote(src, dst, send, recv, **where):
        return pltpu.make_async_remote_copy(
            src_ref=src, dst_ref=dst, send_sem=send, recv_sem=recv, device_id=where, device_id_type=MESH
        )

    sent = []

    def go(copy):
        copy.start()
        sent.append(copy)

    group = 16
    pairs = [
        (lat_hbm, lat_ref), (sel_hbm, sel_ref), (ab_hbm, ab_ref), (aw_hbm, aw_ref), (bank_hbm, bank_ref),
        *((x_hbm.at[pl.ds(g, group)], xraw.at[pl.ds(g, group)]) for g in range(0, ch, group)),
        (f_hbm, fraw),
    ]
    loads = [pltpu.make_async_copy(src, dst, load_s.at[i]) for i, (src, dst) in enumerate(pairs)]
    for load in loads:
        load.start()

    barrier = pltpu.get_barrier_semaphore()
    greeted = 0
    for dc in (*FAR_CHANS, 0):
        for dr in (*FAR_ROWS, 0):
            if dr or dc:
                pl.semaphore_signal(
                    barrier, inc=1,
                    device_id={"rows": lax.rem(r + dr, ROWS), "chan": lax.rem(c + dc, CHANS)},
                    device_id_type=MESH,
                )
                greeted += 1
    for db in FAR_SAMPLES:
        for dc in (*FAR_CHANS, 0):
            pl.semaphore_signal(
                barrier, inc=1,
                device_id={"samples": lax.rem(b + db, SAMPLES), "chan": lax.rem(c + dc, CHANS)},
                device_id_type=MESH,
            )
            greeted += 1

    gs[...] = jnp.zeros_like(gs)
    gbuf[ROWS // 2 :] = jnp.zeros((ROWS // 2, *gbuf.shape[1:]), BF16)
    ker_ref[...] = jnp.zeros_like(ker_ref)
    for row in (0, 1, height + 2, height + 3, height + 4):
        xbuf[row] = jnp.zeros(xbuf.shape[1:], BF16)
    for load in loads[:5]:
        load.wait()

    lat = lat_ref[...]
    latb[pl.ds(b, 1)] = jnp.broadcast_to(lat[None], (1, 8, lat.shape[1]))
    sel = sel_ref[...].astype(F32)
    selrow = jnp.zeros((8, 128), F32)
    for k in range(nb):
        selrow = jnp.where(lane_iota((8, 128)) == k, sel[:, k : k + 1], selrow)
    selb[pl.ds(b, 1)] = selrow[None]
    square = lax.broadcasted_iota(jnp.int32, (ib, ib), 0) == lane_iota((ib, ib))
    bias = jnp.sum(jnp.where(square, ab_ref[...], 0.0), axis=1, keepdims=True)
    style = jnp.sum(aw_ref[...] * lat, axis=1, keepdims=True) + bias
    for kh in range(3):
        for kw in range(3):
            tap = sum(sel[:, k : k + 1] * bank_ref[k, 3 * kh + kw] for k in range(nb))
            ker_ref[kw, :, (2 - kh) * ch : (3 - kh) * ch] = tap
    ker = ker_ref[...]
    plain_ref[...] = ker * style[None]
    plain = plain_ref[...]
    en[pl.ds(r, 1)] = over_taps(plain * plain)[None]

    side, level = r // 4, lax.rem(r, 4)
    tile, lanes = 3 * ib // 2, 128
    styled = plain.astype(BF16).reshape(3 * ib, 4 * ch)
    for quarter in range(4):
        top, start = (quarter // 2) * tile, (quarter % 2) * lanes
        mown[quarter] = styled[top : top + tile, start : start + lanes]
    ms[pl.ds(r, 1)] = mown[pl.ds(level, 1)]

    for g in range(0, ch, group):
        loads[5 + g // group].wait()
        xbuf[2 : 2 + height, pl.ds(c, 1), g : g + group] = (
            jnp.transpose(xraw[g : g + group].astype(F32), (1, 0, 2)).astype(BF16)[:, None]
        )

    pl.semaphore_wait(barrier, greeted)

    for d in FAR_ROWS:
        there = lax.rem(r + d, ROWS)
        go(remote(mown.at[lax.rem(there, 4)], ms.at[r], ms_s.at[d], ms_r.at[d], rows=there))
    for d in FAR_ROWS:
        go(remote(en.at[r], en.at[r], en_s.at[d], en_r.at[d], rows=lax.rem(r + d, ROWS)))
    half = height // 2

    def rows_of(shard, first, count):
        return xbuf.at[pl.ds(first + 2, count), shard]

    to_right, to_left = {"chan": right}, {"chan": left}
    go(remote(rows_of(c, 0, half), rows_of(c, 0, half), ag_s.at[0, 0], ag_r.at[0, 0], **to_right))
    go(remote(rows_of(c, half, half), rows_of(c, half, half), ag_s.at[1, 0], ag_r.at[1, 0], **to_left))

    most = half - 1
    go(remote(rows_of(c, half, 1), rows_of(c, half, 1), ag_s.at[0, 4], ag_r.at[0, 4], **to_right))
    go(remote(rows_of(c, most, 1), rows_of(c, most, 1), ag_s.at[1, 4], ag_r.at[1, 4], **to_left))
    for d in range(1, SAMPLES):
        there = lax.rem(b + d, SAMPLES)
        go(remote(latb.at[b], latb.at[b], in_s.at[0, d], in_r.at[0, d], samples=there))
        go(remote(selb.at[b], selb.at[b], in_s.at[1, d], in_r.at[1, d], samples=there))

    loads[-1].wait()

    def lay_f(g, carry):
        some = pl.ds(pl.multiple_of(g * group, group), group)
        f_ref[:, some] = jnp.transpose(fraw[some].astype(F32), (1, 0, 2)).astype(BF16)
        return carry

    lax.fori_loop(0, ch // group, lay_f, 0)

    def edge(src, dst, send, recv, up):
        there = jnp.maximum(r - 1, 0) if up else jnp.minimum(r + 1, ROWS - 1)
        i = 0 if up else 1
        return remote(src, dst.at[1 - i], send.at[i], recv.at[1 - i], rows=there)

    not_first, not_last = r > 0, r < ROWS - 1

    @pl.when(not_first)
    def _():
        edge(f_ref.at[0], fhalo, fh_s, fh_r, True).start()

    @pl.when(not_last)
    def _():
        edge(f_ref.at[height - 1], fhalo, fh_s, fh_r, False).start()

    def shift_into(at, f):
        wide = f.astype(F32)
        for kw, moved in enumerate((moved_right(wide).astype(BF16), f, moved_left(wide).astype(BF16))):
            for part in range(2):
                first = (3 * part + kw) * ib
                fs[at, first : first + ib] = moved[part * ib : (part + 1) * ib]

    def shifted(h, carry):
        shift_into(h + 1, f_ref[h])
        return carry

    lax.fori_loop(0, height, shifted, 0)

    for d in range(1, ROWS):
        src = lax.rem(r + ROWS - d, ROWS)
        remote(mown.at[0], ms.at[src], ms_s.at[d], ms_r.at[d], rows=src).wait_recv()
    my[pl.ds(c, 1)] = ms[pl.ds(2 * c, 2)][None]
    for d in (1, 3, 2):
        there = lax.rem(c + d, CHANS)
        go(remote(ms.at[pl.ds(2 * there, 2)], my.at[c], my_s.at[d], my_r.at[d], chan=there))
    go(remote(rows_of(c, half + 1, most), rows_of(c, half + 1, most), ag_s.at[0, 1], ag_r.at[0, 1], **to_right))
    go(remote(rows_of(c, 0, most), rows_of(c, 0, most), ag_s.at[1, 1], ag_r.at[1, 1], **to_left))

    for d in range(1, ROWS):
        src = lax.rem(r + ROWS - d, ROWS)
        remote(en.at[src], en.at[src], en_s.at[d], en_r.at[d], rows=src).wait_recv()
    scale = lax.rsqrt(jnp.sum(en[...], axis=0) + EPS)
    sc[pl.ds(c, 1)] = scale[None]
    for d in range(1, CHANS):
        go(remote(sc.at[c], sc.at[c], sc_s.at[d], sc_r.at[d], chan=lax.rem(c + d, CHANS)))
    scale = jnp.concatenate([scale, scale], axis=1)[None]

    @pl.when(not_first)
    def _():
        edge(f_ref.at[0], fhalo, fh_s, fh_r, False).wait_recv()
        shift_into(0, fhalo[0])

    @pl.when(r == 0)
    def _():
        fs[0] = jnp.zeros(fs.shape[1:], BF16)

    @pl.when(not_last)
    def _():
        edge(f_ref.at[0], fhalo, fh_s, fh_r, True).wait_recv()
        shift_into(height + 1, fhalo[1])

    @pl.when(r == ROWS - 1)
    def _():
        fs[height + 1] = jnp.zeros(fs.shape[1:], BF16)

    def grad_step(acc, shard, q):
        around = xbuf[q : q + 3, pl.ds(shard, 1)].reshape(3 * ch, width)
        return acc + lax.dot_general(
            fs[q], around, (((1,), (1,)), ((), ())), preferred_element_type=F32
        )

    def grad_rows(acc, shard, steps):
        for q in steps:
            acc = grad_step(acc, shard, q)
        return acc

    no_grad = jnp.zeros((tall, 3 * ch), F32)

    keep = lax.rem(r, 2)
    partner = r + 1 - 2 * keep

    def swap(i):
        return remote(gp.at[i, 1 - keep], gx.at[i], gx_s.at[i], gx_r.at[i], rows=partner)

    def send_grad(i, acc, slope=None):
        gs[i, :, :, : 3 * ch] = acc.reshape(2, 3 * ib, 3 * ch).astype(BF16)
        if slope:
            send_slope(i, *slope)
        for part in range(2):
            wide = packed(acc[part * 3 * ib : (part + 1) * 3 * ib])
            gw[i, part] = wide
            gp[i, part] = wide.astype(BF16)
        if i < 3:
            go(swap(i))

    def block(i, shard):
        return remote(gk.at[i], gbuf.at[r // 2], g_s.at[i], g_r.at[r // 2], rows=2 * c + keep, chan=shard)

    def send_block(i, shard):
        swap(i).wait_recv()
        gk[i] = (gw[i, keep] + gx[i].astype(F32)).astype(BF16)
        if i == 0:
            @pl.when(r // 2 == c)
            def _():
                pltpu.make_async_copy(gk.at[0], gbuf.at[r // 2], g_r.at[r // 2]).start()

            @pl.when(r // 2 != c)
            def _():
                block(0, c).start()
        else:
            go(block(i, shard))

    send_grad(0, grad_rows(no_grad, c, range(height + 2)))

    most = half - 1

    def from_left(k, first, count, shard):
        return remote(rows_of(shard, first, count), rows_of(shard, first, count), ag_s.at[0, k], ag_r.at[0, k], **to_right)

    def from_right(k, first, count, shard):
        return remote(rows_of(shard, first, count), rows_of(shard, first, count), ag_s.at[1, k], ag_r.at[1, k], **to_left)

    def from_left(k, first, count, shard):
        return remote(rows_of(shard, first, count), rows_of(shard, first, count), ag_s.at[0, k], ag_r.at[0, k], **to_right)

    def from_right(k, first, count, shard):
        return remote(rows_of(shard, first, count), rows_of(shard, first, count), ag_s.at[1, k], ag_r.at[1, k], **to_left)

    from_left(0, 0, half, left).wait_recv()
    go(from_left(2, 0, most, left))
    go(from_left(3, most, 1, left))
    from_right(0, half, half, right).wait_recv()
    go(from_right(2, half + 1, most, right))
    go(from_right(3, half, 1, right))

    def both_steps(acc_left, acc_right, steps):
        for q in steps:
            acc_left = grad_step(acc_left, left, q)
            acc_right = grad_step(acc_right, right, height + 1 - q)
        return acc_left, acc_right

    acc_left, acc_right = both_steps(no_grad, no_grad, range(half))

    send_block(0, c)

    for d in range(1, CHANS):
        src = lax.rem(c + CHANS - d, CHANS)
        remote(ms.at[pl.ds(0, 2)], my.at[src], my_s.at[d], my_r.at[d], chan=src).wait_recv()

    def quarter_of(level, shards=slice(None)):
        top = pl.multiple_of((level // 2) * tile, tile)
        start = pl.multiple_of(lax.rem(level, 2) * lanes, lanes)
        return mm.at[shards, :, pl.ds(top, tile), pl.ds(start, lanes)]

    def peer(d):
        return 4 * side + lax.rem(level + d, 4)

    mine = pltpu.make_async_copy(my, quarter_of(level), mm_r.at[0])
    mine.start()
    for d in (2, 1, 3):
        go(remote(my, quarter_of(level), mm_s.at[d], mm_r.at[d], rows=peer(d)))

    from_left(4, half, 1, left).wait_recv()
    from_right(4, most, 1, right).wait_recv()
    from_left(1, half + 1, most, left).wait_recv()
    from_right(1, 0, most, right).wait_recv()

    acc_left, acc_right = both_steps(acc_left, acc_right, range(half, height + 2))
    send_grad(1, acc_left)
    send_grad(2, acc_right)


    from_left(2, 0, most, opp).wait_recv()
    from_right(2, half + 1, most, opp).wait_recv()

    early = list(range(most)) + list(range(height + 2 - most, height + 2))
    acc_opp = grad_rows(no_grad, opp, early)

    send_block(1, left)
    send_block(2, right)

    for d in range(1, 4):
        src = lax.rem(level + 4 - d, 4)
        remote(my, quarter_of(src), mm_s.at[d], mm_r.at[d], rows=peer(4 - d)).wait_recv()
    mine.wait()

    def send_slope(i, k, shard):
        slo[i] = over_taps(gs[i].astype(F32) * mm[shard].astype(F32))
        for d in (*FAR_ROWS, 0):
            if k == 0 and d == 0:
                slv[pl.ds(r, 1), pl.ds(c, 1)] = slo[0][None, None]
            else:
                go(remote(
                    slo.at[i], slv.at[r, c], sl_s.at[d, k], sl_r.at[d, k], rows=lax.rem(r + d, ROWS), chan=shard
                ))

    send_slope(0, 0, c)
    send_slope(1, 3, left)
    send_slope(2, 1, right)

    from_left(3, most, 1, opp).wait_recv()
    from_right(3, half, 1, opp).wait_recv()

    send_grad(3, grad_rows(acc_opp, opp, range(most, height + 2 - most)), slope=(2, opp))
    for part in range(2):
        go(remote(gp.at[3, part], gbuf.at[r], gf_s.at[part], g_r.at[r], rows=2 * c + part, chan=opp))

    for d in range(1, CHANS):
        src = lax.rem(c + CHANS - d, CHANS)
        remote(sc.at[src], sc.at[src], sc_s.at[d], sc_r.at[d], chan=src).wait_recv()
    for shard in range(CHANS):
        modulated = mm[shard].reshape(tall, 4 * ch).astype(F32)
        modulated = (modulated * jnp.concatenate([sc[shard], sc[shard]], axis=1)).astype(BF16)
        for kh in range(3):
            at = (kh * CHANS + shard) * ch
            mall[:, at : at + ch] = modulated[:, kh * ch : (kh + 1) * ch]

    def row_out(q):
        first, last = max(q, 2), min(q + 3, height + 2)
        deep = CHANS * ch
        total = jnp.dot(
            mall[:, (first - q) * deep : (last - q) * deep],
            xbuf[first:last].reshape((last - first) * deep, width),
            preferred_element_type=F32,
        )
        for part in range(2):
            t = total[3 * part * ib : 3 * (part + 1) * ib]
            dacc[q, part * ib : (part + 1) * ib] = t[ib : 2 * ib] + moved_left(t[:ib]) + moved_right(t[2 * ib :])

    row_out(0)
    row_out(height + 1)
    dsend[0] = dacc[0].astype(BF16)
    dsend[1] = dacc[height + 1].astype(BF16)

    @pl.when(not_first)
    def _():
        edge(dsend.at[0], dhalo, dh_s, dh_r, True).start()

    @pl.when(not_last)
    def _():
        edge(dsend.at[1], dhalo, dh_s, dh_r, False).start()

    for q in range(1, height + 1):
        row_out(q)

    for src in range(ROWS // 2):
        remote(gk.at[0], gbuf.at[src], g_s.at[0], g_r.at[src], rows=partner).wait_recv()

    @pl.when(lax.rem(c + CHANS - r // 2, CHANS) == 2)
    def _():
        for src in range(ROWS // 2, ROWS):
            remote(gk.at[0], gbuf.at[src], g_s.at[0], g_r.at[src], rows=partner).wait_recv()

    for d in range(ROWS):
        for k in range(CHANS):
            if d or k:
                rs, cs = lax.rem(r + ROWS - d, ROWS), lax.rem(c + CHANS - k, CHANS)
                remote(slo.at[0], slv.at[rs, cs], sl_s.at[d, k], sl_r.at[d, k], rows=rs, chan=cs).wait_recv()

    grad = gbuf[0].astype(F32)
    for src in range(1, ROWS):
        grad = grad + gbuf[src].astype(F32)
    grad = unpacked(grad).reshape(3, ib, 4 * ch)
    slope = jnp.sum(slv[...], axis=(0, 1))
    slope = jnp.concatenate([slope, slope], axis=1)[None]
    plain_grad = grad * scale - plain * (slope * (scale * scale * scale))
    by_input = jnp.sum(plain_grad * ker, axis=0)
    by_input = jnp.concatenate([by_input, jnp.zeros((128 - ib, by_input.shape[1]), F32)], axis=0)
    style_part = lax.dot_general(
        jnp.ones((8, by_input.shape[1]), F32), by_input, (((1,), (1,)), ((), ())),
        preferred_element_type=F32, precision=lax.Precision.HIGHEST,
    )
    st[pl.ds(b, 1), pl.ds(c, 1)] = style_part[0:1][None, None]
    for dc in (*FAR_CHANS, 0):
        for db in (*FAR_SAMPLES, 0):
            if db or dc:
                go(remote(
                    st.at[b, c], st.at[b, c], st_s.at[db, dc], st_r.at[db, dc],
                    samples=lax.rem(b + db, SAMPLES), chan=lax.rem(c + dc, CHANS),
                ))
    kg[pl.ds(b, 1)] = packed((plain_grad * style[None]).reshape(3 * ib, 4 * ch))[None].astype(BF16)
    for d in FAR_SAMPLES:
        go(remote(kg.at[b], kg.at[b], kg_s.at[d], kg_r.at[d], samples=lax.rem(b + d, SAMPLES)))

    @pl.when(not_first)
    def _():
        edge(dsend.at[0], dhalo, dh_s, dh_r, False).wait_recv()
        dacc[1] = dacc[1] + dhalo[0].astype(F32)

    @pl.when(not_last)
    def _():
        edge(dsend.at[0], dhalo, dh_s, dh_r, True).wait_recv()
        dacc[height] = dacc[height] + dhalo[1].astype(F32)

    def lay_d(g, carry):
        some = pl.ds(pl.multiple_of(g * group, group), group)
        d_ref[some] = jnp.transpose(dacc[pl.ds(1, height), some], (1, 0, 2)).astype(BF16)
        return carry

    lax.fori_loop(0, ch // group, lay_d, 0)

    for d in range(1, SAMPLES):
        src = lax.rem(b + SAMPLES - d, SAMPLES)
        remote(latb.at[src], latb.at[src], in_s.at[0, d], in_r.at[0, d], samples=src).wait_recv()
        remote(selb.at[src], selb.at[src], in_s.at[1, d], in_r.at[1, d], samples=src).wait_recv()
    for db in range(SAMPLES):
        for dc in range(CHANS):
            if db or dc:
                bs, cs = lax.rem(b + SAMPLES - db, SAMPLES), lax.rem(c + CHANS - dc, CHANS)
                remote(
                    st.at[bs, cs], st.at[bs, cs], st_s.at[db, dc], st_r.at[db, dc], samples=bs, chan=cs
                ).wait_recv()

    for d in range(1, SAMPLES):
        src = lax.rem(b + SAMPLES - d, SAMPLES)
        remote(kg.at[src], kg.at[src], kg_s.at[d], kg_r.at[d], samples=src).wait_recv()

    for copy in sent:
        copy.wait_send()

    @pl.when(r // 2 != c)
    def _():
        block(0, c).wait_send()

    @pl.when(not_first)
    def _():
        edge(f_ref.at[0], fhalo, fh_s, fh_r, True).wait_send()
        edge(dsend.at[0], dhalo, dh_s, dh_r, True).wait_send()

    @pl.when(not_last)
    def _():
        edge(f_ref.at[0], fhalo, fh_s, fh_r, False).wait_send()
        edge(dsend.at[1], dhalo, dh_s, dh_r, False).wait_send()


def write_out(d_ref, kg, st, latb, selb, d_hbm, bg_hbm, awg_hbm, abg_hbm, bg_ref, awg_ref, abg_ref, sems):
    nb, _, ib, ch = bg_ref.shape
    quarter = d_ref.shape[0] // 4
    copies = []
    for i in range(4):
        some = pl.ds(i * quarter, quarter)
        copies.append(pltpu.make_async_copy(d_ref.at[some], d_hbm.at[some], sems.at[2 + nb + i]))
        copies[-1].start()
    each = [kg[s].astype(F32) for s in range(SAMPLES)]
    for k in range(nb):
        total = unpacked(sum(selb[s][0:1, k : k + 1] * each[s] for s in range(SAMPLES)))
        for kw in range(3):
            for kh in range(3):
                bg_ref[k, 3 * kh + kw] = total[kw * ib : (kw + 1) * ib, (2 - kh) * ch : (3 - kh) * ch]
        copies.append(pltpu.make_async_copy(bg_ref.at[k], bg_hbm.at[k], sems.at[2 + k]))
        copies[-1].start()
    diagonal = lax.broadcasted_iota(jnp.int32, (ib, 128), 0) == lane_iota((ib, 128))
    style_sum = jnp.zeros((1, 128), F32)
    affine = jnp.zeros(awg_ref.shape, F32)
    for s in range(SAMPLES):
        row = st[s, 0] + st[s, 1] + st[s, 2] + st[s, 3]
        style_sum = style_sum + row
        column = jnp.sum(jnp.where(diagonal, row, 0.0), axis=1, keepdims=True)
        affine = affine + column * latb[s][0:1]
    awg_ref[...] = affine
    abg_ref[...] = style_sum[:, :ib]
    copies.append(pltpu.make_async_copy(awg_ref, awg_hbm, sems.at[0]))
    copies[-1].start()
    copies.append(pltpu.make_async_copy(abg_ref, abg_hbm, sems.at[1]))
    copies[-1].start()
    for copy in copies:
        copy.wait()


def on_device(feature, out_grad, bank, select, latent, affine_w, affine_b):
    _, ch, height, width = out_grad.shape
    nb, taps, _, ib = bank.shape
    z = latent.shape[1]
    lanes = 4 * ch
    vmem, hbm = pl.BlockSpec(memory_space=pltpu.VMEM), pl.BlockSpec(memory_space=pltpu.HBM)
    dma = pltpu.SemaphoreType.DMA
    parts = pl.pallas_call(
        kernel,
        out_shape=(
            jax.ShapeDtypeStruct((ch, height, width), BF16),
            jax.ShapeDtypeStruct((SAMPLES, 9 * ib // 2, 128), BF16),
            jax.ShapeDtypeStruct((SAMPLES, CHANS, 1, 128), F32),
            jax.ShapeDtypeStruct((SAMPLES, 8, z), F32),
            jax.ShapeDtypeStruct((SAMPLES, 8, 128), F32),
        ),
        in_specs=[hbm] * 7,
        out_specs=(vmem,) * 5,
        scratch_shapes=[
            pltpu.VMEM((ch, height, width), BF16),
            pltpu.VMEM((ch, height, width), BF16),
            pltpu.VMEM((height, ch, width), BF16),
            pltpu.VMEM((nb, taps, ib, ch), F32),
            pltpu.VMEM((1, nb), jnp.int32),
            pltpu.VMEM((1, z), F32),
            pltpu.VMEM((ib, z), F32),
            pltpu.VMEM((1, ib), F32),
            pltpu.VMEM((height + 5, CHANS, ch, width), BF16),
            pltpu.VMEM((height + 2, 3 * ch, width), BF16),
            pltpu.VMEM((2, ch, width), BF16),
            pltpu.VMEM((4, 3 * ib // 2, 128), BF16),
            pltpu.VMEM((ROWS, 3 * ib // 2, 128), BF16),
            pltpu.VMEM((CHANS, 2, 3 * ib // 2, 128), BF16),
            pltpu.VMEM((CHANS, 2, 3 * ib, lanes), BF16),
            pltpu.VMEM((6 * ib, 3 * CHANS * ch), BF16),
            pltpu.VMEM((CHANS, 2, 3 * ib, lanes), BF16),
            pltpu.VMEM((CHANS, 2, 9 * ib // 2, 128), BF16),
            pltpu.VMEM((CHANS, 2, 9 * ib // 2, 128), F32),
            pltpu.VMEM((CHANS, 9 * ib // 2, 128), BF16),
            pltpu.VMEM((CHANS, 9 * ib // 2, 128), BF16),
            pltpu.VMEM((ROWS, 9 * ib // 2, 128), BF16),
            pltpu.VMEM((ROWS, 1, 128), F32),
            pltpu.VMEM((CHANS, 1, 128), F32),
            pltpu.VMEM((ROWS, CHANS, 1, 128), F32),
            pltpu.VMEM((CHANS, 1, 128), F32),
            pltpu.VMEM((3, ib, lanes), F32),
            pltpu.VMEM((3, ib, lanes), F32),
            pltpu.VMEM((height + 2, ch, width), F32),
            pltpu.VMEM((2, ch, width), BF16),
            pltpu.VMEM((2, ch, width), BF16),
            dma((2, 5)), dma((2, 5)),
            dma((2,)), dma((2,)),
            dma((2,)), dma((2,)),
            dma((6 + ch // 16,)),
            dma((2, SAMPLES)), dma((2, SAMPLES)),
            dma((ROWS,)), dma((ROWS,)),
            dma((CHANS,)), dma((CHANS,)),
            dma((ROWS,)), dma((ROWS,)), dma((CHANS,)), dma((CHANS,)), dma((5,)), dma((5,)),
            dma((CHANS,)), dma((CHANS,)), dma((CHANS,)), dma((2,)), dma((ROWS,)),
            dma((ROWS, CHANS)), dma((ROWS, CHANS)),
            dma((SAMPLES,)), dma((SAMPLES,)),
            dma((SAMPLES, CHANS)), dma((SAMPLES, CHANS)),
        ],
        compiler_params=pltpu.CompilerParams(
            collective_id=0, has_side_effects=True, vmem_limit_bytes=48 * 1024 * 1024
        ),
    )(
        *(pltpu.with_memory_space_constraint(a, pltpu.HBM) for a in (
            out_grad[0], feature[0], jnp.transpose(bank, (0, 1, 3, 2)), select, latent,
            jnp.transpose(affine_w), affine_b[None],
        ))
    )
    d, bg, awg, abg = pl.pallas_call(
        write_out,
        out_shape=(
            jax.ShapeDtypeStruct((ch, height, width), BF16),
            jax.ShapeDtypeStruct((nb, taps, ib, ch), F32),
            jax.ShapeDtypeStruct((ib, z), F32),
            jax.ShapeDtypeStruct((1, ib), F32),
        ),
        in_specs=[vmem] * 5,
        out_specs=(hbm,) * 4,
        scratch_shapes=[
            pltpu.VMEM((nb, taps, ib, ch), F32),
            pltpu.VMEM((ib, z), F32),
            pltpu.VMEM((1, ib), F32),
            dma((6 + nb,)),
        ],
        compiler_params=pltpu.CompilerParams(vmem_limit_bytes=16 * 1024 * 1024),
    )(*parts)
    return d[None], jnp.transpose(bg, (0, 1, 3, 2)), jnp.transpose(awg), abg[0]


def solution(mesh):
    return jax.shard_map(
        on_device,
        mesh=mesh,
        in_specs=(
            P("samples", "chan", "rows", None),
            P("samples", "chan", "rows", None),
            P(None, None, "chan", "rows"),
            P("samples", None),
            P("samples", None),
            P(None, "rows"),
            P("rows"),
        ),
        out_specs=(
            P("samples", "chan", "rows", None),
            P(None, None, "chan", "rows"),
            P(None, "rows"),
            P("rows"),
        ),
        check_vma=False,
    )
```
